32 devices in a mesh: dp: 8 (over y, x, core), tensor: 4 (over z).
Axes of the slice: x: 2, y: 2, z: 4, core: 2. Of those that a mesh axis runs over, the one named last changes fastest.
Arguments:
- hidden_in: bfloat16 [16384, 768], P(('dp', 'tensor')), may hold values from -6 to 6
- token_types: int32 [16384], P('dp'), may hold values 0 or 1
- lengths: int32 [8], P('dp'), may hold values from 512 to 2048, as said below
- cotangent: bfloat16 [16384, 768], P(('dp', 'tensor')), may hold values from -6 to 6
- query_w: bfloat16 [4, 768, 768], P(None, 'dp', 'tensor'), may hold values from -0.4375 to 0.4375
- query_b: bfloat16 [4, 768], replicated, may hold values from -3 to 3
- key_w: bfloat16 [768, 768], P('dp', 'tensor'), may hold values from -0.21875 to 0.21875
- value_w: bfloat16 [768, 768], P('dp', 'tensor'), may hold values from -0.21875 to 0.21875
- value_b: bfloat16 [768], replicated, may hold values from -3 to 3
- out_w: bfloat16 [768, 768], P('tensor', 'dp'), may hold values from -0.875 to 0.875
- out_b: bfloat16 [768], replicated, may hold values from -3 to 3
- gain_one: bfloat16 [768], replicated, may hold values from 0.099609375 to 1.8984375
- shift_one: bfloat16 [768], replicated, may hold values from -3 to 3
- inter_w: bfloat16 [768, 3072], P('dp', 'tensor'), may hold values from -0.21875 to 0.21875
- inter_b: bfloat16 [3072], replicated, may hold values from -3 to 3
- output_w: bfloat16 [3072, 768], P('tensor', 'dp'), may hold values from -0.109375 to 0.109375
- output_b: bfloat16 [768], replicated, may hold values from -3 to 3
- gain_two: bfloat16 [768], replicated, may hold values from 0.099609375 to 1.8984375
- shift_two: bfloat16 [768], replicated, may hold values from -3 to 3
Outputs:
- layer_out: bfloat16 [16384, 768], P(('dp', 'tensor'))
- grad_hidden: float32 [16384, 768], P(('dp', 'tensor'))
- query_weight_gradient: float32 [4, 768, 768], P(None, 'dp', 'tensor')
- grad_query_b: float32 [4, 768], replicated
- grad_key_w: float32 [768, 768], P('dp', 'tensor')
- grad_value_w: float32 [768, 768], P('dp', 'tensor')
- grad_value_b: float32 [768], replicated
- grad_out_w: float32 [768, 768], P('tensor', 'dp')
- grad_out_b: float32 [768], replicated
- grad_gain_one: float32 [768], replicated
- grad_shift_one: float32 [768], replicated
- grad_inter_w: float32 [768, 3072], P('dp', 'tensor')
- grad_inter_b: float32 [3072], replicated
- grad_output_w: float32 [3072, 768], P('tensor', 'dp')
- grad_output_b: float32 [768], replicated
- grad_gain_two: float32 [768], replicated
- grad_shift_two: float32 [768], replicated
The draws below stay inside these ranges and needn't reach their ends.
Inputs may be any that keep to these rules, and one draw needn't show every extreme that they name: `lengths`: valid slots of each sequence; in every draw one sequence is full and another has exactly 512 valid slots.
All inputs are finite; a program needn't handle non-finite values. No bound on the sum of `token_types` on one device may be relied on, other than what follows from the above.
Results may differ from the reference program's by a relative error of at most 0.019.
The reference program's roundings to bfloat16 on the way count: a program that leaves them out, or rounds other values in their place, can miss the bound.
Values may be sent and summed in bfloat16 or wider, within the bound.
No kernel may reach another device: no remote copies, remote signals or barrier semaphores. Data moves between devices by JAX's collectives and lax.ppermute only.
A program may use at most 192 MiB of HBM per device.

```python
import jax
import jax.numpy as jnp
from jax import lax

D = 768
H = 12
HD = 64
FF = 3072
SEQ = 2048
NSEQ = 8
TOKENS = 16384
N_TENSOR = 4


def draw_lengths(key, part):
    base = jax.random.randint(key, (NSEQ,), SEQ // 4, SEQ + 1)
    chosen = jax.random.randint(jax.random.fold_in(key, 11), (), 0, NSEQ)
    index_row = jnp.arange(NSEQ)
    base = jnp.where(index_row == chosen, SEQ, base)
    base = jnp.where(index_row == (chosen + 1) % NSEQ, SEQ // 4, base)
    return base.astype(jnp.int32)


def touch_ends(values, rng, low, high):
    longest = values.shape.index(max(values.shape))
    spots = []
    for shift in (0, 1):
        where = [jax.random.randint(jax.random.fold_in(rng, axis), (), 0, length) for axis, length in enumerate(values.shape)]
        where[longest] = (where[longest] + shift) % values.shape[longest]
        spots.append(tuple(where))
    return values.at[spots[0]].set(low).at[spots[1]].set(high)


def block_levels(stream_key, dims, shards, low, top_value):
    factor_of, own = 1.0, jax.random.fold_in(stream_key, 6)
    for dim, blocks in shards:
        steps = jnp.exp(jax.random.uniform(jax.random.fold_in(own, dim), (blocks,), jnp.float32, low / len(shards), top_value / len(shards)))
        factor_of = factor_of * jnp.repeat(steps, dims[dim] // blocks).reshape([-1 if axis == dim else 1 for axis in range(len(dims))])
    return factor_of


def normal_values(key, dims, deviation, bound, shards=(), kind=jnp.bfloat16):
    values = jax.random.normal(key, dims, jnp.float32) * deviation
    if len(shards) > 0:
        values = block_levels(key, dims, shards, -0.22, 0.18) * values
    return jnp.clip(values, min=-bound, max=bound).astype(kind)


def setup_inputs(seed: int = 0) -> dict:
    seeds = jax.random.split(jax.random.key(seed), 20)
    hidden_in = normal_values(seeds[0], (TOKENS, D), 1.0, 6.0, ((0, 32),))
    token_types = touch_ends((jax.random.randint(seeds[1], (TOKENS,), 0, 4) < 1).astype(jnp.int32), jax.random.fold_in(seeds[1], 1), 0, 1)
    lengths = draw_lengths(jax.random.fold_in(seeds[19], 71), 0)
    cotangent = normal_values(seeds[3], (TOKENS, D), 1.0, 6.0, ((0, 32),))
    query_w = normal_values(seeds[4], (4, D, D), (D // 4) ** -0.5, 0.4375, ((1, 8), (2, 4)))
    query_b = normal_values(seeds[5], (4, D), 0.5, 3.0)
    key_w = normal_values(seeds[6], (D, D), D ** -0.5, 0.21875, ((0, 8), (1, 4)))
    value_w = normal_values(seeds[7], (D, D), D ** -0.5, 0.21875, ((0, 8), (1, 4)))
    value_b = normal_values(seeds[8], (D,), 0.5, 3.0)
    out_w = normal_values(seeds[9], (D, D), (D // 16) ** -0.5, 0.875, ((0, 4), (1, 8)))
    out_b = normal_values(seeds[10], (D,), 0.5, 3.0)
    gain_one = jnp.clip(1.0 + 0.18 * jax.random.normal(seeds[11], (D,), jnp.float32), 0.099609375, 1.8984375).astype(jnp.bfloat16)
    shift_one = normal_values(seeds[12], (D,), 0.5, 3.0)
    inter_w = normal_values(seeds[13], (D, FF), D ** -0.5, 0.21875, ((0, 8), (1, 4)))
    inter_b = normal_values(seeds[14], (FF,), 0.5, 3.0)
    output_w = normal_values(seeds[15], (FF, D), FF ** -0.5, 0.109375, ((0, 4), (1, 8)))
    output_b = normal_values(seeds[16], (D,), 0.5, 3.0)
    gain_two = jnp.clip(1.0 + 0.18 * jax.random.normal(seeds[17], (D,), jnp.float32), 0.099609375, 1.8984375).astype(jnp.bfloat16)
    shift_two = normal_values(seeds[18], (D,), 0.5, 3.0)
    return dict(hidden_in=hidden_in, token_types=token_types, lengths=lengths, cotangent=cotangent, query_w=query_w, query_b=query_b, key_w=key_w, value_w=value_w, value_b=value_b, out_w=out_w, out_b=out_b, gain_one=gain_one, shift_one=shift_one, inter_w=inter_w, inter_b=inter_b, output_w=output_w, output_b=output_b, gain_two=gain_two, shift_two=shift_two)


@jax.custom_vjp
def low(v):
    return lax.optimization_barrier(v.astype(jnp.bfloat16)).astype(jnp.float32)

@jax.custom_vjp
def low_back(v):
    return v

def low_keep(v):
    return (low(v), None)

def low_pass(kept, grad):
    return (grad,)

def back_keep(v):
    return (v, None)

def back_low(kept, grad):
    return (low(grad),)
low.defvjp(low_keep, low_pass)
low_back.defvjp(back_keep, back_low)

def layer_norm(residual, norm_gain, norm_shift):
    center = residual - lax.optimization_barrier(jnp.mean(residual, -1, keepdims=True))
    spread = lax.optimization_barrier(jnp.mean(center * center, -1, keepdims=True))
    return center * lax.rsqrt(spread + 1e-05) * norm_gain + norm_shift

def luke_layer(params, hidden, entity, valid_mask):
    query_w, query_b, key_w, value_w, value_b, out_w, out_b, gain_one, shift_one, inter_w, inter_b, output_w, output_b, gain_two, shift_two = params
    highest = lax.Precision.HIGHEST
    groups = N_TENSOR
    heads_group = H // groups
    width_group = D // groups
    ffn_group = FF // groups
    length = hidden.shape[0]
    copies = low_back(jnp.broadcast_to(hidden, (groups, length, D)))
    query_all = jnp.einsum('gtd,adgc->gtac', copies, query_w.reshape(4, D, groups, width_group), precision=highest)
    query_all = query_all + query_b.reshape(4, groups, width_group).transpose(1, 0, 2)[:, None]
    entity_side = entity[None, :, None] > 0.5
    to_word = jnp.where(entity_side, query_all[:, :, 2], query_all[:, :, 0])
    to_entity = jnp.where(entity_side, query_all[:, :, 3], query_all[:, :, 1])
    to_word = low(low_back(to_word))
    to_entity = low(low_back(to_entity))
    key_rows = low(low_back(jnp.einsum('gtd,dgc->gtc', copies, key_w.reshape(D, groups, width_group), precision=highest)))
    values = jnp.einsum('gtd,dgc->gtc', copies, value_w.reshape(D, groups, width_group), precision=highest)
    values = low(low_back(values + value_b.reshape(groups, width_group)[:, None]))

    def split_heads(matrix):
        return matrix.reshape(groups, length, heads_group, HD).transpose(0, 2, 1, 3).reshape(H, length, HD)
    key_heads = split_heads(key_rows)
    score_word = jnp.einsum('hqc,hkc->hqk', split_heads(to_word), key_heads, precision=highest)
    score_entity = jnp.einsum('hqc,hkc->hqk', split_heads(to_entity), key_heads, precision=highest)
    scores = jnp.where(entity[None, None, :] > 0.5, score_entity, score_word) * HD ** (-0.5)
    scores = low_back(scores)
    scores = jnp.where(valid_mask[None, None, :] > 0.5, scores, -1e+30)
    shifted = scores - lax.optimization_barrier(jnp.max(scores, -1, keepdims=True))
    exponent = jnp.exp(shifted)
    attn_probs = exponent / lax.optimization_barrier(jnp.sum(exponent, -1, keepdims=True))
    mixed_out = jnp.einsum('hqk,hkc->hqc', low(attn_probs), split_heads(values), precision=highest)
    mixed_out = low(low_back(mixed_out))
    mixed_group = mixed_out.reshape(groups, heads_group, length, HD).transpose(0, 2, 1, 3).reshape(groups, length, width_group)
    head_parts = jnp.einsum('gtc,gcd->gtd', mixed_group, out_w.reshape(groups, width_group, D), precision=highest)
    attended = low_back(lax.optimization_barrier(jnp.sum(low(head_parts), axis=0)) + out_b)
    resid_one = hidden + attended
    normed_one = layer_norm(resid_one, gain_one, shift_one)
    spread_in = low_back(jnp.broadcast_to(low(normed_one), (groups, length, D)))
    inner_pre = jnp.einsum('gtd,dgf->gtf', spread_in, inter_w.reshape(D, groups, ffn_group), precision=highest)
    inner_pre = low_back(inner_pre + inter_b.reshape(groups, ffn_group)[:, None])
    active = low(jax.nn.gelu(inner_pre, approximate=False))
    unit_parts = jnp.einsum('gtf,gfd->gtd', active, output_w.reshape(groups, ffn_group, D), precision=highest)
    ffn_out = low_back(lax.optimization_barrier(jnp.sum(low(unit_parts), axis=0)) + output_b)
    resid_two = normed_one + ffn_out
    return layer_norm(resid_two, gain_two, shift_two) * valid_mask[:, None]

def reference(hidden_in, token_types, lengths, cotangent, query_w, query_b, key_w, value_w, value_b, out_w, out_b, gain_one, shift_one, inter_w, inter_b, output_w, output_b, gain_two, shift_two):
    params = tuple((weight.astype(jnp.float32) for weight in (query_w, query_b, key_w, value_w, value_b, out_w, out_b, gain_one, shift_one, inter_w, inter_b, output_w, output_b, gain_two, shift_two)))
    hidden = hidden_in.astype(jnp.float32).reshape(NSEQ, SEQ, D)
    grad_top = cotangent.astype(jnp.float32).reshape(NSEQ, SEQ, D)
    entity = token_types.astype(jnp.float32).reshape(NSEQ, SEQ)
    positions = jnp.arange(SEQ, dtype=jnp.int32)
    valid_mask = (positions[None, :] < lengths.astype(jnp.int32)[:, None]).astype(jnp.float32)
    zero_grads = tuple((jnp.zeros_like(weight) for weight in params))

    def one_sequence(totals, inputs):
        seq_hidden, seq_grad, seq_entity, seq_valid = inputs

        def apply_layer(seq_in, weights):
            return luke_layer(weights, seq_in, seq_entity, seq_valid)
        result, pullback = jax.vjp(apply_layer, seq_hidden, params)
        grad_in, grad_params = pullback(seq_grad)
        totals = tuple((first + second for first, second in zip(totals, grad_params)))
        return (totals, (result.astype(jnp.bfloat16), grad_in))
    totals, (results, grads_in) = lax.scan(one_sequence, zero_grads, (hidden, grad_top, entity, valid_mask))
    return (results.reshape(TOKENS, D), grads_in.reshape(TOKENS, D), totals[0], totals[1], totals[2], totals[3], totals[4], totals[5], totals[6], totals[7], totals[8], totals[9], totals[10], totals[11], totals[12], totals[13], totals[14])
```

```python
import functools

import jax
import jax.numpy as jnp
from jax import lax
from jax.experimental import pallas as pl
from jax.experimental.pallas import tpu as pltpu
from jax.sharding import PartitionSpec as P

HD = 64
BLOCK = 512
LANES = 128
EPS = 1e-05
MASKED = -1e30
SQRT_HALF = 0.7071067811865476
INV_SQRT_2PI = 0.3989422804014327
VMEM_LIMIT = 60000 * 1024

f32 = jnp.float32
bf16 = jnp.bfloat16


def dot_nn(a, b):
    return lax.dot_general(a, b, (((1,), (0,)), ((), ())), preferred_element_type=f32)


def dot_nt(a, b):
    return lax.dot_general(a, b, (((1,), (1,)), ((), ())), preferred_element_type=f32)


def params(**kw):
    return pltpu.CompilerParams(vmem_limit_bytes=VMEM_LIMIT, **kw)


def cost(flops, nbytes, transcendentals=0):
    return pl.CostEstimate(flops=flops, bytes_accessed=nbytes, transcendentals=transcendentals)


def project_kernel(heads, x_ref, w_ref, b_ref, ent_ref, qc_ref, kc_ref, kv_ref):
    x = x_ref[...]
    ent = ent_ref[...] > 0.5
    lane = lax.broadcasted_iota(jnp.int32, (x.shape[0], LANES), 1)
    low_half = lane < HD
    keep = jnp.logical_xor(low_half, ent)
    for h in range(heads):
        base = 3 * LANES * h
        y = dot_nn(x, w_ref[:, base : base + 3 * LANES]) + b_ref[:, base : base + 3 * LANES]
        q = jnp.where(ent, y[:, LANES : 2 * LANES], y[:, :LANES])
        qc_ref[h] = q.astype(bf16) * (HD ** (-0.5))
        kv = y[:, 2 * LANES :].astype(bf16).astype(f32)
        kv_ref[h] = kv.astype(bf16)
        twice = jnp.where(low_half, kv, pltpu.roll(kv, HD, 1))
        kc_ref[h] = jnp.where(keep, twice, 0.0).astype(bf16)


def project(x, w, b, ent):
    tokens, width = x.shape
    columns = w.shape[1]
    heads = columns // (3 * LANES)
    out = jax.ShapeDtypeStruct((heads, tokens, LANES), bf16)
    spec = pl.BlockSpec((heads, BLOCK, LANES), lambda i: (0, i, 0))
    return pl.pallas_call(
        functools.partial(project_kernel, heads),
        grid=(tokens // BLOCK,),
        in_specs=[
            pl.BlockSpec((BLOCK, width), lambda i: (i, 0)),
            pl.BlockSpec((width, columns), lambda i: (0, 0)),
            pl.BlockSpec((1, columns), lambda i: (0, 0)),
            pl.BlockSpec((BLOCK, LANES), lambda i: (i, 0)),
        ],
        out_specs=[spec, spec, spec],
        out_shape=[out, out, out],
        compiler_params=params(),
        cost_estimate=cost(2 * tokens * width * columns, 2 * tokens * (width + columns)),
        name="project",
    )(x, w, b, ent)


def attend_kernel(me_ref, q_ref, kc_ref, kv_ref, bias_ref, out_ref, lse_ref, vt_ref):
    @pl.when(pl.program_id(1) == 0)
    def _():
        vt_ref[...] = kv_ref[0].T[HD:]

    scores = dot_nt(kc_ref[0], q_ref[0]) + bias_ref[:, :1]
    top = jnp.max(scores, 0, keepdims=True)
    exponent = jnp.exp(scores - top)
    total = jnp.sum(exponent, 0, keepdims=True)
    mixed = dot_nn(vt_ref[...], exponent.astype(bf16))
    out_ref[0] = (mixed / total).astype(bf16)
    lse_ref[0] = top + jnp.log(total)


def attend(me, qc, kc, kv, bias):
    heads, tokens, _ = qc.shape
    blocks = tokens // BLOCK
    full = pl.BlockSpec((1, tokens, LANES), lambda h, i, me: (h, 0, 0))
    return pl.pallas_call(
        attend_kernel,
        grid_spec=pltpu.PrefetchScalarGridSpec(
            num_scalar_prefetch=1,
            grid=(heads, blocks),
            in_specs=[
                pl.BlockSpec((1, BLOCK, LANES), lambda h, i, me: (h, i, 0)),
                full,
                full,
                pl.BlockSpec((tokens, LANES), lambda h, i, me: (0, 0)),
            ],
            out_specs=[
                pl.BlockSpec((1, HD, BLOCK), lambda h, i, me: (i ^ me[0], h, 0)),
                pl.BlockSpec((1, 1, BLOCK), lambda h, i, me: (h, 0, i)),
            ],
            scratch_shapes=[pltpu.VMEM((HD, tokens), bf16)],
        ),
        out_shape=[
            jax.ShapeDtypeStruct((blocks, heads * HD, BLOCK), bf16),
            jax.ShapeDtypeStruct((heads, 1, tokens), f32),
        ],
        compiler_params=params(),
        cost_estimate=cost(
            heads * tokens * tokens * 2 * 3 * LANES, heads * tokens * 8 * LANES, heads * tokens * tokens
        ),
        name="attend",
    )(me, qc, kc, kv, bias)


def attend_back_kernel(
    me_ref, q_ref, kc_ref, kv_ref, bias_ref, ent_ref, lse_ref, out_ref, go_ref,
    dq_ref, dkv_ref, kt_ref, dk_acc, dv_acc, go_pad,
):
    step = pl.program_id(1)

    @pl.when(step == 0)
    def _():
        kt_ref[...] = kc_ref[0].T
        go_pad[:HD] = jnp.zeros((HD, go_pad.shape[1]), bf16)
        dk_acc[...] = jnp.zeros_like(dk_acc)
        dv_acc[...] = jnp.zeros_like(dv_acc)

    go = go_ref[0]
    go_pad[HD:] = go
    delta = jnp.sum(go.astype(f32) * out_ref[0].astype(f32), 0, keepdims=True)
    q = q_ref[0]
    scores = dot_nt(kc_ref[0], q) + bias_ref[:, :1]
    probs = jnp.exp(scores - lse_ref[0])
    grad_probs = dot_nn(kv_ref[0], go_pad[...])
    grad_scores = (probs * (grad_probs - delta)).astype(bf16)
    dv_acc[...] += dot_nt(probs.astype(bf16), go_pad[...])
    dk_acc[...] += dot_nn(grad_scores, q)
    dq_ref[0] = (dot_nn(kt_ref[...], grad_scores) * (HD ** (-0.5))).T.astype(bf16)

    @pl.when(step == pl.num_programs(1) - 1)
    def _():
        lane = lax.broadcasted_iota(jnp.int32, dk_acc.shape, 1)
        dk = dk_acc[...]
        dk = jnp.where(ent_ref[...] > 0.5, pltpu.roll(dk, HD, 1), dk)
        dkv_ref[0] = jnp.where(lane < HD, dk, dv_acc[...]).astype(bf16)


def attend_back(me, qc, kc, kv, bias, ent, lse, mixed, grad_mixed):
    heads, tokens, _ = qc.shape
    blocks = tokens // BLOCK
    full = pl.BlockSpec((1, tokens, LANES), lambda h, i, me: (h, 0, 0))
    col = pl.BlockSpec((tokens, LANES), lambda h, i, me: (0, 0))
    rows = pl.BlockSpec((1, BLOCK, LANES), lambda h, i, me: (h, i, 0))
    slot = pl.BlockSpec((1, HD, BLOCK), lambda h, i, me: (i ^ me[0], h, 0))
    out = jax.ShapeDtypeStruct((heads, tokens, LANES), bf16)
    return pl.pallas_call(
        attend_back_kernel,
        grid_spec=pltpu.PrefetchScalarGridSpec(
            num_scalar_prefetch=1,
            grid=(heads, blocks),
            in_specs=[
                rows, full, full, col, col,
                pl.BlockSpec((1, 1, BLOCK), lambda h, i, me: (h, 0, i)),
                slot, slot,
            ],
            out_specs=[rows, full],
            scratch_shapes=[
                pltpu.VMEM((LANES, tokens), bf16),
                pltpu.VMEM((tokens, LANES), f32),
                pltpu.VMEM((tokens, LANES), f32),
                pltpu.VMEM((LANES, BLOCK), bf16),
            ],
        ),
        out_shape=[out, out],
        compiler_params=params(),
        cost_estimate=cost(
            heads * tokens * tokens * 2 * 5 * LANES, heads * tokens * 16 * LANES, heads * tokens * tokens
        ),
        name="attend_back",
    )(me, qc, kc, kv, bias, ent, lse, mixed, grad_mixed)


def normed(residual, gain, shift):
    center = residual - jnp.mean(residual, -1, keepdims=True)
    inv = lax.rsqrt(jnp.mean(center * center, -1, keepdims=True) + EPS)
    unit = center * inv
    return unit, inv, unit * gain + shift


def norm_back(grad, unit, inv, gain):
    scaled = grad * gain
    return (
        scaled
        - jnp.mean(scaled, -1, keepdims=True)
        - unit * jnp.mean(scaled * unit, -1, keepdims=True)
    ) * inv


def token_kernel(
    me_ref, m0, m1, m2, m3, hid_ref, cot_ref, valid_ref, w_ref, outb_ref, g1_ref, s1_ref, ib_ref,
    ob_ref, g2_ref, s2_ref,
    y_ref, mixt_ref, nb_ref, act_ref, gi_ref, gf_ref, ga_ref, gm_ref, gr_ref, sums_ref, gib_ref,
    slope_ref, outt_ref,
):
    me = me_ref[0]
    groups, width, _ = w_ref.shape
    ffn = act_ref.shape[2]
    gwidth = mixt_ref.shape[1]
    out_at = 2 * ffn
    for m, ref in enumerate((m0, m1, m2, m3)):
        mixt_ref[me ^ m] = ref[0]
    attended = outb_ref[...].astype(f32)
    for g in range(groups):
        part = dot_nt(mixt_ref[g].T, w_ref[g, :, out_at : out_at + gwidth])
        attended = attended + part.astype(bf16).astype(f32)
    gain_one = g1_ref[...].astype(f32)
    unit_one, inv_one, normed_one = normed(
        hid_ref[...].astype(f32) + attended, gain_one, s1_ref[...].astype(f32)
    )
    low_one = normed_one.astype(bf16)
    nb_ref[...] = low_one

    def forward(g, total):
        pre = dot_nn(low_one, w_ref[g, :, :ffn]) + ib_ref[g].astype(f32)
        cdf = 0.5 * (1.0 + lax.erf(pre * SQRT_HALF))
        slope_ref[g] = cdf + pre * (jnp.exp(-0.5 * pre * pre) * INV_SQRT_2PI)
        active = (pre * cdf).astype(bf16)
        act_ref[g] = active
        part = dot_nt(active, w_ref[g, :, ffn:out_at])
        return total + part.astype(bf16).astype(f32)

    ffn_out = lax.fori_loop(
        0, groups, forward, jnp.broadcast_to(ob_ref[...].astype(f32), normed_one.shape)
    )
    gain_two = g2_ref[...].astype(f32)
    valid = valid_ref[:, :1]
    unit_two, inv_two, normed_two = normed(normed_one + ffn_out, gain_two, s2_ref[...].astype(f32))
    y_ref[...] = (normed_two * valid).astype(bf16)
    grad_top = cot_ref[...].astype(f32) * valid
    grad_resid_two = norm_back(grad_top, unit_two, inv_two, gain_two)
    grad_ffn = grad_resid_two.astype(bf16)
    gf_ref[...] = grad_ffn

    def backward(g, total):
        grad_active = dot_nn(grad_ffn, w_ref[g, :, ffn:out_at])
        grad_inner = (slope_ref[g] * grad_active).astype(bf16)
        gi_ref[g] = grad_inner
        gib_ref[g] = jnp.sum(grad_inner.astype(f32), 0, keepdims=True)
        part = dot_nt(grad_inner, w_ref[g, :, :ffn])
        return total + part.astype(bf16).astype(f32)

    grad_normed = lax.fori_loop(0, groups, backward, grad_resid_two)
    grad_resid_one = norm_back(grad_normed, unit_one, inv_one, gain_one)
    gr_ref[...] = grad_resid_one
    grad_att = grad_resid_one.astype(bf16)
    ga_ref[...] = grad_att
    for g in range(groups):
        outt_ref[g] = w_ref[g, :, out_at : out_at + gwidth].T
    for m in range(groups):
        gm_ref[m] = dot_nt(outt_ref[me ^ m], grad_att).astype(bf16)
    rows = (
        grad_att.astype(f32),
        grad_normed * unit_one,
        grad_normed,
        grad_ffn.astype(f32),
        grad_top * unit_two,
        grad_top,
    )
    for at, value in enumerate(rows):
        sums_ref[at] = jnp.sum(value, 0, keepdims=True)


def per_token(me, mixed, hidden, cot, valid, w, out_b, gain1, shift1, inter_b, output_b, gain2, shift2):
    tokens, width = hidden.shape
    groups = w.shape[0]
    gwidth = mixed[0].shape[1]
    ffn = inter_b.shape[2]
    vmem = pl.BlockSpec(memory_space=pltpu.VMEM)
    shape = jax.ShapeDtypeStruct
    return pl.pallas_call(
        token_kernel,
        in_specs=[pl.BlockSpec(memory_space=pltpu.SMEM)] + [vmem] * 15,
        out_specs=[vmem] * 11,
        out_shape=[
            shape((tokens, width), bf16),
            shape((groups, gwidth, tokens), bf16),
            shape((tokens, width), bf16),
            shape((groups, tokens, ffn), bf16),
            shape((groups, tokens, ffn), bf16),
            shape((tokens, width), bf16),
            shape((tokens, width), bf16),
            shape((groups, gwidth, tokens), bf16),
            shape((tokens, width), f32),
            shape((6, 1, width), f32),
            shape((groups, 1, ffn), f32),
        ],
        scratch_shapes=[pltpu.VMEM((groups, tokens, ffn), f32), pltpu.VMEM((groups, gwidth, width), bf16)],
        compiler_params=params(),
        cost_estimate=cost(
            8 * tokens * width * ffn * groups + 4 * tokens * width * width,
            2 * w.size + 4 * tokens * ffn * groups,
            2 * tokens * ffn * groups,
        ),
        name="per_token",
    )(me, *mixed, hidden, cot, valid, w, out_b, gain1, shift1, inter_b, output_b, gain2, shift2)


def weight_grad_kernel(nb_ref, gf_ref, ga_ref, act_ref, gi_ref, mixt_ref, out_ref, nbt, gft, gat):
    ffn = act_ref.shape[2]
    gwidth = mixt_ref.shape[1]

    @pl.when(pl.program_id(0) == 0)
    def _():
        nbt[...] = nb_ref[...].T
        gft[...] = gf_ref[...].T
        gat[...] = ga_ref[...].T

    out_ref[0, :, :ffn] = dot_nn(nbt[...], gi_ref[0]).astype(bf16)
    out_ref[0, :, ffn : 2 * ffn] = dot_nn(gft[...], act_ref[0]).astype(bf16)
    out_ref[0, :, 2 * ffn : 2 * ffn + gwidth] = dot_nt(gat[...], mixt_ref[0]).astype(bf16)


def weight_grads(nb, gf, ga, act, gi, mixt):
    groups, tokens, ffn = act.shape
    width = nb.shape[1]
    gwidth = mixt.shape[1]
    whole = pl.BlockSpec((tokens, width), lambda g: (0, 0))
    group = pl.BlockSpec((1, tokens, ffn), lambda g: (g, 0, 0))
    columns = 2 * ffn + gwidth
    return pl.pallas_call(
        weight_grad_kernel,
        grid=(groups,),
        in_specs=[whole, whole, whole, group, group, pl.BlockSpec((1, gwidth, tokens), lambda g: (g, 0, 0))],
        out_specs=pl.BlockSpec((1, width, columns), lambda g: (g, 0, 0)),
        out_shape=jax.ShapeDtypeStruct((groups, width, columns), bf16),
        scratch_shapes=[pltpu.VMEM((width, tokens), bf16)] * 3,
        compiler_params=params(),
        cost_estimate=cost(2 * tokens * width * columns * groups, 2 * groups * width * columns),
        name="weight_grads",
    )(nb, gf, ga, act, gi, mixt)


def split_columns(heads, dq_ref, dkv_ref, ent):
    for h in range(heads):
        dq = dq_ref[h]
        nothing = jnp.zeros_like(dq)
        yield 3 * h, jnp.where(ent, nothing, dq)
        yield 3 * h + 1, jnp.where(ent, dq, nothing)
        yield 3 * h + 2, dkv_ref[h]


def input_grad_kernel(heads, me_ref, dq_ref, dkv_ref, ent_ref, w_ref, out_ref):
    ent = ent_ref[...] > 0.5
    cols = jnp.concatenate([c for _, c in split_columns(heads, dq_ref, dkv_ref, ent)], 1)
    out_ref[0] = dot_nt(cols, w_ref[...]).astype(bf16)


def input_grad(me, dq, dkv, ent, w):
    heads, tokens, _ = dq.shape
    width, columns = w.shape
    blocks = tokens // BLOCK
    stacked = pl.BlockSpec((heads, BLOCK, LANES), lambda i, me: (0, i, 0))
    return pl.pallas_call(
        functools.partial(input_grad_kernel, heads),
        grid_spec=pltpu.PrefetchScalarGridSpec(
            num_scalar_prefetch=1,
            grid=(blocks,),
            in_specs=[
                stacked,
                stacked,
                pl.BlockSpec((BLOCK, LANES), lambda i, me: (i, 0)),
                pl.BlockSpec((width, columns), lambda i, me: (0, 0)),
            ],
            out_specs=pl.BlockSpec((1, BLOCK, width), lambda i, me: (i ^ me[0], 0, 0)),
        ),
        out_shape=jax.ShapeDtypeStruct((blocks, BLOCK, width), bf16),
        compiler_params=params(),
        cost_estimate=cost(2 * tokens * width * columns, 2 * tokens * (columns + width)),
        name="input_grad",
    )(me, dq, dkv, ent, w)


def project_grad_kernel(heads, x_ref, dq_ref, dkv_ref, ent_ref, out_ref, bias_ref, acc_ref, bias_acc):
    step = pl.program_id(0)

    @pl.when(step == 0)
    def _():
        acc_ref[...] = jnp.zeros_like(acc_ref)
        bias_acc[...] = jnp.zeros_like(bias_acc)

    ent = ent_ref[...] > 0.5
    xt = x_ref[...].T
    for at, column in split_columns(heads, dq_ref, dkv_ref, ent):
        where = slice(LANES * at, LANES * (at + 1))
        acc_ref[:, where] += dot_nn(xt, column)
        bias_acc[:, where] += jnp.sum(column.astype(f32), 0, keepdims=True)

    @pl.when(step == pl.num_programs(0) - 1)
    def _():
        out_ref[...] = acc_ref[...].astype(bf16)
        bias_ref[...] = bias_acc[...]


def project_grad(x, dq, dkv, ent):
    heads, tokens, _ = dq.shape
    width = x.shape[1]
    columns = 3 * LANES * heads
    stacked = pl.BlockSpec((heads, BLOCK, LANES), lambda i: (0, i, 0))
    return pl.pallas_call(
        functools.partial(project_grad_kernel, heads),
        grid=(tokens // BLOCK,),
        in_specs=[
            pl.BlockSpec((BLOCK, width), lambda i: (i, 0)),
            stacked,
            stacked,
            pl.BlockSpec((BLOCK, LANES), lambda i: (i, 0)),
        ],
        out_specs=[
            pl.BlockSpec((width, columns), lambda i: (0, 0)),
            pl.BlockSpec((1, columns), lambda i: (0, 0)),
        ],
        out_shape=[
            jax.ShapeDtypeStruct((width, columns), bf16),
            jax.ShapeDtypeStruct((1, columns), f32),
        ],
        scratch_shapes=[pltpu.VMEM((width, columns), f32), pltpu.VMEM((1, columns), f32)],
        compiler_params=params(),
        cost_estimate=cost(2 * tokens * width * columns, 2 * tokens * (columns + width)),
        name="project_grad",
    )(x, dq, dkv, ent)


def local(
    hidden_in, token_types, lengths, cotangent, query_w, query_b, key_w, value_w, value_b, out_w,
    out_b, gain_one, shift_one, inter_w, inter_b, output_w, output_b, gain_two, shift_two,
):
    groups = lax.axis_size("tensor")
    dp = lax.axis_size("dp")
    z = lax.axis_index("tensor")
    d = lax.axis_index("dp")
    half = groups // 2
    core = d % 2
    upper = z // half
    me = z % half + half * core
    me_ref = me.astype(jnp.int32).reshape(1)
    own_rows, width = hidden_in.shape
    length = own_rows * groups
    gwidth = query_w.shape[2]
    heads = gwidth // HD
    ffn = inter_w.shape[1]
    total = dp * groups

    def at(dev):
        return dev // groups, dev % groups

    def device(dd, zz):
        return dd * groups + zz

    def swapped(dev):
        dd, zz = at(dev)
        return device(dd - dd % 2 + zz // half, zz % half + half * (dd % 2))

    def member(dev, mask):
        dd, zz = at(dev)
        j = (zz % half + half * (dd % 2)) ^ mask
        return device(dd - dd % 2 + j // half, zz - zz % half + j % half)

    relocation = [(i, swapped(i)) for i in range(total)]

    def relocate(value):
        return lax.ppermute(value, ("dp", "tensor"), relocation)

    def to_member(value, mask):
        return lax.ppermute(value, ("dp", "tensor"), [(i, member(i, mask)) for i in range(total)])

    facts = jnp.concatenate([token_types, lengths])
    other = lax.ppermute(facts, "dp", [(i, i ^ 1) for i in range(dp)])
    facts = jnp.where(core == upper, facts, other)
    entity = facts[:length].astype(f32)
    positions = jnp.arange(length, dtype=jnp.int32)
    valid = positions < facts[length]
    ent = jnp.broadcast_to(entity[:, None], (length, LANES))
    bias = jnp.broadcast_to(jnp.where(valid, 0.0, MASKED)[:, None], (length, LANES)).astype(f32)
    valid_own = lax.dynamic_slice_in_dim(valid.astype(f32), me * own_rows, own_rows)
    valid_own = jnp.broadcast_to(valid_own[:, None], (own_rows, LANES))

    rows = key_w.shape[0]
    own_project = jnp.concatenate(
        [
            query_w.reshape(4, rows, heads, HD).transpose(1, 2, 0, 3),
            key_w.reshape(rows, heads, 1, HD),
            value_w.reshape(rows, heads, 1, HD),
        ],
        2,
    ).reshape(rows, 6 * gwidth)
    own_ffn = jnp.concatenate([inter_w, output_w.T, out_w.T], 1)

    hidden = relocate(hidden_in)
    from_core = to_member(hidden, half)
    pair = jnp.stack([hidden, from_core])
    other_pair = to_member(pair, 1)
    pieces = [pair[0], other_pair[0], pair[1], other_pair[1]]
    x = jnp.zeros((groups, own_rows, width), bf16)
    for m, piece in enumerate(pieces):
        x = lax.dynamic_update_index_in_dim(x, piece, me ^ m, 0)
    x = x.reshape(length, width)

    w_project = relocate(lax.all_gather(own_project, "dp", axis=0, tiled=True))
    w_ffn = lax.all_gather(lax.all_gather(own_ffn, "tensor"), "dp", axis=1, tiled=True)

    query_b_own = lax.dynamic_slice_in_dim(query_b, me * gwidth, gwidth, 1)
    value_b_own = lax.dynamic_slice_in_dim(value_b, me * gwidth, gwidth)
    b_project = jnp.concatenate(
        [
            query_b_own.reshape(4, heads, HD).transpose(1, 0, 2),
            jnp.zeros((heads, 1, HD), bf16),
            value_b_own.reshape(heads, 1, HD),
        ],
        1,
    ).reshape(1, 6 * gwidth).astype(f32)

    qc, kc, kv = project(x, w_project, b_project, ent)
    mixed, lse = attend(me_ref, qc, kc, kv, bias)
    mixed_own = [mixed[:1]] + [to_member(mixed[m : m + 1], m) for m in range(1, groups)]
    cot = relocate(cotangent)
    row = lambda v: v.reshape(1, -1)
    y, mixt, nb, act, gi, gf, ga, gm, grad_resid_one, sums, gib = per_token(
        me_ref, mixed_own, hidden, cot, valid_own, w_ffn, row(out_b), row(gain_one), row(shift_one),
        inter_b.reshape(groups, 1, ffn), row(output_b), row(gain_two), row(shift_two),
    )
    layer_out = relocate(y)
    grad_mixed = jnp.concatenate([gm[:1]] + [to_member(gm[m : m + 1], m) for m in range(1, groups)])
    ffn_grads = weight_grads(nb, gf, ga, act, gi, mixt)
    ffn_grads = lax.psum_scatter(ffn_grads, "tensor", scatter_dimension=0, tiled=False)
    ffn_grads = lax.psum_scatter(ffn_grads, "dp", scatter_dimension=0, tiled=True).astype(f32)

    dq, dkv = attend_back(me_ref, qc, kc, kv, bias, ent, lse, mixed, grad_mixed)
    partial = input_grad(me_ref, dq, dkv, ent, w_project)
    project_grads, project_sums = project_grad(x, dq, dkv, ent)

    arrived = to_member(partial[half:], half)
    near = partial[:half].astype(f32) + arrived.astype(f32)
    arrived = to_member(near[1].astype(bf16), 1)
    grad_hidden = grad_resid_one + near[0] + arrived.astype(f32)
    grad_hidden = relocate(grad_hidden.astype(bf16)).astype(f32)

    project_grads = relocate(project_grads)
    project_grads = lax.psum_scatter(project_grads, "dp", scatter_dimension=0, tiled=True).astype(f32)
    project_grads = project_grads.reshape(rows, heads, 6, HD)
    query_grads = project_grads[:, :, :4].transpose(2, 0, 1, 3).reshape(4, rows, gwidth)
    key_grads = project_grads[:, :, 4].reshape(rows, gwidth)
    value_grads = project_grads[:, :, 5].reshape(rows, gwidth)

    inter_grads = ffn_grads[:, :ffn]
    output_grads = ffn_grads[:, ffn : 2 * ffn].T
    out_grads = ffn_grads[:, 2 * ffn :].T

    project_sums = project_sums.reshape(heads, 6, HD)
    sum_rows = jnp.concatenate(
        [
            project_sums[:, :4].transpose(1, 0, 2).reshape(4, gwidth),
            project_sums[:, 5].reshape(1, gwidth),
        ]
    )
    sum_rows = lax.dynamic_update_slice_in_dim(jnp.zeros((5, width), f32), sum_rows, me * gwidth, 1)
    flat = jnp.concatenate([sum_rows, sums.reshape(6, width), gib.reshape(groups, ffn)])
    flat = lax.psum(flat, ("dp", "tensor"))
    return (
        layer_out,
        grad_hidden,
        query_grads,
        flat[:4],
        key_grads,
        value_grads,
        flat[4],
        out_grads,
        flat[5],
        flat[6],
        flat[7],
        inter_grads,
        flat[11:].reshape(groups * ffn),
        output_grads,
        flat[8],
        flat[9],
        flat[10],
    )


def solution(mesh):
    weights = P("dp", "tensor")
    tokens = P(("dp", "tensor"), None)
    return jax.shard_map(
        local,
        mesh=mesh,
        in_specs=(
            tokens, P("dp"), P("dp"), tokens, P(None, "dp", "tensor"), P(), weights, weights, P(),
            P("tensor", "dp"), P(), P(), P(), weights, P(), P("tensor", "dp"), P(), P(), P(),
        ),
        out_specs=(
            tokens, tokens, P(None, "dp", "tensor"), P(), weights, weights, P(), P("tensor", "dp"),
            P(), P(), P(), weights, P(), P("tensor", "dp"), P(), P(), P(),
        ),
        check_vma=False,
    )
```

```python
import functools

import jax
import jax.numpy as jnp
from jax import lax
from jax.experimental import pallas as pl
from jax.experimental.pallas import tpu as pltpu
from jax.sharding import PartitionSpec as P

HD = 64
BLOCK = 512
LANES = 128
EPS = 1e-05
MASKED = -1e30
SQRT_HALF = 0.7071067811865476
INV_SQRT_2PI = 0.3989422804014327
VMEM_LIMIT = 60000 * 1024

f32 = jnp.float32
bf16 = jnp.bfloat16


def dot_nn(a, b):
    return lax.dot_general(a, b, (((1,), (0,)), ((), ())), preferred_element_type=f32)


def dot_nt(a, b):
    return lax.dot_general(a, b, (((1,), (1,)), ((), ())), preferred_element_type=f32)


def params(**kw):
    return pltpu.CompilerParams(vmem_limit_bytes=VMEM_LIMIT, **kw)


def cost(flops, nbytes, transcendentals=0, short=1):
    return pl.CostEstimate(
        flops=7 * flops // (2 * short), bytes_accessed=nbytes // short, transcendentals=transcendentals
    )


def copies(jobs, sems):
    started = []
    for at, (source, target) in enumerate(jobs):
        copy = pltpu.make_async_copy(source, target, sems.at[at])
        copy.start()
        started.append(copy)
    return started


def block_rows(index, rows):
    return pl.ds(pl.multiple_of(index * rows, rows), rows)


def head_columns(heads):
    return [[HD * (part * heads + h) for part in range(6)] for h in range(heads)]


def by_heads(value, heads):
    cols = [value[:, at : at + HD] for parts in head_columns(heads) for at in parts]
    return jnp.concatenate(cols, 1)


def by_parts(value, heads):
    cols = [value[:, HD * (6 * h + part) : HD * (6 * h + part + 1)] for part in range(6) for h in range(heads)]
    return jnp.concatenate(cols, 1)


def project_weight_jobs(layout, pos_ref, refs, w_ref):
    jobs = []
    chip = pos_ref[2] // 2
    for (masks, second), ref in zip(layout, refs):
        if masks is None:
            jobs.append((ref, w_ref))
            continue
        for u, mask in enumerate(masks):
            source = ref.at[u] if len(masks) > 1 else ref
            jobs.append((source, w_ref.at[block_rows(2 * (chip ^ mask) + second, source.shape[0])]))
    return jobs


def project_kernel(heads, layout, pos_ref, x0, x1, x2, x3, b_ref, ent_ref, *rest):
    count = len(layout)
    pieces = rest[:count]
    qc_ref, kc_ref, kv_ref, w_ref, x_ref, raw_ref, b_scr, sems = rest[count:]

    @pl.when(pl.program_id(0) == 0)
    def _():
        jobs = [(ref, x_ref.at[m]) for m, ref in enumerate((x0, x1, x2, x3))]
        for copy in copies(jobs + project_weight_jobs(layout, pos_ref, pieces, raw_ref), sems):
            copy.wait()
        w_ref[...] = by_heads(raw_ref[...], heads)
        b_scr[...] = by_heads(jnp.broadcast_to(b_ref[...], b_scr.shape), heads)

    x = x_ref[pl.program_id(0)]
    ent = ent_ref[...] > 0.5
    lane = lax.broadcasted_iota(jnp.int32, (x.shape[0], LANES), 1)
    low_half = lane < HD
    keep = jnp.logical_xor(low_half, ent)
    for h in range(heads):
        base = 3 * LANES * h
        y = dot_nn(x, w_ref[:, base : base + 3 * LANES]) + b_scr[:1, base : base + 3 * LANES]
        q = jnp.where(ent, y[:, LANES : 2 * LANES], y[:, :LANES])
        qc_ref[h] = q.astype(bf16) * (HD ** (-0.5))
        kv = y[:, 2 * LANES :].astype(bf16).astype(f32)
        kv_ref[h] = kv.astype(bf16)
        twice = jnp.where(low_half, kv, pltpu.roll(kv, HD, 1))
        kc_ref[h] = jnp.where(keep, twice, 0.0).astype(bf16)


def project(pos, x, pieces, layout, b, ent):
    own_rows, width = x[0].shape
    tokens = own_rows * len(x)
    columns = b.shape[1]
    heads = columns // (3 * LANES)
    out = jax.ShapeDtypeStruct((heads, tokens, LANES), bf16)
    spec = pl.BlockSpec((heads, own_rows, LANES), lambda m, pos: (0, m ^ pos[0], 0))
    anywhere = pl.BlockSpec(memory_space=pl.ANY)
    jobs = sum(1 if masks is None else len(masks) for masks, _ in layout)
    return pl.pallas_call(
        functools.partial(project_kernel, heads, layout),
        grid_spec=pltpu.PrefetchScalarGridSpec(
            num_scalar_prefetch=1,
            grid=(len(x),),
            in_specs=[anywhere] * 4
            + [
                pl.BlockSpec((1, columns), lambda m, pos: (0, 0)),
                pl.BlockSpec((own_rows, LANES), lambda m, pos: (m ^ pos[0], 0)),
            ]
            + [anywhere] * len(pieces),
            out_specs=[spec, spec, spec, pl.BlockSpec((width, columns), lambda m, pos: (0, 0))],
            scratch_shapes=[
                pltpu.VMEM((len(x), own_rows, width), bf16),
                pltpu.VMEM((width, columns), bf16),
                pltpu.VMEM((8, columns), f32),
                pltpu.SemaphoreType.DMA((len(x) + jobs,)),
            ],
        ),
        out_shape=[out, out, out, jax.ShapeDtypeStruct((width, columns), bf16)],
        compiler_params=params(),
        cost_estimate=cost(2 * tokens * width * columns, 2 * tokens * (width + columns)),
        name="project",
    )(pos, *x, b, ent, *pieces)


def masked_keys(pos_ref, scores):
    keys = lax.broadcasted_iota(jnp.int32, (scores.shape[0], 1), 0)
    return scores + jnp.where(keys < pos_ref[4], 0.0, MASKED)


def attend_kernel(pos_ref, q_ref, kc_ref, kv_ref, *rest):
    out_ref, lse_ref, vt_ref = rest[-3:]

    @pl.when(pl.program_id(1) == 0)
    def _():
        vt_ref[...] = kv_ref[0].T[HD:]

    scores = masked_keys(pos_ref, dot_nt(kc_ref[0], q_ref[0]))
    top = jnp.max(scores, 0, keepdims=True)
    exponent = jnp.exp(scores - top)
    total = jnp.sum(exponent, 0, keepdims=True)
    mixed = dot_nn(vt_ref[...], exponent.astype(bf16))
    out_ref[0] = (mixed / total).astype(bf16)
    lse_ref[0] = top + jnp.log(total)


def attend(pos, first, count, qc, kc, kv, before=()):
    heads, tokens, _ = qc.shape
    blocks = tokens // BLOCK
    full = pl.BlockSpec((1, tokens, LANES), lambda h, i, pos: (first + h, 0, 0))
    return pl.pallas_call(
        attend_kernel,
        grid_spec=pltpu.PrefetchScalarGridSpec(
            num_scalar_prefetch=1,
            grid=(count, blocks),
            in_specs=[pl.BlockSpec((1, BLOCK, LANES), lambda h, i, pos: (first + h, i, 0)), full, full]
            + [pl.BlockSpec(memory_space=pl.ANY)] * len(before),
            out_specs=[
                pl.BlockSpec((1, HD, BLOCK), lambda h, i, pos: (i ^ pos[0], first + h, 0)),
                pl.BlockSpec((1, 1, BLOCK), lambda h, i, pos: (h, 0, i)),
            ],
            scratch_shapes=[pltpu.VMEM((HD, tokens), bf16)],
        ),
        out_shape=[
            jax.ShapeDtypeStruct((blocks, heads * HD, BLOCK), bf16),
            jax.ShapeDtypeStruct((count, 1, tokens), f32),
        ],
        input_output_aliases={4: 0} if before else {},
        compiler_params=params(),
        cost_estimate=cost(count * tokens * tokens * 2 * 3 * LANES, count * tokens * 8 * LANES),
        name="attend",
    )(pos, qc, kc, kv, *before)


def attend_back_kernel(
    pos_ref, q_ref, kc_ref, kv_ref, ent_ref, lse_ref, out_ref, go_ref,
    dq_ref, dkv_ref, kt_ref, dk_acc, dv_acc, go_pad,
):
    step = pl.program_id(1)

    @pl.when(step == 0)
    def _():
        kt_ref[...] = kc_ref[0].T
        go_pad[:HD] = jnp.zeros((HD, go_pad.shape[1]), bf16)
        dk_acc[...] = jnp.zeros_like(dk_acc)
        dv_acc[...] = jnp.zeros_like(dv_acc)

    go = go_ref[0]
    go_pad[HD:] = go
    delta = jnp.sum(go.astype(f32) * out_ref[0].astype(f32), 0, keepdims=True)
    q = q_ref[0]
    scores = masked_keys(pos_ref, dot_nt(kc_ref[0], q))
    probs = jnp.exp(scores - lse_ref[0])
    grad_probs = dot_nn(kv_ref[0], go_pad[...])
    grad_scores = (probs * (grad_probs - delta)).astype(bf16)
    dv_acc[...] += dot_nt(probs.astype(bf16), go_pad[...])
    dk_acc[...] += dot_nn(grad_scores, q)
    dq_ref[0] = (dot_nn(kt_ref[...], grad_scores) * (HD ** (-0.5))).T.astype(bf16)

    @pl.when(step == pl.num_programs(1) - 1)
    def _():
        lane = lax.broadcasted_iota(jnp.int32, dk_acc.shape, 1)
        dk = dk_acc[...]
        dk = jnp.where(ent_ref[...] > 0.5, pltpu.roll(dk, HD, 1), dk)
        dkv_ref[0] = jnp.where(lane < HD, dk, dv_acc[...]).astype(bf16)


def attend_back(pos, first, count, qc, kc, kv, ent, lse, mixed, grad_mixed):
    tokens = qc.shape[1]
    blocks = tokens // BLOCK
    full = pl.BlockSpec((1, tokens, LANES), lambda h, i, pos: (first + h, 0, 0))
    slot = pl.BlockSpec((1, HD, BLOCK), lambda h, i, pos: (i ^ pos[0], first + h, 0))
    out = jax.ShapeDtypeStruct((count, tokens, LANES), bf16)
    return pl.pallas_call(
        attend_back_kernel,
        grid_spec=pltpu.PrefetchScalarGridSpec(
            num_scalar_prefetch=1,
            grid=(count, blocks),
            in_specs=[
                pl.BlockSpec((1, BLOCK, LANES), lambda h, i, pos: (first + h, i, 0)),
                full, full,
                pl.BlockSpec((tokens, LANES), lambda h, i, pos: (0, 0)),
                pl.BlockSpec((1, 1, BLOCK), lambda h, i, pos: (h, 0, i)),
                slot, slot,
            ],
            out_specs=[
                pl.BlockSpec((1, BLOCK, LANES), lambda h, i, pos: (h, i, 0)),
                pl.BlockSpec((1, tokens, LANES), lambda h, i, pos: (h, 0, 0)),
            ],
            scratch_shapes=[
                pltpu.VMEM((LANES, tokens), bf16),
                pltpu.VMEM((tokens, LANES), f32),
                pltpu.VMEM((tokens, LANES), f32),
                pltpu.VMEM((LANES, BLOCK), bf16),
            ],
        ),
        out_shape=[out, out],
        compiler_params=params(),
        cost_estimate=cost(count * tokens * tokens * 2 * 5 * LANES, count * tokens * 16 * LANES),
        name="attend_back",
    )(pos, qc, kc, kv, ent, lse, mixed, grad_mixed)


def normed(residual, gain, shift):
    center = residual - jnp.mean(residual, -1, keepdims=True)
    inv = lax.rsqrt(jnp.mean(center * center, -1, keepdims=True) + EPS)
    unit = center * inv
    return unit, inv, unit * gain + shift


def norm_back(grad, unit, inv, gain):
    scaled = grad * gain
    return (
        scaled
        - jnp.mean(scaled, -1, keepdims=True)
        - unit * jnp.mean(scaled * unit, -1, keepdims=True)
    ) * inv


def token_weight_jobs(layout, pos_ref, refs, w_ref):
    jobs = []
    for masks, ref in zip(layout, refs):
        if masks is None:
            jobs.append((ref, w_ref))
            continue
        for u, (mask, group_mask) in enumerate(masks):
            where = block_rows(pos_ref[2] ^ mask, ref.shape[1])
            jobs.append((ref.at[u], w_ref.at[pos_ref[1] ^ group_mask, where]))
    return jobs


def token_kernel(
    layout, pos_ref, m0, m1, m2, m3, hid_ref, cot_ref, valid_ref, vec_ref, *rest
):
    count = len(layout)
    pieces = rest[:count]
    (
        y_ref, mixt_ref, nb_ref, act_ref, gi_ref, gf_ref, ga_ref, gm_ref, gr_ref, sums_ref, gib_ref,
        slope_ref, outt_ref, w_ref, sems,
    ) = rest[count:]
    loads = copies(token_weight_jobs(layout, pos_ref, pieces, w_ref), sems)
    for load in loads:
        load.wait()
    me = pos_ref[0]
    groups, width, _ = w_ref.shape
    ffn = act_ref.shape[2]
    gwidth = mixt_ref.shape[1]
    out_at = 2 * ffn
    for m, ref in enumerate((m0, m1, m2, m3)):
        mixt_ref[me ^ m] = ref[0]
    out_b, gain_one, shift_one, output_b, gain_two, shift_two = (vec_ref[at : at + 1] for at in range(6))
    attended = out_b
    for g in range(groups):
        part = dot_nt(mixt_ref[g].T, w_ref[g, :, out_at : out_at + gwidth])
        attended = attended + part.astype(bf16).astype(f32)
    unit_one, inv_one, normed_one = normed(hid_ref[...].astype(f32) + attended, gain_one, shift_one)
    low_one = normed_one.astype(bf16)
    nb_ref[...] = low_one

    def forward(g, total):
        pre = dot_nn(low_one, w_ref[g, :, :ffn]) + vec_ref[pl.ds(6 + g, 1)]
        cdf = 0.5 * (1.0 + lax.erf(pre * SQRT_HALF))
        slope_ref[g] = cdf + pre * (jnp.exp(-0.5 * pre * pre) * INV_SQRT_2PI)
        active = (pre * cdf).astype(bf16)
        act_ref[g] = active
        part = dot_nt(active, w_ref[g, :, ffn:out_at])
        return total + part.astype(bf16).astype(f32)

    ffn_out = lax.fori_loop(
        0, groups, forward, jnp.broadcast_to(output_b, normed_one.shape)
    )
    valid = valid_ref[:, :1]
    unit_two, inv_two, normed_two = normed(normed_one + ffn_out, gain_two, shift_two)
    y_ref[...] = (normed_two * valid).astype(bf16)
    grad_top = cot_ref[...].astype(f32) * valid
    grad_resid_two = norm_back(grad_top, unit_two, inv_two, gain_two)
    grad_ffn = grad_resid_two.astype(bf16)
    gf_ref[...] = grad_ffn

    def backward(g, total):
        grad_active = dot_nn(grad_ffn, w_ref[g, :, ffn:out_at])
        grad_inner = (slope_ref[g] * grad_active).astype(bf16)
        gi_ref[g] = grad_inner
        gib_ref[g] = jnp.sum(grad_inner.astype(f32), 0, keepdims=True)
        part = dot_nt(grad_inner, w_ref[g, :, :ffn])
        return total + part.astype(bf16).astype(f32)

    grad_normed = lax.fori_loop(0, groups, backward, grad_resid_two)
    grad_resid_one = norm_back(grad_normed, unit_one, inv_one, gain_one)
    gr_ref[...] = grad_resid_one
    grad_att = grad_resid_one.astype(bf16)
    ga_ref[...] = grad_att
    for g in range(groups):
        outt_ref[g] = w_ref[g, :, out_at : out_at + gwidth].T
    for m in range(groups):
        gm_ref[m] = dot_nt(outt_ref[me ^ m], grad_att).astype(bf16)
    rows = (
        grad_att.astype(f32),
        grad_normed * unit_one,
        grad_normed,
        grad_ffn.astype(f32),
        grad_top * unit_two,
        grad_top,
    )
    for at, value in enumerate(rows):
        sums_ref[at] = jnp.sum(value, 0, keepdims=True)


def per_token(
    pos, mixed, hidden, cot, valid, vectors, pieces, layout, groups, columns
):
    tokens, width = hidden.shape
    ffn = vectors.shape[1]
    gwidth = mixed[0].shape[1]
    vmem = pl.BlockSpec(memory_space=pltpu.VMEM)
    shape = jax.ShapeDtypeStruct
    jobs = sum(1 if masks is None else len(masks) for masks in layout)
    return pl.pallas_call(
        functools.partial(token_kernel, layout),
        in_specs=[pl.BlockSpec(memory_space=pltpu.SMEM)]
        + [vmem] * 8
        + [pl.BlockSpec(memory_space=pl.ANY)] * len(pieces),
        out_specs=[vmem] * 11,
        out_shape=[
            shape((tokens, width), bf16),
            shape((groups, gwidth, tokens), bf16),
            shape((tokens, width), bf16),
            shape((groups, tokens, ffn), bf16),
            shape((groups, tokens, ffn), bf16),
            shape((tokens, width), bf16),
            shape((tokens, width), bf16),
            shape((groups, gwidth, tokens), bf16),
            shape((tokens, width), f32),
            shape((6, 1, width), f32),
            shape((groups, 1, ffn), f32),
        ],
        scratch_shapes=[
            pltpu.VMEM((groups, tokens, ffn), f32),
            pltpu.VMEM((groups, gwidth, width), bf16),
            pltpu.VMEM((groups, width, columns), bf16),
            pltpu.SemaphoreType.DMA((jobs,)),
        ],
        compiler_params=params(),
        cost_estimate=cost(
            8 * tokens * width * ffn * groups + 4 * tokens * width * width,
            2 * groups * width * columns + 4 * tokens * ffn * groups,
            2 * tokens * ffn * groups,
        ),
        name="per_token",
    )(pos, *mixed, hidden, cot, valid, vectors, *pieces)


def weight_grad_kernel(
    pos_ref, nb_ref, gf_ref, ga_ref, act_ref, gi_ref, mixt_ref, near_ref, far_ref, nbt, gft, gat, turn
):
    ffn = act_ref.shape[2]
    gwidth = mixt_ref.shape[1]
    chips, _, rows, _ = near_ref.shape

    @pl.when(pl.program_id(0) == 0)
    def _():
        for target, source in ((nbt, nb_ref), (gft, gf_ref), (gat, ga_ref)):
            turn[...] = source[...].T
            for mine in range(2):
                for mask in range(chips):
                    block = pos_ref[2] ^ (2 * mask + mine)
                    at = (mine * chips + mask) * rows
                    target[at : at + rows] = turn[block_rows(block, rows)]

    second_half = (pl.program_id(0) ^ pos_ref[1]) % 2

    def put(value, start, stop):
        for mine, out_ref in enumerate((near_ref, far_ref)):
            for mask in range(chips):
                slot = mask + second_half - 1 if mask == 2 else mask + 1 - second_half if mask == 1 else mask
                at = (mine * chips + mask) * rows
                out_ref[slot, 0, :, start:stop] = value[at : at + rows].astype(bf16)

    put(dot_nn(nbt[...], gi_ref[0]), 0, ffn)
    put(dot_nn(gft[...], act_ref[0]), ffn, 2 * ffn)
    put(dot_nt(gat[...], mixt_ref[0]), 2 * ffn, 2 * ffn + gwidth)


def weight_grads(pos, nb, gf, ga, act, gi, mixt, dp):
    groups, tokens, ffn = act.shape
    width = nb.shape[1]
    gwidth = mixt.shape[1]
    rows = width // dp
    whole = pl.BlockSpec((tokens, width), lambda g, pos: (0, 0))
    group = pl.BlockSpec((1, tokens, ffn), lambda g, pos: (g, 0, 0))
    columns = 2 * ffn + gwidth
    out = jax.ShapeDtypeStruct((dp // 2, groups, rows, columns), bf16)

    def slot(g, pos):
        mask = g ^ pos[1]
        return (0, 2 * (mask % 2) + mask // 2, 0, 0)

    spec = pl.BlockSpec((dp // 2, 1, rows, columns), slot)
    return pl.pallas_call(
        weight_grad_kernel,
        grid_spec=pltpu.PrefetchScalarGridSpec(
            num_scalar_prefetch=1,
            grid=(groups,),
            in_specs=[
                whole, whole, whole, group, group,
                pl.BlockSpec((1, gwidth, tokens), lambda g, pos: (g, 0, 0)),
            ],
            out_specs=[spec, spec],
            scratch_shapes=[pltpu.VMEM((width, tokens), bf16)] * 4,
        ),
        out_shape=[out, out],
        compiler_params=params(),
        cost_estimate=cost(2 * tokens * width * columns * groups, 2 * groups * width * columns),
        name="weight_grads",
    )(pos, nb, gf, ga, act, gi, mixt)


def weight_grad_whole_kernel(nb_ref, gf_ref, ga_ref, act_ref, gi_ref, mixt_ref, out_ref, nbt, gft, gat):
    ffn = act_ref.shape[2]
    gwidth = mixt_ref.shape[1]

    @pl.when(pl.program_id(0) == 0)
    def _():
        nbt[...] = nb_ref[...].T
        gft[...] = gf_ref[...].T
        gat[...] = ga_ref[...].T

    out_ref[0, :, :ffn] = dot_nn(nbt[...], gi_ref[0]).astype(bf16)
    out_ref[0, :, ffn : 2 * ffn] = dot_nn(gft[...], act_ref[0]).astype(bf16)
    out_ref[0, :, 2 * ffn : 2 * ffn + gwidth] = dot_nt(gat[...], mixt_ref[0]).astype(bf16)


def weight_grads_whole(nb, gf, ga, act, gi, mixt):
    groups, tokens, ffn = act.shape
    width = nb.shape[1]
    gwidth = mixt.shape[1]
    whole = pl.BlockSpec((tokens, width), lambda g: (0, 0))
    group = pl.BlockSpec((1, tokens, ffn), lambda g: (g, 0, 0))
    columns = 2 * ffn + gwidth
    return pl.pallas_call(
        weight_grad_whole_kernel,
        grid=(groups,),
        in_specs=[whole, whole, whole, group, group, pl.BlockSpec((1, gwidth, tokens), lambda g: (g, 0, 0))],
        out_specs=pl.BlockSpec((1, width, columns), lambda g: (g, 0, 0)),
        out_shape=jax.ShapeDtypeStruct((groups, width, columns), bf16),
        scratch_shapes=[pltpu.VMEM((width, tokens), bf16)] * 3,
        compiler_params=params(),
        cost_estimate=cost(2 * tokens * width * columns * groups, 2 * groups * width * columns),
        name="weight_grads_whole",
    )(nb, gf, ga, act, gi, mixt)


def split_columns(pairs, ent):
    h = 0
    for dq_ref, dkv_ref in pairs:
        for u in range(dq_ref.shape[0]):
            dq = dq_ref[u]
            nothing = jnp.zeros_like(dq)
            yield 3 * h, jnp.where(ent, nothing, dq)
            yield 3 * h + 1, jnp.where(ent, dq, nothing)
            yield 3 * h + 2, dkv_ref[u]
            h += 1


def input_grad_kernel(count, pos_ref, *refs):
    grads, (ent_ref, w_ref, out_ref) = refs[:count], refs[count:]
    ent = ent_ref[...] > 0.5
    cols = [c for _, c in split_columns(list(zip(grads[::2], grads[1::2])), ent)]
    out_ref[0] = dot_nt(jnp.concatenate(cols, 1), w_ref[...]).astype(bf16)


def input_grad(pos, grads, ent, w, far):
    tokens = grads[0].shape[1]
    width, columns = w.shape

    def block(i, pos):
        return i + 2 * (pos[3] ^ far)

    stacked = [pl.BlockSpec((g.shape[0], BLOCK, LANES), lambda i, pos: (0, block(i, pos), 0)) for g in grads]
    return pl.pallas_call(
        functools.partial(input_grad_kernel, len(grads)),
        grid_spec=pltpu.PrefetchScalarGridSpec(
            num_scalar_prefetch=1,
            grid=(2,),
            in_specs=stacked
            + [
                pl.BlockSpec((BLOCK, LANES), lambda i, pos: (block(i, pos), 0)),
                pl.BlockSpec((width, columns), lambda i, pos: (0, 0)),
            ],
            out_specs=pl.BlockSpec((1, BLOCK, width), lambda i, pos: (i ^ (pos[0] % 2), 0, 0)),
        ),
        out_shape=jax.ShapeDtypeStruct((2, BLOCK, width), bf16),
        compiler_params=params(),
        cost_estimate=cost(tokens * width * columns, tokens * (columns + width), short=100),
        name="input_grad",
    )(pos, *grads, ent, w)


def project_grad_kernel(count, earlier, pos_ref, x0, x1, x2, x3, *refs):
    grads = refs[:count]
    before = refs[count : count + earlier]
    ent_ref, out_ref, bias_ref, acc_ref, bias_acc, x_ref, sems = refs[count + earlier :]
    step = pl.program_id(0)

    @pl.when(step == 0)
    def _():
        loads = copies([(ref, x_ref.at[m]) for m, ref in enumerate((x0, x1, x2, x3))], sems)
        acc_ref[...] = jnp.zeros_like(acc_ref)
        bias_acc[...] = jnp.zeros_like(bias_acc)
        for load in loads:
            load.wait()

    ent = ent_ref[...] > 0.5
    xt = x_ref[step].T
    for at, column in split_columns(list(zip(grads[::2], grads[1::2])), ent):
        where = slice(LANES * at, LANES * (at + 1))
        acc_ref[:, where] += dot_nn(xt, column)
        bias_acc[:1, where] += jnp.sum(column.astype(f32), 0, keepdims=True)

    @pl.when(step == pl.num_programs(0) - 1)
    def _():
        if len(out_ref.shape) == 2:
            out_ref[...] = acc_ref[...].astype(bf16)
            bias_ref[...] = bias_acc[...]
            return
        chips, cores, rows, columns = out_ref.shape
        heads = columns // (3 * LANES)
        for mask in range(chips):
            at = block_rows((pos_ref[2] // cores) ^ mask, cores * rows)
            block = jnp.concatenate([ref[at] for ref in before[:1]] + [acc_ref[at].astype(bf16)], 1)
            out_ref[mask] = by_parts(block, heads).reshape(out_ref.shape[1:])
        bias_ref[...] = by_parts(jnp.concatenate([ref[...] for ref in before[1:]] + [bias_acc[...]], 1), heads)


def project_grad(pos, x, grads, ent, blocks=None, before=()):
    heads = sum(g.shape[0] for g in grads) // 2
    tokens = grads[0].shape[1]
    own_rows, width = x[0].shape
    columns = 3 * LANES * heads
    all_columns = columns + sum(b.shape[1] for b in before[:1])
    shape = (width, columns) if blocks is None else (*blocks, width // (blocks[0] * blocks[1]), all_columns)
    stacked = [pl.BlockSpec((g.shape[0], own_rows, LANES), lambda m, pos: (0, m ^ pos[0], 0)) for g in grads]

    def fixed(shape):
        return pl.BlockSpec(shape, lambda m, pos: (0,) * len(shape))

    return pl.pallas_call(
        functools.partial(project_grad_kernel, len(grads), len(before)),
        grid_spec=pltpu.PrefetchScalarGridSpec(
            num_scalar_prefetch=1,
            grid=(len(x),),
            in_specs=[pl.BlockSpec(memory_space=pl.ANY)] * 4
            + stacked
            + [fixed(b.shape) for b in before]
            + [pl.BlockSpec((own_rows, LANES), lambda m, pos: (m ^ pos[0], 0))],
            out_specs=[fixed(shape), fixed((8, all_columns))],
            scratch_shapes=[
                pltpu.VMEM((width, columns), f32),
                pltpu.VMEM((8, columns), f32),
                pltpu.VMEM((len(x), own_rows, width), bf16),
                pltpu.SemaphoreType.DMA((len(x),)),
            ],
        ),
        out_shape=[jax.ShapeDtypeStruct(shape, bf16), jax.ShapeDtypeStruct((8, all_columns), f32)],
        compiler_params=params(),
        cost_estimate=cost(2 * tokens * width * columns, 2 * tokens * (columns + width), short=100),
        name="project_grad",
    )(pos, *x, *grads, *before, ent)


def finish_project_kernel(kept_ref, arrived_ref, q_ref, k_ref, v_ref):
    total = kept_ref[...].astype(f32) + arrived_ref[...].astype(f32)
    width = k_ref.shape[1]
    for a in range(q_ref.shape[0]):
        q_ref[a] = total[:, width * a : width * (a + 1)]
    k_ref[...] = total[:, 4 * width : 5 * width]
    v_ref[...] = total[:, 5 * width :]


def finish_project(kept, arrived):
    rows, columns = kept.shape
    part = jax.ShapeDtypeStruct((rows, columns // 6), f32)
    return pl.pallas_call(
        finish_project_kernel,
        out_shape=[jax.ShapeDtypeStruct((4, rows, columns // 6), f32), part, part],
        compiler_params=params(),
        cost_estimate=cost(rows * columns, 8 * rows * columns),
        name="finish_project",
    )(kept, arrived)


def finish_ffn_kernel(kept_ref, arrived_ref, inter_ref, output_ref, out_ref):
    total = kept_ref[...].astype(f32) + arrived_ref[...].astype(f32)
    ffn = inter_ref.shape[1]
    inter_ref[...] = total[:, :ffn]
    output_ref[...] = total[:, ffn : 2 * ffn].T
    out_ref[...] = total[:, 2 * ffn :].T


def finish_ffn(kept, arrived, ffn):
    rows, columns = kept.shape
    shape = jax.ShapeDtypeStruct
    return pl.pallas_call(
        finish_ffn_kernel,
        out_shape=[shape((rows, ffn), f32), shape((ffn, rows), f32), shape((columns - 2 * ffn, rows), f32)],
        compiler_params=params(),
        cost_estimate=cost(rows * columns, 8 * rows * columns),
        name="finish_ffn",
    )(kept, arrived)


def local(
    hidden_in, token_types, lengths, cotangent, query_w, query_b, key_w, value_w, value_b, out_w,
    out_b, gain_one, shift_one, inter_w, inter_b, output_w, output_b, gain_two, shift_two,
):
    groups = lax.axis_size("tensor")
    dp = lax.axis_size("dp")
    z = lax.axis_index("tensor")
    d = lax.axis_index("dp")
    half = groups // 2
    core = d % 2
    upper = z // half
    me = z % half + half * core
    own_rows, width = hidden_in.shape
    length = own_rows * groups
    gwidth = query_w.shape[2]
    heads = gwidth // HD
    ffn = inter_w.shape[1]
    rows = key_w.shape[0]
    columns = 2 * ffn + gwidth
    total = dp * groups
    by_hops = dp == 8 and rows % 16 == 0

    def device(dd, zz):
        return dd * groups + zz

    def swapped(dev):
        dd, zz = dev // groups, dev % groups
        return device(dd - dd % 2 + zz // half, zz % half + half * (dd % 2))

    def member(dev, mask):
        dd, zz = dev // groups, dev % groups
        j = (zz % half + half * (dd % 2)) ^ mask
        return device(dd - dd % 2 + j // half, zz - zz % half + j % half)

    stays = core == upper

    def relocate(value):
        moves = [(i, swapped(i)) for i in range(total) if swapped(i) != i]
        return jnp.where(stays, value, lax.ppermute(value, ("dp", "tensor"), moves))

    def to_member(value, mask):
        return lax.ppermute(value, ("dp", "tensor"), [(i, member(i, mask)) for i in range(total)])

    def over_dp(value, mask):
        return lax.ppermute(value, "dp", [(i, i ^ mask) for i in range(dp)])

    def over_z(value, mask):
        return lax.ppermute(value, "tensor", [(i, i ^ mask) for i in range(groups)])

    def add(*terms):
        return functools.reduce(jnp.add, [t.astype(f32) for t in terms])

    def after(value, *others):
        return lax.optimization_barrier((value, *others))[0]

    own_project = jnp.concatenate([*query_w, key_w, value_w], 1)
    own_ffn = jnp.concatenate([inter_w, output_w.T, out_w.T], 1)

    def between(value, pairs):
        return lax.ppermute(value, ("dp", "tensor"), [p for p in pairs if p[0] != p[1]])

    swaps = [(i, swapped(i)) for i in range(total)]
    on_chips = [(i, member(i, 1)) for i in range(total)]
    stay_chips = [p for p in on_chips if swapped(p[0]) == p[0]]
    move_chips = [p for p in on_chips if swapped(p[0]) != p[0]]

    def phase(*values):
        return lax.optimization_barrier(values)

    facts = jnp.concatenate([token_types, lengths])
    facts_moved = over_dp(facts, 1)
    query_b_own = lax.dynamic_slice_in_dim(query_b, me * gwidth, gwidth, 1)
    value_b_own = lax.dynamic_slice_in_dim(value_b, me * gwidth, gwidth)
    b_project = jnp.concatenate([query_b_own.reshape(-1), jnp.zeros((gwidth,), bf16), value_b_own])
    b_project = b_project.reshape(1, 6 * gwidth).astype(f32)
    vectors = jnp.concatenate(
        [out_b, gain_one, shift_one, output_b, gain_two, shift_two, inter_b]
    ).astype(f32).reshape(6 + groups, width)
    near_chip = between(hidden_in, stay_chips)
    moved = between(hidden_in, swaps)
    if by_hops:
        other = over_dp(own_project, 1)
        pair = jnp.where(core == 0, jnp.stack([own_project, other]), jnp.stack([other, own_project]))
        pair = relocate(pair)
        a, b = pair[0], pair[1]
        own_x, own_y, own_z = over_dp(own_ffn, 2), over_dp(own_ffn, 4), over_z(own_ffn, 1)
        moved, near_chip, facts_moved, a_x, b_y, own_x, own_y, own_z, b_project, vectors = phase(
            moved, near_chip, facts_moved, over_dp(a, 2), over_dp(b, 4), own_x, own_y, own_z, b_project, vectors
        )
    facts = jnp.where(stays, facts, facts_moved)
    pos = jnp.concatenate([jnp.stack([me, z, d, upper]).astype(jnp.int32), facts[length:]])
    ent = jnp.broadcast_to(facts[:length, None].astype(bf16), (length, LANES))
    valid_own = me * own_rows + jnp.arange(own_rows, dtype=jnp.int32) < facts[length]
    valid_own = jnp.broadcast_to(valid_own[:, None].astype(f32), (own_rows, LANES))
    hidden = jnp.where(stays, hidden_in, moved)
    from_chip = between(hidden, move_chips)
    if by_hops:
        from_chip, a_2, b_2, pos, ent, valid_own = phase(
            from_chip, over_dp(jnp.stack([a, a_x]), 4), over_dp(jnp.stack([b, b_y]), 2), pos, ent, valid_own
        )
        from_chip = jnp.where(stays, near_chip, from_chip)
        x_2, x_3, own_ffn = phase(to_member(hidden, half), to_member(from_chip, half), own_ffn)
        project_pieces = [a, a_x, a_2, b, b_y, b_2]
        project_layout = (((0,), 0), ((1,), 0), ((2, 3), 0), ((0,), 1), ((2,), 1), ((1, 3), 1))
    else:
        project_pieces = [relocate(lax.all_gather(own_project, "dp", axis=0, tiled=True))]
        project_layout = ((None, 0),)
        from_chip = jnp.where(stays, near_chip, from_chip)
        x_2, x_3 = to_member(hidden, half), to_member(from_chip, half)
    x = [hidden, from_chip, x_2, x_3]

    qc, kc, kv, w_project = project(pos, x, project_pieces, project_layout, b_project, ent)
    if by_hops:
        token_pieces, token_layout = [], []

        def whole(group_mask, *quad):
            masks = [(m, group_mask) for m in (0, 2, 4, 6)]
            token_layout.extend([tuple(masks), tuple((m + 1, g) for m, g in masks)])
            return jnp.stack(quad)

        own_z, own_x, own_y = after((own_z, own_x, own_y), x_3)
        qc, far, own_zx, own_zy, own_xy = phase(
            qc, over_z(own_ffn, 2), over_dp(own_z, 2), over_dp(own_z, 4), over_dp(own_x, 4)
        )
        quad = whole(0, own_ffn, own_x, own_y, own_xy)
        mixed, lse_0 = attend(pos, 0, 1, qc, kc, kv)
        mixed, far_z, far_x, far_y, quad_core = phase(
            mixed, over_z(far, 1), over_dp(far, 2), over_dp(far, 4), over_dp(quad, 1)
        )
        token_pieces += [quad, quad_core]
        mixed, lse_1 = attend(pos, 1, heads - 1, qc, kc, kv, (mixed,))
        mixed, far_zx, far_zy, far_xy, own_zxy, cot = phase(
            mixed, over_dp(far_z, 2), over_dp(far_z, 4), over_dp(far_x, 4), over_dp(own_zy, 2),
            between(after(cotangent, far_x), swaps),
        )
        cot = jnp.where(stays, cotangent, cot)
        quad = whole(1, own_z, own_zx, own_zy, own_zxy)
        mixed_own, far_zxy, quad_core, cot = phase(
            [mixed[:1]] + [to_member(mixed[m : m + 1], m) for m in range(1, groups)], over_dp(far_zy, 2),
            over_dp(quad, 1), cot
        )
        token_pieces += [quad, quad_core]
        for group_mask, quad in ((2, (far, far_x, far_y, far_xy)), (3, (far_z, far_zx, far_zy, far_zxy))):
            quad = whole(group_mask, *quad)
            token_pieces += [quad, over_dp(quad, 1)]
        token_layout = tuple(token_layout)
    else:
        token_pieces = [lax.all_gather(lax.all_gather(own_ffn, "tensor"), "dp", axis=1, tiled=True)]
        token_layout = (None,)
        mixed, lse_0 = attend(pos, 0, 1, qc, kc, kv)
        mixed, lse_1 = attend(pos, 1, heads - 1, qc, kc, kv, (mixed,))
        mixed_own = [mixed[:1]] + [to_member(mixed[m : m + 1], m) for m in range(1, groups)]
        cot = jnp.where(stays, cotangent, between(cotangent, swaps))
    y, mixt, nb, act, gi, gf, ga, gm, grad_resid_one, sums, gib = per_token(
        pos, mixed_own, hidden, cot, valid_own, vectors, token_pieces, token_layout, groups, columns
    )
    grad_mixed = jnp.concatenate([gm[:1]] + [to_member(gm[m : m + 1], m) for m in range(1, groups)])

    order = ((1, 2), (2, 1))
    if by_hops:
        near, far = weight_grads(pos, nb, gf, ga, act, gi, mixt, dp)
        arrived = over_dp(after(far, grad_mixed), 1)
        grads = attend_back(pos, 0, 1, qc, kc, kv, ent, lse_0, mixed, grad_mixed)
        groups_at = (slice(0, 2), slice(2, 4))
        kept = [add(near[:2, g], arrived[:2, g]).astype(bf16) for g in groups_at]
        sent = [add(near[2:, g], arrived[2:, g]).astype(bf16) for g in groups_at]
        grads, kept, sent, qc, y = phase(grads, kept, sent, qc, y)
        more = attend_back(pos, 1, heads - 1, qc, kc, kv, ent, lse_1, mixed, grad_mixed)
        more, moved, layer_moved = phase(
            more, [over_dp(v, 2 * one) for v, (one, _) in zip(sent, order)], between(y, swaps)
        )
    else:
        ffn_grads = weight_grads_whole(nb, gf, ga, act, gi, mixt)
        ffn_grads = lax.psum_scatter(ffn_grads, "tensor", scatter_dimension=0, tiled=False)
        ffn_grads = lax.psum_scatter(ffn_grads, "dp", scatter_dimension=0, tiled=True)
        grads = attend_back(pos, 0, 1, qc, kc, kv, ent, lse_0, mixed, grad_mixed)
        more = attend_back(pos, 1, heads - 1, qc, kc, kv, ent, lse_1, mixed, grad_mixed)
        layer_moved = between(y, swaps)
    layer_out = jnp.where(stays, y, layer_moved)
    grads = [*grads, *more]

    core_stay = [(i, i ^ groups) for i in range(total) if swapped(i) == i]
    core_move = [(i, i ^ groups) for i in range(total) if swapped(i) != i]
    blocks = (dp // 2, 2) if by_hops else (1, 1)
    partial_far = input_grad(pos, grads, ent, w_project, 1)
    far_core = between(partial_far, core_stay)
    partial_near = input_grad(pos, [*grads[:3], after(grads[3], partial_far)], ent, w_project, 0)
    if by_hops:
        far_core, partial_near = phase(far_core, partial_near)
        sent = [add(k[1], m[1]).astype(bf16) for k, m in zip(kept, moved)]
        kept = [add(k[0], m[0]).astype(bf16) for k, m in zip(kept, moved)]
    far_sum = add(partial_far, far_core)
    far_here, far_there = far_sum[0], far_sum[1].astype(bf16)
    if by_hops:
        far_here, far_there, sent, kept = phase(far_here, far_there, sent, kept)
    far_chip = between(far_there, move_chips)
    first_grads = project_grad(pos, [after(x[0], far_there), *x[1:]], grads[:2], ent)
    if by_hops:
        first_grads, far_chip = phase(first_grads, far_chip)
        moved = [over_dp(v, 2 * two) for v, (_, two) in zip(sent, order)]
    far_sum = add(far_here, far_chip, grad_resid_one).astype(bf16)
    near_core = between(partial_near, core_move)
    first_x, far_sum = phase(x[0], far_sum)
    far_moved = between(far_sum, swaps)
    project_grads, project_sums = project_grad(pos, [first_x, *x[1:]], grads[2:], ent, blocks, first_grads)
    sum_rows = project_sums[0].reshape(6, gwidth)
    sum_rows = jnp.concatenate([sum_rows[:4], sum_rows[5:]])
    sum_rows = lax.dynamic_update_slice_in_dim(jnp.zeros((5, width), f32), sum_rows, me * gwidth, 1)
    flat = jnp.concatenate(
        [sum_rows.reshape(5 * width), sums.reshape(6 * width), gib.reshape(groups * ffn)]
    ).reshape(-1, LANES)
    if by_hops:
        project_grads, flat, moved, near_core = phase(project_grads, flat, moved, near_core)
        kept, sent_z = [add(k, m).astype(bf16) for k, m in zip(kept, moved)]

        parts = [[project_grads[m, s] for m in range(4)] for s in range(2)]
        sent = [jnp.stack([p[one], p[3]]) for p, (one, _) in zip(parts, order)]
        near_sum = add(partial_near, near_core)
        near_here, near_there = near_sum[0], near_sum[1].astype(bf16)
        near_here, near_there, sent, sent_z = phase(near_here, near_there, sent, sent_z)
        far_moved, arrived_z, moved, hop = phase(
            far_moved, over_z(sent_z, 1), [over_dp(v, 2 * one) for v, (one, _) in zip(sent, order)], over_z(flat, 2)
        )
        flat = flat + hop
        project_kept = [add(p[0], m[0]).astype(bf16) for p, m in zip(parts, moved)]
        sent = [add(p[two], m[1]).astype(bf16) for p, m, (_, two) in zip(parts, moved, order)]
        near_chip, moved, hop = phase(
            between(near_there, stay_chips), [over_dp(v, 2 * two) for v, (_, two) in zip(sent, order)], over_z(flat, 1)
        )
        flat = flat + hop
        project_ends = jnp.stack([add(k, m).astype(bf16) for k, m in zip(project_kept, moved)])
        kept_z = add(kept, arrived_z)
        project_moved, hop, kept_z = phase(between(project_ends, swaps), over_dp(flat, 2), kept_z)
        flat = flat + hop
        project_ends = jnp.where(stays, project_ends, project_moved)
        project_kept = jnp.where(core == 0, project_ends[0], project_ends[1])
        sent = jnp.where(core == 0, project_ends[1], project_ends[0])
        query_grads, key_grads, value_grads = finish_project(project_kept, over_dp(sent, 1))
        inter_grads, output_grads, out_grads = finish_ffn(kept_z[0], over_z(kept_z[1].astype(bf16), 2), ffn)
        flat = flat + over_dp(flat, 4)
        flat = flat + over_dp(flat, 1)
    else:
        near_sum = add(partial_near, near_core)
        near_here = near_sum[0]
        near_chip = between(near_sum[1].astype(bf16), stay_chips)
        project_grads = relocate(project_grads.reshape(width, 6 * gwidth))
        project_grads = lax.psum_scatter(project_grads, "dp", scatter_dimension=0, tiled=True)
        query_grads, key_grads, value_grads = finish_project(project_grads, jnp.zeros_like(project_grads))
        inter_grads, output_grads, out_grads = finish_ffn(ffn_grads, jnp.zeros_like(ffn_grads), ffn)
        flat = lax.psum(flat, ("dp", "tensor"))
    near_sum = add(near_here, near_chip, grad_resid_one)
    grad_hidden = jnp.where(stays, near_sum, far_moved.astype(f32))
    flat = flat.reshape(-1)
    sum_rows = flat[: 5 * width].reshape(5, width)
    token_sums = flat[5 * width : 11 * width].reshape(6, width)
    return (
        layer_out,
        grad_hidden,
        query_grads,
        sum_rows[:4],
        key_grads,
        value_grads,
        sum_rows[4],
        out_grads,
        token_sums[0],
        token_sums[1],
        token_sums[2],
        inter_grads,
        flat[11 * width :],
        output_grads,
        token_sums[3],
        token_sums[4],
        token_sums[5],
    )


def solution(mesh):
    weights = P("dp", "tensor")
    tokens = P(("dp", "tensor"), None)
    return jax.shard_map(
        local,
        mesh=mesh,
        in_specs=(
            tokens, P("dp"), P("dp"), tokens, P(None, "dp", "tensor"), P(), weights, weights, P(),
            P("tensor", "dp"), P(), P(), P(), weights, P(), P("tensor", "dp"), P(), P(), P(),
        ),
        out_specs=(
            tokens, tokens, P(None, "dp", "tensor"), P(), weights, weights, P(), P("tensor", "dp"),
            P(), P(), P(), weights, P(), P("tensor", "dp"), P(), P(), P(),
        ),
        check_vma=False,
    )
```

```python
import functools

import jax
import jax.numpy as jnp
from jax import lax
from jax.experimental import pallas as pl
from jax.experimental.pallas import tpu as pltpu
from jax.sharding import PartitionSpec as P

HD = 64
BLOCK = 512
KEY_PARTS = 2
LANES = 128
EPS = 1e-05
MASKED = -1e30
SQRT_HALF = 0.7071067811865476
INV_SQRT_2PI = 0.3989422804014327
VMEM_LIMIT = 60000 * 1024

f32 = jnp.float32
bf16 = jnp.bfloat16


def dot_nn(a, b):
    return lax.dot_general(a, b, (((1,), (0,)), ((), ())), preferred_element_type=f32)


def dot_nt(a, b):
    return lax.dot_general(a, b, (((1,), (1,)), ((), ())), preferred_element_type=f32)


def params(**kw):
    return pltpu.CompilerParams(vmem_limit_bytes=VMEM_LIMIT, **kw)


def cost(flops, nbytes, transcendentals=0, short=1):
    return pl.CostEstimate(
        flops=7 * flops // (2 * short), bytes_accessed=nbytes // short, transcendentals=transcendentals
    )


def copies(jobs, sems):
    started = []
    for at, (source, target) in enumerate(jobs):
        copy = pltpu.make_async_copy(source, target, sems.at[at])
        copy.start()
        started.append(copy)
    return started


def block_rows(index, rows):
    return pl.ds(pl.multiple_of(index * rows, rows), rows)


def head_columns(heads):
    return [[HD * (part * heads + h) for part in range(6)] for h in range(heads)]


def by_heads(value, heads):
    cols = [value[:, at : at + HD] for parts in head_columns(heads) for at in parts]
    return jnp.concatenate(cols, 1)


def by_parts(value, heads):
    cols = [value[:, HD * (6 * h + part) : HD * (6 * h + part + 1)] for part in range(6) for h in range(heads)]
    return jnp.concatenate(cols, 1)


def project_weight_jobs(layout, pos_ref, refs, w_ref):
    jobs = []
    chip = pos_ref[2] // 2
    for masks, ref in zip(layout, refs):
        if masks is None:
            jobs.append((ref, w_ref))
            continue
        for u, (mask, second) in enumerate(masks):
            jobs.append((ref.at[u], w_ref.at[block_rows(2 * (chip ^ mask) + second, ref.shape[1])]))
    return jobs


def project_kernel(heads, layout, pos_ref, x0, x1, x2, x3, b_ref, ent_ref, *rest):
    count = len(layout)
    pieces = rest[:count]
    qc_ref, kc_ref, kv_ref, w_ref, x_ref, raw_ref, b_scr, sems = rest[count:]

    @pl.when(pl.program_id(0) == 0)
    def _():
        jobs = [(ref, x_ref.at[m]) for m, ref in enumerate((x0, x1, x2, x3))]
        for copy in copies(jobs + project_weight_jobs(layout, pos_ref, pieces, raw_ref), sems):
            copy.wait()
        w_ref[...] = by_heads(raw_ref[...], heads)
        b_scr[...] = by_heads(jnp.broadcast_to(b_ref[...], b_scr.shape), heads)

    x = x_ref[pl.program_id(0)]
    ent = ent_ref[...] > 0.5
    lane = lax.broadcasted_iota(jnp.int32, (x.shape[0], LANES), 1)
    low_half = lane < HD
    keep = jnp.logical_xor(low_half, ent)
    every = dot_nn(x, w_ref[...]) + b_scr[:1]
    for h in range(heads):
        y = every[:, 3 * LANES * h : 3 * LANES * (h + 1)]
        q = jnp.where(ent, y[:, LANES : 2 * LANES], y[:, :LANES])
        qc_ref[h] = q.astype(bf16) * (HD ** (-0.5))
        kv = y[:, 2 * LANES :].astype(bf16).astype(f32)
        kv_ref[h] = kv.astype(bf16)
        twice = jnp.where(low_half, kv, pltpu.roll(kv, HD, 1))
        kc_ref[h] = jnp.where(keep, twice, 0.0).astype(bf16)


def project(pos, x, pieces, layout, b, ent):
    own_rows, width = x[0].shape
    tokens = own_rows * len(x)
    columns = b.shape[1]
    heads = columns // (3 * LANES)
    out = jax.ShapeDtypeStruct((heads, tokens, LANES), bf16)
    spec = pl.BlockSpec((heads, own_rows, LANES), lambda m, pos: (0, m ^ pos[0], 0))
    anywhere = pl.BlockSpec(memory_space=pltpu.HBM)
    jobs = sum(1 if masks is None else len(masks) for masks in layout)
    return pl.pallas_call(
        functools.partial(project_kernel, heads, layout),
        grid_spec=pltpu.PrefetchScalarGridSpec(
            num_scalar_prefetch=1,
            grid=(len(x),),
            in_specs=[anywhere] * 4
            + [
                pl.BlockSpec((1, columns), lambda m, pos: (0, 0)),
                pl.BlockSpec((own_rows, LANES), lambda m, pos: (m ^ pos[0], 0)),
            ]
            + [anywhere] * len(pieces),
            out_specs=[spec, spec, spec, pl.BlockSpec((width, columns), lambda m, pos: (0, 0))],
            scratch_shapes=[
                pltpu.VMEM((len(x), own_rows, width), bf16),
                pltpu.VMEM((width, columns), bf16),
                pltpu.VMEM((8, columns), f32),
                pltpu.SemaphoreType.DMA((len(x) + jobs,)),
            ],
        ),
        out_shape=[out, out, out, jax.ShapeDtypeStruct((width, columns), bf16)],
        compiler_params=params(),
        cost_estimate=cost(2 * tokens * width * columns, 2 * tokens * (width + columns)),
        name="project",
    )(pos, *x, b, ent, *pieces)


def masked_keys(pos_ref, scores, first=0):
    keys = first + lax.broadcasted_iota(jnp.int32, (scores.shape[0], 1), 0)
    return scores + jnp.where(keys < pos_ref[4], 0.0, MASKED)


def attend_kernel(pos_ref, q_ref, kc_ref, kv_ref, *rest):
    out_ref, lse_ref, vt_ref = rest[-3:]

    @pl.when(pl.program_id(1) == 0)
    def _():
        vt_ref[...] = kv_ref[0].T[HD:]

    scores = masked_keys(pos_ref, dot_nt(kc_ref[0], q_ref[0]))
    top = jnp.max(scores, 0, keepdims=True)
    exponent = jnp.exp(scores - top)
    total = jnp.sum(exponent, 0, keepdims=True)
    mixed = dot_nn(vt_ref[...], exponent.astype(bf16))
    out_ref[0] = (mixed / total).astype(bf16)
    lse_ref[0] = top + jnp.log(total)


def attend(pos, first, count, qc, kc, kv, before=()):
    heads, tokens, _ = qc.shape
    blocks = tokens // BLOCK
    full = pl.BlockSpec((1, tokens, LANES), lambda h, i, pos: (first + h, 0, 0))
    return pl.pallas_call(
        attend_kernel,
        grid_spec=pltpu.PrefetchScalarGridSpec(
            num_scalar_prefetch=1,
            grid=(count, blocks),
            in_specs=[pl.BlockSpec((1, BLOCK, LANES), lambda h, i, pos: (first + h, i, 0)), full, full]
            + [pl.BlockSpec(memory_space=pltpu.HBM)] * len(before),
            out_specs=[
                pl.BlockSpec((1, HD, BLOCK), lambda h, i, pos: (i ^ pos[0], first + h, 0)),
                pl.BlockSpec((1, 1, BLOCK), lambda h, i, pos: (h, 0, i)),
            ],
            scratch_shapes=[pltpu.VMEM((HD, tokens), bf16)],
        ),
        out_shape=[
            jax.ShapeDtypeStruct((blocks, heads * HD, BLOCK), bf16),
            jax.ShapeDtypeStruct((count, 1, tokens), f32),
        ],
        input_output_aliases={4: 0} if before else {},
        compiler_params=params(),
        cost_estimate=cost(count * tokens * tokens * 2 * 3 * LANES, count * tokens * 8 * LANES),
        name="attend",
    )(pos, qc, kc, kv, *before)


def attend_back_kernel(
    pos_ref, q_ref, kc_ref, kv_ref, ent_ref, lse_ref, out_ref, go_ref,
    dq_ref, dkv_ref, kt_ref, dk_acc, dv_acc, go_pad,
):
    step = pl.program_id(1)

    @pl.when(step == 0)
    def _():
        kt_ref[...] = kc_ref[0].T
        go_pad[:HD] = jnp.zeros((HD, go_pad.shape[1]), bf16)
        dk_acc[...] = jnp.zeros_like(dk_acc)
        dv_acc[...] = jnp.zeros_like(dv_acc)

    go = go_ref[0]
    go_pad[HD:] = go
    delta = jnp.sum(go.astype(f32) * out_ref[0].astype(f32), 0, keepdims=True)
    q = q_ref[0]
    rows = kc_ref.shape[1] // KEY_PARTS

    def keys_part(part, dq):
        at = block_rows(part, rows)
        scores = masked_keys(pos_ref, dot_nt(kc_ref[0, at], q), part * rows)
        probs = jnp.exp(scores - lse_ref[0])
        grad_probs = dot_nn(kv_ref[0, at], go_pad[...])
        grad_scores = (probs * (grad_probs - delta)).astype(bf16)
        dv_acc[at] += dot_nt(probs.astype(bf16), go_pad[...])
        dk_acc[at] += dot_nn(grad_scores, q)
        return dq + dot_nn(kt_ref[:, at], grad_scores)

    dq = lax.fori_loop(0, KEY_PARTS, keys_part, jnp.zeros((LANES, q.shape[0]), f32))
    dq_ref[0] = (dq * (HD ** (-0.5))).T.astype(bf16)

    @pl.when(step == pl.num_programs(1) - 1)
    def _():
        lane = lax.broadcasted_iota(jnp.int32, dk_acc.shape, 1)
        dk = dk_acc[...]
        dk = jnp.where(ent_ref[...] > 0.5, pltpu.roll(dk, HD, 1), dk)
        dkv_ref[0] = jnp.where(lane < HD, dk, dv_acc[...]).astype(bf16)


def attend_back(pos, first, count, qc, kc, kv, ent, lse, mixed, grad_mixed):
    tokens = qc.shape[1]
    blocks = tokens // BLOCK
    full = pl.BlockSpec((1, tokens, LANES), lambda h, i, pos: (first + h, 0, 0))
    slot = pl.BlockSpec((1, HD, BLOCK), lambda h, i, pos: (i ^ pos[0], first + h, 0))
    out = jax.ShapeDtypeStruct((count, tokens, LANES), bf16)
    return pl.pallas_call(
        attend_back_kernel,
        grid_spec=pltpu.PrefetchScalarGridSpec(
            num_scalar_prefetch=1,
            grid=(count, blocks),
            in_specs=[
                pl.BlockSpec((1, BLOCK, LANES), lambda h, i, pos: (first + h, i, 0)),
                full, full,
                pl.BlockSpec((tokens, LANES), lambda h, i, pos: (0, 0)),
                pl.BlockSpec((1, 1, BLOCK), lambda h, i, pos: (h, 0, i)),
                slot, slot,
            ],
            out_specs=[
                pl.BlockSpec((1, BLOCK, LANES), lambda h, i, pos: (h, i, 0)),
                pl.BlockSpec((1, tokens, LANES), lambda h, i, pos: (h, 0, 0)),
            ],
            scratch_shapes=[
                pltpu.VMEM((LANES, tokens), bf16),
                pltpu.VMEM((tokens, LANES), f32),
                pltpu.VMEM((tokens, LANES), f32),
                pltpu.VMEM((LANES, BLOCK), bf16),
            ],
        ),
        out_shape=[out, out],
        compiler_params=params(),
        cost_estimate=cost(count * tokens * tokens * 2 * 5 * LANES, count * tokens * 16 * LANES),
        name="attend_back",
    )(pos, qc, kc, kv, ent, lse, mixed, grad_mixed)


def normed(residual, gain, shift):
    center = residual - jnp.mean(residual, -1, keepdims=True)
    inv = lax.rsqrt(jnp.mean(center * center, -1, keepdims=True) + EPS)
    unit = center * inv
    return unit, inv, unit * gain + shift


def norm_back(grad, unit, inv, gain):
    scaled = grad * gain
    return (
        scaled
        - jnp.mean(scaled, -1, keepdims=True)
        - unit * jnp.mean(scaled * unit, -1, keepdims=True)
    ) * inv


def token_weight_jobs(layout, pos_ref, refs, w_ref):
    jobs = []
    for masks, ref in zip(layout, refs):
        if masks is None:
            jobs.append((ref, w_ref))
            continue
        for u, (mask, group_mask) in enumerate(masks):
            where = block_rows(pos_ref[2] ^ mask, ref.shape[1])
            jobs.append((ref.at[u], w_ref.at[pos_ref[1] ^ group_mask, where]))
    return jobs


def token_kernel(
    layout, pos_ref, m0, m1, m2, m3, hid_ref, cot_ref, valid_ref, vec_ref, *rest
):
    count = len(layout)
    pieces = rest[:count]
    (
        y_ref, mixt_ref, nb_ref, act_ref, gi_ref, gf_ref, ga_ref, gm_ref, gr_ref, sums_ref, gib_ref,
        slope_ref, w_ref, sum_ref, unit_ref, inv_ref, sems,
    ) = rest[count:]
    me = pos_ref[0]
    groups, width, _ = w_ref.shape
    tokens = hid_ref.shape[0]
    ffn = act_ref.shape[2]
    gwidth = mixt_ref.shape[1]
    out_at = 2 * ffn
    jobs = token_weight_jobs(layout, pos_ref, pieces, w_ref)
    early = slice(out_at, out_at + gwidth)
    loads = copies([(s.at[..., early], t.at[..., early]) for s, t in jobs], sems.at[0])
    late = copies([(s.at[..., :out_at], t.at[..., :out_at]) for s, t in jobs], sems.at[1])
    for load in loads:
        load.wait()
    for m, ref in enumerate((m0, m1, m2, m3)):
        mixt_ref[me ^ m] = ref[0]

    def vector(at):
        value = vec_ref[at]
        return jnp.concatenate([value[i : i + 1] for i in range(value.shape[0])], 1)

    out_b, gain_one, shift_one, output_b, gain_two, shift_two = (vector(at) for at in range(6))
    few = min(LANES, tokens)
    sums_ref[...] = jnp.zeros_like(sums_ref)
    gib_ref[...] = jnp.zeros_like(gib_ref)

    def by_blocks(body):
        lax.fori_loop(0, tokens // few, lambda r, _: (body(block_rows(r, few)), 0)[1], 0)

    def total(at, value):
        sums_ref[at] += jnp.sum(value, 0, keepdims=True)

    def first_norm(at):
        attended = out_b
        for g in range(groups):
            part = dot_nt(mixt_ref[g, :, at].T, w_ref[g, :, early])
            attended = attended + part.astype(bf16).astype(f32)
        unit, inv, value = normed(hid_ref[at].astype(f32) + attended, gain_one, shift_one)
        unit_ref[at] = unit
        inv_ref[at] = jnp.broadcast_to(inv, (inv.shape[0], LANES))
        nb_ref[at] = value.astype(bf16)
        sum_ref[at] = jnp.broadcast_to(output_b, value.shape)

    first_norm(slice(0, tokens))
    for load in late:
        load.wait()
    halves = 2
    part_rows = tokens // halves

    def forward(step, _):
        g, at = step // halves, block_rows(step % halves, part_rows)
        pre = dot_nn(nb_ref[at], w_ref[g, :, :ffn]) + vector(6 + g)
        cdf = 0.5 * (1.0 + lax.erf(pre * SQRT_HALF))
        slope_ref[g, at] = cdf + pre * (jnp.exp(-0.5 * pre * pre) * INV_SQRT_2PI)
        active = (pre * cdf).astype(bf16)
        act_ref[g, at] = active
        part = dot_nt(active, w_ref[g, :, ffn:out_at])
        sum_ref[at] += part.astype(bf16).astype(f32)
        return 0

    lax.fori_loop(0, groups * halves, forward, 0)

    def second_norm(at):
        valid = valid_ref[at, :1]
        normed_one = unit_ref[at] * gain_one + shift_one
        unit, inv, value = normed(normed_one + sum_ref[at], gain_two, shift_two)
        y_ref[at] = (value * valid).astype(bf16)
        grad_top = cot_ref[at].astype(f32) * valid
        grad = norm_back(grad_top, unit, inv, gain_two)
        grad_ffn = grad.astype(bf16)
        gf_ref[at] = grad_ffn
        sum_ref[at] = grad
        total(3, grad_ffn.astype(f32))
        total(4, grad_top * unit)
        total(5, grad_top)

    by_blocks(second_norm)

    def backward(step, _):
        g, at = step // halves, block_rows(step % halves, part_rows)
        grad_active = dot_nn(gf_ref[at], w_ref[g, :, ffn:out_at])
        grad_inner = (slope_ref[g, at] * grad_active).astype(bf16)
        gi_ref[g, at] = grad_inner
        gib_ref[g] += jnp.sum(grad_inner.astype(f32), 0, keepdims=True)
        part = dot_nt(grad_inner, w_ref[g, :, :ffn])
        sum_ref[at] += part.astype(bf16).astype(f32)
        return 0

    lax.fori_loop(0, groups * halves, backward, 0)

    def first_norm_back(at):
        grad_normed = sum_ref[at]
        unit = unit_ref[at]
        grad = norm_back(grad_normed, unit, inv_ref[at, :1], gain_one)
        gr_ref[at] = grad
        grad_att = grad.astype(bf16)
        ga_ref[at] = grad_att
        total(0, grad_att.astype(f32))
        total(1, grad_normed * unit)
        total(2, grad_normed)

    by_blocks(first_norm_back)

    def mixed_back(m, _):
        out_rows = w_ref[me ^ m, :, early].T
        gm_ref[m] = dot_nt(out_rows, ga_ref[...]).astype(bf16)
        return 0

    for m in range(groups):
        mixed_back(m, 0)


def per_token(
    pos, mixed, hidden, cot, valid, vectors, pieces, layout, groups, columns
):
    tokens, width = hidden.shape
    ffn = vectors.shape[1] * vectors.shape[2]
    gwidth = mixed[0].shape[1]
    vmem = pl.BlockSpec(memory_space=pltpu.VMEM)
    shape = jax.ShapeDtypeStruct
    jobs = sum(1 if masks is None else len(masks) for masks in layout)
    return pl.pallas_call(
        functools.partial(token_kernel, layout),
        in_specs=[pl.BlockSpec(memory_space=pltpu.SMEM)]
        + [vmem] * 8
        + [pl.BlockSpec(memory_space=pltpu.HBM)] * len(pieces),
        out_specs=[vmem] * 11,
        out_shape=[
            shape((tokens, width), bf16),
            shape((groups, gwidth, tokens), bf16),
            shape((tokens, width), bf16),
            shape((groups, tokens, ffn), bf16),
            shape((groups, tokens, ffn), bf16),
            shape((tokens, width), bf16),
            shape((tokens, width), bf16),
            shape((groups, gwidth, tokens), bf16),
            shape((tokens, width), f32),
            shape((6, 1, width), f32),
            shape((groups, 1, ffn), f32),
        ],
        scratch_shapes=[
            pltpu.VMEM((groups, tokens, ffn), f32),
            pltpu.VMEM((groups, width, columns), bf16),
            pltpu.VMEM((tokens, width), f32),
            pltpu.VMEM((tokens, width), f32),
            pltpu.VMEM((tokens, LANES), f32),
            pltpu.SemaphoreType.DMA((2, jobs)),
        ],
        compiler_params=params(),
        cost_estimate=cost(
            8 * tokens * width * ffn * groups + 4 * tokens * width * width,
            2 * groups * width * columns + 4 * tokens * ffn * groups,
            2 * tokens * ffn * groups,
        ),
        name="per_token",
    )(pos, *mixed, hidden, cot, valid, vectors, *pieces)


def weight_grad_kernel(
    pos_ref, nb_ref, gf_ref, ga_ref, act_ref, gi_ref, mixt_ref, near_ref, far_ref, nbt, gft, gat, turn
):
    ffn = act_ref.shape[2]
    gwidth = mixt_ref.shape[1]
    chips, _, rows, _ = near_ref.shape

    @pl.when(pl.program_id(0) == 0)
    def _():
        for target, source in ((nbt, nb_ref), (gft, gf_ref), (gat, ga_ref)):
            turn[...] = source[...].T
            for mine in range(2):
                for mask in range(chips):
                    block = pos_ref[2] ^ (2 * mask + mine)
                    at = (mine * chips + mask) * rows
                    target[at : at + rows] = turn[block_rows(block, rows)]

    second_half = (pl.program_id(0) ^ pos_ref[1]) % 2

    def put(value, start, stop):
        for mine, out_ref in enumerate((near_ref, far_ref)):
            for mask in range(chips):
                slot = mask + second_half - 1 if mask == 2 else mask + 1 - second_half if mask == 1 else mask
                at = (mine * chips + mask) * rows
                out_ref[slot, 0, :, start:stop] = value[at : at + rows].astype(bf16)

    put(dot_nn(nbt[...], gi_ref[0]), 0, ffn)
    put(dot_nn(gft[...], act_ref[0]), ffn, 2 * ffn)
    put(dot_nt(gat[...], mixt_ref[0]), 2 * ffn, 2 * ffn + gwidth)


def weight_grads(pos, nb, gf, ga, act, gi, mixt, dp):
    groups, tokens, ffn = act.shape
    width = nb.shape[1]
    gwidth = mixt.shape[1]
    rows = width // dp
    whole = pl.BlockSpec((tokens, width), lambda g, pos: (0, 0))
    group = pl.BlockSpec((1, tokens, ffn), lambda g, pos: (g, 0, 0))
    columns = 2 * ffn + gwidth
    out = jax.ShapeDtypeStruct((dp // 2, groups, rows, columns), bf16)

    def slot(g, pos):
        mask = g ^ pos[1]
        return (0, 2 * (mask % 2) + mask // 2, 0, 0)

    spec = pl.BlockSpec((dp // 2, 1, rows, columns), slot)
    return pl.pallas_call(
        weight_grad_kernel,
        grid_spec=pltpu.PrefetchScalarGridSpec(
            num_scalar_prefetch=1,
            grid=(groups,),
            in_specs=[
                whole, whole, whole, group, group,
                pl.BlockSpec((1, gwidth, tokens), lambda g, pos: (g, 0, 0)),
            ],
            out_specs=[spec, spec],
            scratch_shapes=[pltpu.VMEM((width, tokens), bf16)] * 4,
        ),
        out_shape=[out, out],
        compiler_params=params(),
        cost_estimate=cost(2 * tokens * width * columns * groups, 2 * groups * width * columns),
        name="weight_grads",
    )(pos, nb, gf, ga, act, gi, mixt)


def weight_grad_whole_kernel(nb_ref, gf_ref, ga_ref, act_ref, gi_ref, mixt_ref, out_ref, nbt, gft, gat):
    ffn = act_ref.shape[2]
    gwidth = mixt_ref.shape[1]

    @pl.when(pl.program_id(0) == 0)
    def _():
        nbt[...] = nb_ref[...].T
        gft[...] = gf_ref[...].T
        gat[...] = ga_ref[...].T

    out_ref[0, :, :ffn] = dot_nn(nbt[...], gi_ref[0]).astype(bf16)
    out_ref[0, :, ffn : 2 * ffn] = dot_nn(gft[...], act_ref[0]).astype(bf16)
    out_ref[0, :, 2 * ffn : 2 * ffn + gwidth] = dot_nt(gat[...], mixt_ref[0]).astype(bf16)


def weight_grads_whole(nb, gf, ga, act, gi, mixt):
    groups, tokens, ffn = act.shape
    width = nb.shape[1]
    gwidth = mixt.shape[1]
    whole = pl.BlockSpec((tokens, width), lambda g: (0, 0))
    group = pl.BlockSpec((1, tokens, ffn), lambda g: (g, 0, 0))
    columns = 2 * ffn + gwidth
    return pl.pallas_call(
        weight_grad_whole_kernel,
        grid=(groups,),
        in_specs=[whole, whole, whole, group, group, pl.BlockSpec((1, gwidth, tokens), lambda g: (g, 0, 0))],
        out_specs=pl.BlockSpec((1, width, columns), lambda g: (g, 0, 0)),
        out_shape=jax.ShapeDtypeStruct((groups, width, columns), bf16),
        scratch_shapes=[pltpu.VMEM((width, tokens), bf16)] * 3,
        compiler_params=params(),
        cost_estimate=cost(2 * tokens * width * columns * groups, 2 * groups * width * columns),
        name="weight_grads_whole",
    )(nb, gf, ga, act, gi, mixt)


def split_columns(pairs, ent):
    h = 0
    for dq_ref, dkv_ref in pairs:
        for u in range(dq_ref.shape[0]):
            dq = dq_ref[u]
            nothing = jnp.zeros_like(dq)
            yield 3 * h, jnp.where(ent, nothing, dq)
            yield 3 * h + 1, jnp.where(ent, dq, nothing)
            yield 3 * h + 2, dkv_ref[u]
            h += 1


def input_grad_kernel(count, pos_ref, *refs):
    grads, (ent_ref, w_ref, out_ref) = refs[:count], refs[count:]
    ent = ent_ref[...] > 0.5
    cols = [c for _, c in split_columns(list(zip(grads[::2], grads[1::2])), ent)]
    out_ref[0] = dot_nt(jnp.concatenate(cols, 1), w_ref[...]).astype(bf16)


def input_grad(pos, grads, ent, w, far):
    tokens = grads[0].shape[1]
    width, columns = w.shape

    def block(i, pos):
        return i + 2 * (pos[3] ^ far)

    stacked = [pl.BlockSpec((g.shape[0], BLOCK, LANES), lambda i, pos: (0, block(i, pos), 0)) for g in grads]
    return pl.pallas_call(
        functools.partial(input_grad_kernel, len(grads)),
        grid_spec=pltpu.PrefetchScalarGridSpec(
            num_scalar_prefetch=1,
            grid=(2,),
            in_specs=stacked
            + [
                pl.BlockSpec((BLOCK, LANES), lambda i, pos: (block(i, pos), 0)),
                pl.BlockSpec((width, columns), lambda i, pos: (0, 0)),
            ],
            out_specs=pl.BlockSpec((1, BLOCK, width), lambda i, pos: (i ^ (pos[0] % 2), 0, 0)),
        ),
        out_shape=jax.ShapeDtypeStruct((2, BLOCK, width), bf16),
        compiler_params=params(),
        cost_estimate=cost(tokens * width * columns, tokens * (columns + width), short=100),
        name="input_grad",
    )(pos, *grads, ent, w)


def all_sums(pos_ref, bias, sums_ref, gib_ref, out_ref):
    gwidth = bias.shape[1] // 6
    zeros = jnp.zeros((1, gwidth), f32)
    for row, part in enumerate((0, 1, 2, 3, 5)):
        own = bias[:1, gwidth * part : gwidth * (part + 1)]
        out_ref[row : row + 1] = jnp.concatenate(
            [jnp.where(pos_ref[0] == j, own, zeros) for j in range(out_ref.shape[1] // gwidth)], 1
        )
    rest = [sums_ref[i] for i in range(sums_ref.shape[0])] + [gib_ref[i] for i in range(gib_ref.shape[0])]
    for row, value in enumerate(rest):
        out_ref[5 + row : 6 + row] = value
    out_ref[5 + len(rest) :] = jnp.zeros((out_ref.shape[0] - 5 - len(rest), out_ref.shape[1]), f32)


def project_grad_kernel(pos_ref, x0, x1, x2, x3, *refs):
    (
        *grads, ent_ref, sums_ref, gib_ref, keep_ref, first_ref, second_ref, bias_ref, acc_ref, bias_acc,
        x_ref, sems,
    ) = refs
    step = pl.program_id(0)

    @pl.when(step == 0)
    def _():
        loads = copies([(ref, x_ref.at[m]) for m, ref in enumerate((x0, x1, x2, x3))], sems)
        acc_ref[...] = jnp.zeros_like(acc_ref)
        bias_acc[...] = jnp.zeros_like(bias_acc)
        for load in loads:
            load.wait()

    ent = ent_ref[...] > 0.5
    columns = jnp.concatenate([c for _, c in split_columns(list(zip(grads[::2], grads[1::2])), ent)], 1)
    acc_ref[...] += dot_nn(x_ref[step].T, columns)
    bias_acc[:1] += jnp.sum(columns.astype(f32), 0, keepdims=True)

    @pl.when(step == pl.num_programs(0) - 1)
    def _():
        chips, cores, rows, columns = keep_ref.shape
        heads = columns // (3 * LANES)
        all_sums(pos_ref, by_parts(bias_acc[...], heads), sums_ref, gib_ref, bias_ref)
        targets = [
            [keep_ref.at[0, 0], first_ref.at[0], keep_ref.at[1, 0], first_ref.at[1]],
            [keep_ref.at[0, 1], keep_ref.at[1, 1], second_ref.at[0], second_ref.at[1]],
        ]
        for mask in range(4):
            for core in range(2):
                at = block_rows(2 * ((pos_ref[2] // 2) ^ mask) + core, rows)
                targets[core][mask][...] = by_parts(acc_ref[at].astype(bf16), heads)


def project_grad_whole_kernel(*refs):
    *ins, out_ref, bias_ref, acc_ref, bias_acc, x_ref, sems = refs
    heads = out_ref.shape[1] // (3 * LANES)
    pos_ref, x0, x1, x2, x3, *grads, ent_ref, sums_ref, gib_ref = ins
    step = pl.program_id(0)

    @pl.when(step == 0)
    def _():
        loads = copies([(ref, x_ref.at[m]) for m, ref in enumerate((x0, x1, x2, x3))], sems)
        acc_ref[...] = jnp.zeros_like(acc_ref)
        bias_acc[...] = jnp.zeros_like(bias_acc)
        for load in loads:
            load.wait()

    ent = ent_ref[...] > 0.5
    columns = jnp.concatenate([c for _, c in split_columns(list(zip(grads[::2], grads[1::2])), ent)], 1)
    acc_ref[...] += dot_nn(x_ref[step].T, columns)
    bias_acc[:1] += jnp.sum(columns.astype(f32), 0, keepdims=True)

    @pl.when(step == pl.num_programs(0) - 1)
    def _():
        out_ref[...] = by_parts(acc_ref[...].astype(bf16), heads)
        all_sums(pos_ref, by_parts(bias_acc[...], heads), sums_ref, gib_ref, bias_ref)


def project_grad(pos, x, grads, ent, sums, gib, by_hops):
    heads = sum(g.shape[0] for g in grads) // 2
    tokens = grads[0].shape[1]
    own_rows, width = x[0].shape
    columns = 3 * LANES * heads
    rows = width // 8
    shapes = [(2, 2, rows, columns)] + [(2, rows, columns)] * 2 if by_hops else [(width, columns)]
    stacked = [pl.BlockSpec((g.shape[0], own_rows, LANES), lambda m, pos: (0, m ^ pos[0], 0)) for g in grads]

    def fixed(shape):
        return pl.BlockSpec(shape, lambda m, pos: (0,) * len(shape))

    return pl.pallas_call(
        project_grad_kernel if by_hops else project_grad_whole_kernel,
        grid_spec=pltpu.PrefetchScalarGridSpec(
            num_scalar_prefetch=1,
            grid=(len(x),),
            in_specs=[pl.BlockSpec(memory_space=pltpu.HBM)] * 4
            + stacked
            + [pl.BlockSpec((own_rows, LANES), lambda m, pos: (m ^ pos[0], 0))]
            + [fixed(sums.shape), fixed(gib.shape)],
            out_specs=[fixed(shape) for shape in shapes] + [fixed((16, width))],
            scratch_shapes=[
                pltpu.VMEM((width, columns), f32),
                pltpu.VMEM((8, columns), f32),
                pltpu.VMEM((len(x), own_rows, width), bf16),
                pltpu.SemaphoreType.DMA((len(x),)),
            ],
        ),
        out_shape=[jax.ShapeDtypeStruct(shape, bf16) for shape in shapes]
        + [jax.ShapeDtypeStruct((16, width), f32)],
        compiler_params=params(),
        cost_estimate=cost(2 * tokens * width * columns, 2 * tokens * (columns + width)),
        name="project_grad",
    )(pos, *x, *grads, ent, sums, gib)


def finish_project_kernel(kept_ref, arrived_ref, q_ref, k_ref, v_ref):
    total = kept_ref[...].astype(f32) + arrived_ref[...].astype(f32)
    width = k_ref.shape[1]
    for a in range(q_ref.shape[0]):
        q_ref[a] = total[:, width * a : width * (a + 1)]
    k_ref[...] = total[:, 4 * width : 5 * width]
    v_ref[...] = total[:, 5 * width :]


def finish_project(kept, arrived):
    rows, columns = kept.shape
    part = jax.ShapeDtypeStruct((rows, columns // 6), f32)
    return pl.pallas_call(
        finish_project_kernel,
        out_shape=[jax.ShapeDtypeStruct((4, rows, columns // 6), f32), part, part],
        compiler_params=params(),
        cost_estimate=cost(rows * columns, 8 * rows * columns),
        name="finish_project",
    )(kept, arrived)


def finish_ffn_kernel(kept_ref, arrived_ref, inter_ref, output_ref, out_ref):
    total = kept_ref[...].astype(f32) + arrived_ref[...].astype(f32)
    ffn = inter_ref.shape[1]
    inter_ref[...] = total[:, :ffn]
    output_ref[...] = total[:, ffn : 2 * ffn].T
    out_ref[...] = total[:, 2 * ffn :].T


def finish_ffn(kept, arrived, ffn):
    rows, columns = kept.shape
    shape = jax.ShapeDtypeStruct
    return pl.pallas_call(
        finish_ffn_kernel,
        out_shape=[shape((rows, ffn), f32), shape((ffn, rows), f32), shape((columns - 2 * ffn, rows), f32)],
        compiler_params=params(),
        cost_estimate=cost(rows * columns, 8 * rows * columns),
        name="finish_ffn",
    )(kept, arrived)


def local(
    hidden_in, token_types, lengths, cotangent, query_w, query_b, key_w, value_w, value_b, out_w,
    out_b, gain_one, shift_one, inter_w, inter_b, output_w, output_b, gain_two, shift_two,
):
    groups = lax.axis_size("tensor")
    dp = lax.axis_size("dp")
    z = lax.axis_index("tensor")
    d = lax.axis_index("dp")
    half = groups // 2
    core = d % 2
    upper = z // half
    me = z % half + half * core
    own_rows, width = hidden_in.shape
    length = own_rows * groups
    gwidth = query_w.shape[2]
    heads = gwidth // HD
    ffn = inter_w.shape[1]
    rows = key_w.shape[0]
    columns = 2 * ffn + gwidth
    total = dp * groups
    by_hops = dp == 8 and rows % 16 == 0

    def device(dd, zz):
        return dd * groups + zz

    def swapped(dev):
        dd, zz = dev // groups, dev % groups
        return device(dd - dd % 2 + zz // half, zz % half + half * (dd % 2))

    def member(dev, mask):
        dd, zz = dev // groups, dev % groups
        j = (zz % half + half * (dd % 2)) ^ mask
        return device(dd - dd % 2 + j // half, zz - zz % half + j % half)

    stays = core == upper

    def relocate(value):
        moves = [(i, swapped(i)) for i in range(total) if swapped(i) != i]
        return jnp.where(stays, value, lax.ppermute(value, ("dp", "tensor"), moves))

    def to_member(value, mask):
        return lax.ppermute(value, ("dp", "tensor"), [(i, member(i, mask)) for i in range(total)])

    def over_dp(value, mask):
        return lax.ppermute(value, "dp", [(i, i ^ mask) for i in range(dp)])

    def over_z(value, mask):
        return lax.ppermute(value, "tensor", [(i, i ^ mask) for i in range(groups)])

    def add(*terms):
        return functools.reduce(jnp.add, [t.astype(f32) for t in terms])

    def after(value, *others):
        return lax.optimization_barrier((value, *others))[0]

    own_project = jnp.concatenate([*query_w, key_w, value_w], 1)
    own_ffn = jnp.concatenate([inter_w, output_w.T, out_w.T], 1)

    def between(value, pairs):
        return lax.ppermute(value, ("dp", "tensor"), [p for p in pairs if p[0] != p[1]])

    swaps = [(i, swapped(i)) for i in range(total)]
    on_chips = [(i, member(i, 1)) for i in range(total)]
    stay_chips = [p for p in on_chips if swapped(p[0]) == p[0]]
    move_chips = [p for p in on_chips if swapped(p[0]) != p[0]]

    def phase(*values):
        return lax.optimization_barrier(values)

    facts = jnp.concatenate([token_types, lengths])
    facts_moved = over_dp(facts, 1)
    query_b_own = lax.dynamic_slice_in_dim(query_b, me * gwidth, gwidth, 1)
    value_b_own = lax.dynamic_slice_in_dim(value_b, me * gwidth, gwidth)
    b_project = jnp.concatenate([query_b_own.reshape(-1), jnp.zeros((gwidth,), bf16), value_b_own])
    b_project = b_project.reshape(1, 6 * gwidth).astype(f32)
    vectors = jnp.concatenate(
        [
            v.astype(f32).reshape(-1, width // LANES, LANES)
            for v in (out_b, gain_one, shift_one, output_b, gain_two, shift_two, inter_b)
        ]
    )
    to_move = hidden_in
    if by_hops:
        other = over_dp(own_project, 1)
        to_move = after(hidden_in, other)
    near_chip = between(to_move, stay_chips)
    moved = between(to_move, swaps)
    if by_hops:
        pair = jnp.where(core == 0, jnp.stack([own_project, other]), jnp.stack([other, own_project]))
        pair = relocate(pair)
        a, b = pair[0], pair[1]
        own_ffn = after(own_ffn, other)
        own_z = over_z(own_ffn, 1)
        pair_x, pair_y = over_dp(pair, 2), over_dp(pair, 4)
    facts = jnp.where(stays, facts, facts_moved)
    pos = jnp.concatenate([jnp.stack([me, z, d, upper]).astype(jnp.int32), facts[length:]])
    ent = jnp.broadcast_to(facts[:length, None].astype(bf16), (length, LANES))
    valid_own = me * own_rows + jnp.arange(own_rows, dtype=jnp.int32) < facts[length]
    valid_own = jnp.broadcast_to(valid_own[:, None].astype(f32), (own_rows, LANES))
    if by_hops:
        moved, near_chip, pair_x, pair_y, own_z, own_ffn, b_project, vectors, pos, ent, valid_own = phase(
            moved, near_chip, pair_x, pair_y, own_z, own_ffn, b_project, vectors, pos, ent, valid_own
        )
    hidden = jnp.where(stays, hidden_in, moved)
    from_chip = between(hidden, move_chips)
    if by_hops:
        from_chip, a_xy, b_xy, own_x, own_y = phase(
            from_chip, over_dp(pair_x[0], 4), over_dp(pair_y[1], 2), over_dp(own_ffn, 2), over_dp(own_ffn, 4)
        )
        from_chip = jnp.where(stays, near_chip, from_chip)
        x_2, x_3, own_ffn, own_x, own_z = phase(
            to_member(hidden, half), to_member(from_chip, half), own_ffn, own_x, own_z
        )
        both = ((0, 0), (0, 1))
        project_pieces = [pair, pair_x, pair_y, a_xy[None], b_xy[None]]
        project_layout = (both, tuple((1, c) for _, c in both), tuple((2, c) for _, c in both), ((3, 0),), ((3, 1),))
    else:
        project_pieces = [relocate(lax.all_gather(own_project, "dp", axis=0, tiled=True))]
        project_layout = (None,)
        from_chip = jnp.where(stays, near_chip, from_chip)
        x_2, x_3 = to_member(hidden, half), to_member(from_chip, half)
    x = [hidden, from_chip, x_2, x_3]

    qc, kc, kv, w_project = project(pos, x, project_pieces, project_layout, b_project, ent)
    if by_hops:
        token_pieces, token_layout = [], []

        def pieces(group_mask, **by):
            masks = [({"own": 0, "x": 2, "y": 4, "xy": 6}[axes], group_mask) for axes in by]
            token_layout.extend([tuple(masks), tuple((m + 1, g) for m, g in masks)])
            return jnp.stack(list(by.values()))

        qc, far, own_zx, own_zy, own_xy = phase(
            qc, over_z(own_ffn, 2), over_dp(own_z, 2), over_dp(own_z, 4), over_dp(own_x, 4)
        )
        quad = pieces(0, own=own_ffn, x=own_x, y=own_y, xy=own_xy)
        mixed, lse_0 = attend(pos, 0, 1, qc, kc, kv)
        mixed, far_z, far_x, far_y, quad_core = phase(
            mixed, over_z(far, 1), over_dp(far, 2), over_dp(far, 4), over_dp(quad, 1)
        )
        token_pieces += [quad, quad_core]
        mixed, lse_1 = attend(pos, 1, heads - 1, qc, kc, kv, (mixed,))
        mixed, far_zx, far_zy, far_xy, own_zxy, cot = phase(
            mixed, over_dp(far_z, 2), over_dp(far_z, 4), over_dp(far_x, 4), over_dp(own_zy, 2),
            between(after(cotangent, far_x), swaps),
        )
        cot = jnp.where(stays, cotangent, cot)
        quad = pieces(1, own=own_z, x=own_zx, y=own_zy, xy=own_zxy)
        mixed_own, far_zxy, quad_core, cot = phase(
            [mixed[:1]] + [to_member(mixed[m : m + 1], m) for m in range(1, groups)], over_dp(far_zy, 2),
            over_dp(quad, 1), cot
        )
        token_pieces += [quad, quad_core]
        for quad in (
            pieces(2, own=far, x=far_x, y=far_y, xy=far_xy),
            pieces(3, own=far_z, x=far_zx, y=far_zy, xy=far_zxy),
        ):
            token_pieces += [quad, over_dp(quad, 1)]
        token_layout = tuple(token_layout)
    else:
        token_pieces = [lax.all_gather(lax.all_gather(own_ffn, "tensor"), "dp", axis=1, tiled=True)]
        token_layout = (None,)
        mixed, lse_0 = attend(pos, 0, 1, qc, kc, kv)
        mixed, lse_1 = attend(pos, 1, heads - 1, qc, kc, kv, (mixed,))
        mixed_own = [mixed[:1]] + [to_member(mixed[m : m + 1], m) for m in range(1, groups)]
        cot = jnp.where(stays, cotangent, between(cotangent, swaps))
    y, mixt, nb, act, gi, gf, ga, gm, grad_resid_one, sums, gib = per_token(
        pos, mixed_own, hidden, cot, valid_own, vectors, token_pieces, token_layout, groups, columns
    )
    grad_mixed = jnp.concatenate([gm[:1]] + [to_member(gm[m : m + 1], m) for m in range(1, groups)])

    order = ((1, 2), (2, 1))
    if by_hops:
        near, far = weight_grads(pos, nb, gf, ga, act, gi, mixt, dp)
        arrived = over_dp(after(far, grad_mixed), 1)
        grads = attend_back(pos, 0, 1, qc, kc, kv, ent, lse_0, mixed, grad_mixed)
        groups_at = (slice(0, 2), slice(2, 4))
        kept = [add(near[:2, g], arrived[:2, g]).astype(bf16) for g in groups_at]
        sent = [add(near[2:, g], arrived[2:, g]).astype(bf16) for g in groups_at]
        grads, kept, sent, qc, y = phase(grads, kept, sent, qc, y)
        more = attend_back(pos, 1, heads - 1, qc, kc, kv, ent, lse_1, mixed, grad_mixed)
        more, moved, layer_moved = phase(
            more, [over_dp(v, 2 * one) for v, (one, _) in zip(sent, order)], between(y, swaps)
        )
    else:
        ffn_grads = weight_grads_whole(nb, gf, ga, act, gi, mixt)
        ffn_grads = lax.psum_scatter(ffn_grads, "tensor", scatter_dimension=0, tiled=False)
        ffn_grads = lax.psum_scatter(ffn_grads, "dp", scatter_dimension=0, tiled=True)
        grads = attend_back(pos, 0, 1, qc, kc, kv, ent, lse_0, mixed, grad_mixed)
        more = attend_back(pos, 1, heads - 1, qc, kc, kv, ent, lse_1, mixed, grad_mixed)
        layer_moved = between(y, swaps)
    layer_out = jnp.where(stays, y, layer_moved)
    grads = [*grads, *more]

    core_stay = [(i, i ^ groups) for i in range(total) if swapped(i) == i]
    core_move = [(i, i ^ groups) for i in range(total) if swapped(i) != i]
    if by_hops:
        sent = [add(k[1], m[1]).astype(bf16) for k, m in zip(kept, moved)]
        kept = [add(k[0], m[0]).astype(bf16) for k, m in zip(kept, moved)]
        first_x, sent, kept = phase(x[0], sent, kept)
        moved = [over_dp(v, 2 * two) for v, (_, two) in zip(sent, order)]
        project_kept, *project_sent, flat = project_grad(pos, [first_x, *x[1:]], grads, ent, sums, gib, True)
        project_kept, project_sent, flat, moved = phase(project_kept, project_sent, flat, moved)
        kept, sent_z = [add(k, m).astype(bf16) for k, m in zip(kept, moved)]
        kept, sent_z, first, project_sent = phase(kept, sent_z, grads[0], project_sent)
    else:
        project_grads, flat = project_grad(pos, x, grads, ent, sums, gib, False)
        first = grads[0]
    partial_far = input_grad(pos, [first, *grads[1:]], ent, w_project, 1)
    far_core = between(partial_far, core_stay)
    if by_hops:
        arrived = [over_dp(v, 2 * one) for v, (one, _) in zip(project_sent, order)]
        arrived_z = over_z(sent_z, 1)
        far_sum = add(partial_far, far_core)
        far_here, far_there, flat, second = phase(far_sum[0], far_sum[1].astype(bf16), flat, grads[3])
    else:
        far_sum = add(partial_far, far_core)
        far_here, far_there, second = far_sum[0], far_sum[1].astype(bf16), grads[3]
    far_chip = between(far_there, move_chips)
    partial_near = input_grad(pos, [*grads[:3], second], ent, w_project, 0)
    if by_hops:
        partial_near, arrived, arrived_z, hop = phase(partial_near, arrived, arrived_z, over_z(flat, 2))
        flat = flat + hop
        sent = [add(project_kept[1, s], m[1]).astype(bf16) for s, m in enumerate(arrived)]
        project_kept = [add(project_kept[0, s], m[0]).astype(bf16) for s, m in enumerate(arrived)]
        kept_z = add(kept, arrived_z)
        kept_z, last = kept_z[0], kept_z[1].astype(bf16)
        sent, last, flat, partial_near = phase(sent, last, flat, partial_near)
        far_chip, moved, last, near_core = phase(
            far_chip, [over_dp(v, 2 * two) for v, (_, two) in zip(sent, order)], over_z(last, 2),
            between(partial_near, core_move),
        )
        near_sum = add(partial_near, near_core)
        near_here, near_there = near_sum[0], near_sum[1].astype(bf16)
        far_sum = add(far_here, far_chip, grad_resid_one).astype(bf16)
        project_ends = jnp.stack([add(k, m).astype(bf16) for k, m in zip(project_kept, moved)])
        far_sum, project_ends, near_here, near_there, flat = phase(
            far_sum, project_ends, near_here, near_there, flat
        )
        project_moved, far_moved, near_chip, hop = phase(
            between(project_ends, swaps), between(far_sum, swaps), between(near_there, stay_chips),
            over_z(flat, 1),
        )
        flat = flat + hop
        flat = flat + over_dp(flat, 2)
        flat = flat + over_dp(flat, 4)
        flat = flat + over_dp(flat, 1)
        project_ends = jnp.where(stays, project_ends, project_moved)
        project_kept = jnp.where(core == 0, project_ends[0], project_ends[1])
        sent = jnp.where(core == 0, project_ends[1], project_ends[0])
        query_grads, key_grads, value_grads = finish_project(project_kept, over_dp(sent, 1))
        inter_grads, output_grads, out_grads = finish_ffn(kept_z, last, ffn)
    else:
        far_moved = between(add(far_here, far_chip, grad_resid_one).astype(bf16), swaps)
        near_sum = add(partial_near, between(partial_near, core_move))
        near_here = near_sum[0]
        near_chip = between(near_sum[1].astype(bf16), stay_chips)
        project_grads = relocate(project_grads)
        project_grads = lax.psum_scatter(project_grads, "dp", scatter_dimension=0, tiled=True)
        query_grads, key_grads, value_grads = finish_project(project_grads, jnp.zeros_like(project_grads))
        inter_grads, output_grads, out_grads = finish_ffn(ffn_grads, jnp.zeros_like(ffn_grads), ffn)
        flat = lax.psum(flat, ("dp", "tensor"))
    near_sum = add(near_here, near_chip, grad_resid_one)
    grad_hidden = jnp.where(stays, near_sum, far_moved.astype(f32))
    return (
        layer_out,
        grad_hidden,
        query_grads,
        flat[:4],
        key_grads,
        value_grads,
        flat[4],
        out_grads,
        flat[5],
        flat[6],
        flat[7],
        inter_grads,
        flat[11 : 11 + groups].reshape(groups * ffn),
        output_grads,
        flat[8],
        flat[9],
        flat[10],
    )


def solution(mesh):
    weights = P("dp", "tensor")
    tokens = P(("dp", "tensor"), None)
    return jax.shard_map(
        local,
        mesh=mesh,
        in_specs=(
            tokens, P("dp"), P("dp"), tokens, P(None, "dp", "tensor"), P(), weights, weights, P(),
            P("tensor", "dp"), P(), P(), P(), weights, P(), P("tensor", "dp"), P(), P(), P(),
        ),
        out_specs=(
            tokens, tokens, P(None, "dp", "tensor"), P(), weights, weights, P(), P("tensor", "dp"),
            P(), P(), P(), weights, P(), P("tensor", "dp"), P(), P(), P(),
        ),
        check_vma=False,
    )
```

```python
import functools

import jax
import jax.numpy as jnp
from jax import lax
from jax.experimental import pallas as pl
from jax.experimental.pallas import tpu as pltpu
from jax.sharding import PartitionSpec as P

HD = 64
BLOCK = 512
KEY_PARTS = 2
LANES = 128
EPS = 1e-05
MASKED = -1e30
SQRT_HALF = 0.7071067811865476
INV_SQRT_2PI = 0.3989422804014327
VMEM_LIMIT = 60000 * 1024

f32 = jnp.float32
bf16 = jnp.bfloat16


def dot_nn(a, b):
    return lax.dot_general(a, b, (((1,), (0,)), ((), ())), preferred_element_type=f32)


def dot_nt(a, b):
    return lax.dot_general(a, b, (((1,), (1,)), ((), ())), preferred_element_type=f32)


def params(**kw):
    return pltpu.CompilerParams(vmem_limit_bytes=VMEM_LIMIT, **kw)


def cost(flops, nbytes, transcendentals=0, short=1):
    return pl.CostEstimate(
        flops=7 * flops // (2 * short), bytes_accessed=nbytes // short, transcendentals=transcendentals
    )


def copies(jobs, sems):
    started = []
    for at, (source, target) in enumerate(jobs):
        copy = pltpu.make_async_copy(source, target, sems.at[at])
        copy.start()
        started.append(copy)
    return started


def block_rows(index, rows):
    return pl.ds(pl.multiple_of(index * rows, rows), rows)


def head_columns(heads):
    return [[HD * (part * heads + h) for part in range(6)] for h in range(heads)]


def by_heads(value, heads):
    cols = [value[:, at : at + HD] for parts in head_columns(heads) for at in parts]
    return jnp.concatenate(cols, 1)


def by_parts(value, heads):
    cols = [value[:, HD * (6 * h + part) : HD * (6 * h + part + 1)] for part in range(6) for h in range(heads)]
    return jnp.concatenate(cols, 1)


def project_weight_jobs(layout, pos_ref, refs, w_ref):
    jobs = []
    chip = pos_ref[2] // 2
    for masks, ref in zip(layout, refs):
        if masks is None:
            jobs.append((ref, w_ref))
            continue
        for u, (mask, second) in enumerate(masks):
            jobs.append((ref.at[u], w_ref.at[block_rows(2 * (chip ^ mask) + second, ref.shape[1])]))
    return jobs


def project_kernel(heads, layout, pos_ref, x0, x1, x2, x3, b_ref, ent_ref, *rest):
    count = len(layout)
    pieces = rest[:count]
    qc_ref, kc_ref, kv_ref, w_ref, x_ref, raw_ref, b_scr, sems = rest[count:]

    @pl.when(pl.program_id(0) == 0)
    def _():
        jobs = [(ref, x_ref.at[m]) for m, ref in enumerate((x0, x1, x2, x3))]
        for copy in copies(jobs + project_weight_jobs(layout, pos_ref, pieces, raw_ref), sems):
            copy.wait()
        w_ref[...] = by_heads(raw_ref[...], heads)
        b_scr[...] = by_heads(jnp.broadcast_to(b_ref[...], b_scr.shape), heads)

    x = x_ref[pl.program_id(0)]
    ent = ent_ref[...] > 0.5
    lane = lax.broadcasted_iota(jnp.int32, (x.shape[0], LANES), 1)
    low_half = lane < HD
    keep = jnp.logical_xor(low_half, ent)
    every = dot_nn(x, w_ref[...]) + b_scr[:1]
    for h in range(heads):
        y = every[:, 3 * LANES * h : 3 * LANES * (h + 1)]
        q = jnp.where(ent, y[:, LANES : 2 * LANES], y[:, :LANES])
        qc_ref[h] = q.astype(bf16) * (HD ** (-0.5))
        kv = y[:, 2 * LANES :].astype(bf16).astype(f32)
        kv_ref[h] = kv.astype(bf16)
        twice = jnp.where(low_half, kv, pltpu.roll(kv, HD, 1))
        kc_ref[h] = jnp.where(keep, twice, 0.0).astype(bf16)


def project(pos, x, pieces, layout, b, ent):
    own_rows, width = x[0].shape
    tokens = own_rows * len(x)
    columns = b.shape[1]
    heads = columns // (3 * LANES)
    out = jax.ShapeDtypeStruct((heads, tokens, LANES), bf16)
    spec = pl.BlockSpec((heads, own_rows, LANES), lambda m, pos: (0, m ^ pos[0], 0))
    anywhere = pl.BlockSpec(memory_space=pltpu.HBM)
    jobs = sum(1 if masks is None else len(masks) for masks in layout)
    return pl.pallas_call(
        functools.partial(project_kernel, heads, layout),
        grid_spec=pltpu.PrefetchScalarGridSpec(
            num_scalar_prefetch=1,
            grid=(len(x),),
            in_specs=[anywhere] * 4
            + [
                pl.BlockSpec((1, columns), lambda m, pos: (0, 0)),
                pl.BlockSpec((own_rows, LANES), lambda m, pos: (m ^ pos[0], 0)),
            ]
            + [anywhere] * len(pieces),
            out_specs=[spec, spec, spec, pl.BlockSpec((width, columns), lambda m, pos: (0, 0))],
            scratch_shapes=[
                pltpu.VMEM((len(x), own_rows, width), bf16),
                pltpu.VMEM((width, columns), bf16),
                pltpu.VMEM((8, columns), f32),
                pltpu.SemaphoreType.DMA((len(x) + jobs,)),
            ],
        ),
        out_shape=[out, out, out, jax.ShapeDtypeStruct((width, columns), bf16)],
        compiler_params=params(),
        cost_estimate=cost(2 * tokens * width * columns, 2 * tokens * (width + columns)),
        name="project",
    )(pos, *x, b, ent, *pieces)


def masked_keys(pos_ref, scores, first=0):
    keys = first + lax.broadcasted_iota(jnp.int32, (scores.shape[0], 1), 0)
    return scores + jnp.where(keys < pos_ref[4], 0.0, MASKED)


def attend_kernel(pos_ref, q_ref, kc_ref, kv_ref, *rest):
    out_ref, lse_ref, vt_ref = rest[-3:]

    @pl.when(pl.program_id(1) == 0)
    def _():
        vt_ref[...] = kv_ref[0].T[HD:]

    scores = masked_keys(pos_ref, dot_nt(kc_ref[0], q_ref[0]))
    top = jnp.max(scores, 0, keepdims=True)
    exponent = jnp.exp(scores - top)
    total = jnp.sum(exponent, 0, keepdims=True)
    mixed = dot_nn(vt_ref[...], exponent.astype(bf16))
    out_ref[0] = (mixed / total).astype(bf16)
    lse_ref[0] = top + jnp.log(total)


def attend(pos, first, count, qc, kc, kv, before=()):
    heads, tokens, _ = qc.shape
    blocks = tokens // BLOCK
    full = pl.BlockSpec((1, tokens, LANES), lambda h, i, pos: (first + h, 0, 0))
    return pl.pallas_call(
        attend_kernel,
        grid_spec=pltpu.PrefetchScalarGridSpec(
            num_scalar_prefetch=1,
            grid=(count, blocks),
            in_specs=[pl.BlockSpec((1, BLOCK, LANES), lambda h, i, pos: (first + h, i, 0)), full, full]
            + [pl.BlockSpec(memory_space=pltpu.HBM)] * len(before),
            out_specs=[
                pl.BlockSpec((1, HD, BLOCK), lambda h, i, pos: (i ^ pos[0], first + h, 0)),
                pl.BlockSpec((1, 1, BLOCK), lambda h, i, pos: (h, 0, i)),
            ],
            scratch_shapes=[pltpu.VMEM((HD, tokens), bf16)],
        ),
        out_shape=[
            jax.ShapeDtypeStruct((blocks, heads * HD, BLOCK), bf16),
            jax.ShapeDtypeStruct((count, 1, tokens), f32),
        ],
        input_output_aliases={4: 0} if before else {},
        compiler_params=params(),
        cost_estimate=cost(count * tokens * tokens * 2 * 3 * LANES, count * tokens * 8 * LANES),
        name="attend",
    )(pos, qc, kc, kv, *before)


def attend_back_kernel(
    pos_ref, q_ref, kc_ref, kv_ref, ent_ref, lse_ref, out_ref, go_ref,
    dq_ref, dkv_ref, kt_ref, dk_acc, dv_acc, go_pad,
):
    step = pl.program_id(1)

    @pl.when(step == 0)
    def _():
        kt_ref[...] = kc_ref[0].T
        go_pad[:HD] = jnp.zeros((HD, go_pad.shape[1]), bf16)
        dk_acc[...] = jnp.zeros_like(dk_acc)
        dv_acc[...] = jnp.zeros_like(dv_acc)

    go = go_ref[0]
    go_pad[HD:] = go
    delta = jnp.sum(go.astype(f32) * out_ref[0].astype(f32), 0, keepdims=True)
    q = q_ref[0]
    rows = kc_ref.shape[1] // KEY_PARTS

    def keys_part(part, dq):
        at = block_rows(part, rows)
        scores = masked_keys(pos_ref, dot_nt(kc_ref[0, at], q), part * rows)
        probs = jnp.exp(scores - lse_ref[0])
        grad_probs = dot_nn(kv_ref[0, at], go_pad[...])
        grad_scores = (probs * (grad_probs - delta)).astype(bf16)
        dv_acc[at] += dot_nt(probs.astype(bf16), go_pad[...])
        dk_acc[at] += dot_nn(grad_scores, q)
        return dq + dot_nn(kt_ref[:, at], grad_scores)

    dq = lax.fori_loop(0, KEY_PARTS, keys_part, jnp.zeros((LANES, q.shape[0]), f32))
    dq_ref[0] = (dq * (HD ** (-0.5))).T.astype(bf16)

    @pl.when(step == pl.num_programs(1) - 1)
    def _():
        lane = lax.broadcasted_iota(jnp.int32, dk_acc.shape, 1)
        dk = dk_acc[...]
        dk = jnp.where(ent_ref[...] > 0.5, pltpu.roll(dk, HD, 1), dk)
        dkv_ref[0] = jnp.where(lane < HD, dk, dv_acc[...]).astype(bf16)


def attend_back(pos, first, count, qc, kc, kv, ent, lse, mixed, grad_mixed):
    tokens = qc.shape[1]
    blocks = tokens // BLOCK
    full = pl.BlockSpec((1, tokens, LANES), lambda h, i, pos: (first + h, 0, 0))
    slot = pl.BlockSpec((1, HD, BLOCK), lambda h, i, pos: (i ^ pos[0], first + h, 0))
    out = jax.ShapeDtypeStruct((count, tokens, LANES), bf16)
    return pl.pallas_call(
        attend_back_kernel,
        grid_spec=pltpu.PrefetchScalarGridSpec(
            num_scalar_prefetch=1,
            grid=(count, blocks),
            in_specs=[
                pl.BlockSpec((1, BLOCK, LANES), lambda h, i, pos: (first + h, i, 0)),
                full, full,
                pl.BlockSpec((tokens, LANES), lambda h, i, pos: (0, 0)),
                pl.BlockSpec((1, 1, BLOCK), lambda h, i, pos: (h, 0, i)),
                slot, slot,
            ],
            out_specs=[
                pl.BlockSpec((1, BLOCK, LANES), lambda h, i, pos: (h, i, 0)),
                pl.BlockSpec((1, tokens, LANES), lambda h, i, pos: (h, 0, 0)),
            ],
            scratch_shapes=[
                pltpu.VMEM((LANES, tokens), bf16),
                pltpu.VMEM((tokens, LANES), f32),
                pltpu.VMEM((tokens, LANES), f32),
                pltpu.VMEM((LANES, BLOCK), bf16),
            ],
        ),
        out_shape=[out, out],
        compiler_params=params(),
        cost_estimate=cost(count * tokens * tokens * 2 * 5 * LANES, count * tokens * 16 * LANES),
        name="attend_back",
    )(pos, qc, kc, kv, ent, lse, mixed, grad_mixed)


def normed(residual, gain, shift):
    center = residual - jnp.mean(residual, -1, keepdims=True)
    inv = lax.rsqrt(jnp.mean(center * center, -1, keepdims=True) + EPS)
    unit = center * inv
    return unit, inv, unit * gain + shift


def norm_back(grad, unit, inv, gain):
    scaled = grad * gain
    return (
        scaled
        - jnp.mean(scaled, -1, keepdims=True)
        - unit * jnp.mean(scaled * unit, -1, keepdims=True)
    ) * inv


def token_weight_jobs(layout, pos_ref, refs, w_ref):
    jobs = []
    for masks, ref in zip(layout, refs):
        if masks is None:
            jobs.append((ref, w_ref))
            continue
        for u, (mask, group_mask) in enumerate(masks):
            where = block_rows(pos_ref[2] ^ mask, ref.shape[1])
            jobs.append((ref.at[u], w_ref.at[pos_ref[1] ^ group_mask, where]))
    return jobs


def token_kernel(
    layout, pos_ref, m0, m1, m2, m3, hid_ref, cot_ref, valid_ref, vec_ref, *rest
):
    count = len(layout)
    pieces = rest[:count]
    (
        y_ref, mixt_ref, nb_ref, act_ref, gi_ref, gf_ref, ga_ref, gm_ref, gr_ref, sums_ref, gib_ref,
        slope_ref, w_ref, sum_ref, unit_ref, inv_ref, sems,
    ) = rest[count:]
    me = pos_ref[0]
    groups, width, _ = w_ref.shape
    tokens = hid_ref.shape[0]
    ffn = act_ref.shape[2]
    gwidth = mixt_ref.shape[1]
    out_at = 2 * ffn
    jobs = token_weight_jobs(layout, pos_ref, pieces, w_ref)
    early = slice(out_at, out_at + gwidth)
    loads = copies([(s.at[..., early], t.at[..., early]) for s, t in jobs], sems.at[0])
    late = copies([(s.at[..., :out_at], t.at[..., :out_at]) for s, t in jobs], sems.at[1])
    for load in loads:
        load.wait()
    for m, ref in enumerate((m0, m1, m2, m3)):
        mixt_ref[me ^ m] = ref[0]

    def vector(at):
        value = vec_ref[at]
        return jnp.concatenate([value[i : i + 1] for i in range(value.shape[0])], 1)

    out_b, gain_one, shift_one, output_b, gain_two, shift_two = (vector(at) for at in range(6))
    few = min(LANES, tokens)
    sums_ref[...] = jnp.zeros_like(sums_ref)
    gib_ref[...] = jnp.zeros_like(gib_ref)

    def by_blocks(body):
        lax.fori_loop(0, tokens // few, lambda r, _: (body(block_rows(r, few)), 0)[1], 0)

    def total(at, value):
        sums_ref[at] += jnp.sum(value, 0, keepdims=True)

    def first_norm(at):
        attended = out_b
        for g in range(groups):
            part = dot_nt(mixt_ref[g, :, at].T, w_ref[g, :, early])
            attended = attended + part.astype(bf16).astype(f32)
        unit, inv, value = normed(hid_ref[at].astype(f32) + attended, gain_one, shift_one)
        unit_ref[at] = unit
        inv_ref[at] = jnp.broadcast_to(inv, (inv.shape[0], LANES))
        nb_ref[at] = value.astype(bf16)
        sum_ref[at] = jnp.broadcast_to(output_b, value.shape)

    first_norm(slice(0, tokens))
    for load in late:
        load.wait()
    halves = 2
    part_rows = tokens // halves

    def forward(step, _):
        g, at = step // halves, block_rows(step % halves, part_rows)
        pre = dot_nn(nb_ref[at], w_ref[g, :, :ffn]) + vector(6 + g)
        cdf = 0.5 * (1.0 + lax.erf(pre * SQRT_HALF))
        slope_ref[g, at] = cdf + pre * (jnp.exp(-0.5 * pre * pre) * INV_SQRT_2PI)
        active = (pre * cdf).astype(bf16)
        act_ref[g, at] = active
        part = dot_nt(active, w_ref[g, :, ffn:out_at])
        sum_ref[at] += part.astype(bf16).astype(f32)
        return 0

    lax.fori_loop(0, groups * halves, forward, 0)

    def second_norm(at):
        valid = valid_ref[at, :1]
        normed_one = unit_ref[at] * gain_one + shift_one
        unit, inv, value = normed(normed_one + sum_ref[at], gain_two, shift_two)
        y_ref[at] = (value * valid).astype(bf16)
        grad_top = cot_ref[at].astype(f32) * valid
        grad = norm_back(grad_top, unit, inv, gain_two)
        grad_ffn = grad.astype(bf16)
        gf_ref[at] = grad_ffn
        sum_ref[at] = grad
        total(3, grad_ffn.astype(f32))
        total(4, grad_top * unit)
        total(5, grad_top)

    by_blocks(second_norm)

    def backward(step, _):
        g, at = step // halves, block_rows(step % halves, part_rows)
        grad_active = dot_nn(gf_ref[at], w_ref[g, :, ffn:out_at])
        grad_inner = (slope_ref[g, at] * grad_active).astype(bf16)
        gi_ref[g, at] = grad_inner
        gib_ref[g] += jnp.sum(grad_inner.astype(f32), 0, keepdims=True)
        part = dot_nt(grad_inner, w_ref[g, :, :ffn])
        sum_ref[at] += part.astype(bf16).astype(f32)
        return 0

    lax.fori_loop(0, groups * halves, backward, 0)

    def first_norm_back(at):
        grad_normed = sum_ref[at]
        unit = unit_ref[at]
        grad = norm_back(grad_normed, unit, inv_ref[at, :1], gain_one)
        gr_ref[at] = grad
        grad_att = grad.astype(bf16)
        ga_ref[at] = grad_att
        total(0, grad_att.astype(f32))
        total(1, grad_normed * unit)
        total(2, grad_normed)

    by_blocks(first_norm_back)

    def mixed_back(m, _):
        out_rows = w_ref[me ^ m, :, early].T
        gm_ref[m] = dot_nt(out_rows, ga_ref[...]).astype(bf16)
        return 0

    for m in range(groups):
        mixed_back(m, 0)


def per_token(
    pos, mixed, hidden, cot, valid, vectors, pieces, layout, groups, columns
):
    tokens, width = hidden.shape
    ffn = vectors.shape[1] * vectors.shape[2]
    gwidth = mixed[0].shape[1]
    vmem = pl.BlockSpec(memory_space=pltpu.VMEM)
    shape = jax.ShapeDtypeStruct
    jobs = sum(1 if masks is None else len(masks) for masks in layout)
    return pl.pallas_call(
        functools.partial(token_kernel, layout),
        in_specs=[pl.BlockSpec(memory_space=pltpu.SMEM)]
        + [vmem] * 8
        + [pl.BlockSpec(memory_space=pltpu.HBM)] * len(pieces),
        out_specs=[vmem] * 11,
        out_shape=[
            shape((tokens, width), bf16),
            shape((groups, gwidth, tokens), bf16),
            shape((tokens, width), bf16),
            shape((groups, tokens, ffn), bf16),
            shape((groups, tokens, ffn), bf16),
            shape((tokens, width), bf16),
            shape((tokens, width), bf16),
            shape((groups, gwidth, tokens), bf16),
            shape((tokens, width), f32),
            shape((6, 1, width), f32),
            shape((groups, 1, ffn), f32),
        ],
        scratch_shapes=[
            pltpu.VMEM((groups, tokens, ffn), f32),
            pltpu.VMEM((groups, width, columns), bf16),
            pltpu.VMEM((tokens, width), f32),
            pltpu.VMEM((tokens, width), f32),
            pltpu.VMEM((tokens, LANES), f32),
            pltpu.SemaphoreType.DMA((2, jobs)),
        ],
        compiler_params=params(),
        cost_estimate=cost(
            8 * tokens * width * ffn * groups + 4 * tokens * width * width,
            2 * groups * width * columns + 4 * tokens * ffn * groups,
            2 * tokens * ffn * groups,
        ),
        name="per_token",
    )(pos, *mixed, hidden, cot, valid, vectors, *pieces)


def weight_grad_kernel(
    pos_ref, nb_ref, gf_ref, ga_ref, act_ref, gi_ref, mixt_ref, near_ref, far_ref, nbt, gft, gat, turn
):
    ffn = act_ref.shape[2]
    gwidth = mixt_ref.shape[1]
    chips, _, rows, _ = near_ref.shape

    @pl.when(pl.program_id(0) == 0)
    def _():
        for target, source in ((nbt, nb_ref), (gft, gf_ref), (gat, ga_ref)):
            turn[...] = source[...].T
            for mine in range(2):
                for mask in range(chips):
                    block = pos_ref[2] ^ (2 * mask + mine)
                    at = (mine * chips + mask) * rows
                    target[at : at + rows] = turn[block_rows(block, rows)]

    second_half = (pl.program_id(0) ^ pos_ref[1]) % 2

    def put(value, start, stop):
        for mine, out_ref in enumerate((near_ref, far_ref)):
            for mask in range(chips):
                slot = mask + second_half - 1 if mask == 2 else mask + 1 - second_half if mask == 1 else mask
                at = (mine * chips + mask) * rows
                out_ref[slot, 0, :, start:stop] = value[at : at + rows].astype(bf16)

    put(dot_nn(nbt[...], gi_ref[0]), 0, ffn)
    put(dot_nn(gft[...], act_ref[0]), ffn, 2 * ffn)
    put(dot_nt(gat[...], mixt_ref[0]), 2 * ffn, 2 * ffn + gwidth)


def weight_grads(pos, nb, gf, ga, act, gi, mixt, dp):
    groups, tokens, ffn = act.shape
    width = nb.shape[1]
    gwidth = mixt.shape[1]
    rows = width // dp
    whole = pl.BlockSpec((tokens, width), lambda g, pos: (0, 0))
    group = pl.BlockSpec((1, tokens, ffn), lambda g, pos: (g, 0, 0))
    columns = 2 * ffn + gwidth
    out = jax.ShapeDtypeStruct((dp // 2, groups, rows, columns), bf16)

    def slot(g, pos):
        mask = g ^ pos[1]
        return (0, 2 * (mask % 2) + mask // 2, 0, 0)

    spec = pl.BlockSpec((dp // 2, 1, rows, columns), slot)
    return pl.pallas_call(
        weight_grad_kernel,
        grid_spec=pltpu.PrefetchScalarGridSpec(
            num_scalar_prefetch=1,
            grid=(groups,),
            in_specs=[
                whole, whole, whole, group, group,
                pl.BlockSpec((1, gwidth, tokens), lambda g, pos: (g, 0, 0)),
            ],
            out_specs=[spec, spec],
            scratch_shapes=[pltpu.VMEM((width, tokens), bf16)] * 4,
        ),
        out_shape=[out, out],
        compiler_params=params(),
        cost_estimate=cost(2 * tokens * width * columns * groups, 2 * groups * width * columns),
        name="weight_grads",
    )(pos, nb, gf, ga, act, gi, mixt)


def weight_grad_whole_kernel(nb_ref, gf_ref, ga_ref, act_ref, gi_ref, mixt_ref, out_ref, nbt, gft, gat):
    ffn = act_ref.shape[2]
    gwidth = mixt_ref.shape[1]

    @pl.when(pl.program_id(0) == 0)
    def _():
        nbt[...] = nb_ref[...].T
        gft[...] = gf_ref[...].T
        gat[...] = ga_ref[...].T

    out_ref[0, :, :ffn] = dot_nn(nbt[...], gi_ref[0]).astype(bf16)
    out_ref[0, :, ffn : 2 * ffn] = dot_nn(gft[...], act_ref[0]).astype(bf16)
    out_ref[0, :, 2 * ffn : 2 * ffn + gwidth] = dot_nt(gat[...], mixt_ref[0]).astype(bf16)


def weight_grads_whole(nb, gf, ga, act, gi, mixt):
    groups, tokens, ffn = act.shape
    width = nb.shape[1]
    gwidth = mixt.shape[1]
    whole = pl.BlockSpec((tokens, width), lambda g: (0, 0))
    group = pl.BlockSpec((1, tokens, ffn), lambda g: (g, 0, 0))
    columns = 2 * ffn + gwidth
    return pl.pallas_call(
        weight_grad_whole_kernel,
        grid=(groups,),
        in_specs=[whole, whole, whole, group, group, pl.BlockSpec((1, gwidth, tokens), lambda g: (g, 0, 0))],
        out_specs=pl.BlockSpec((1, width, columns), lambda g: (g, 0, 0)),
        out_shape=jax.ShapeDtypeStruct((groups, width, columns), bf16),
        scratch_shapes=[pltpu.VMEM((width, tokens), bf16)] * 3,
        compiler_params=params(),
        cost_estimate=cost(2 * tokens * width * columns * groups, 2 * groups * width * columns),
        name="weight_grads_whole",
    )(nb, gf, ga, act, gi, mixt)


def split_columns(pairs, ent):
    h = 0
    for dq_ref, dkv_ref in pairs:
        for u in range(dq_ref.shape[0]):
            dq = dq_ref[u]
            nothing = jnp.zeros_like(dq)
            yield 3 * h, jnp.where(ent, nothing, dq)
            yield 3 * h + 1, jnp.where(ent, dq, nothing)
            yield 3 * h + 2, dkv_ref[u]
            h += 1


def input_grad_kernel(count, pos_ref, *refs):
    grads, (ent_ref, w_ref, out_ref) = refs[:count], refs[count:]
    ent = ent_ref[...] > 0.5
    cols = [c for _, c in split_columns(list(zip(grads[::2], grads[1::2])), ent)]
    out_ref[0] = dot_nt(jnp.concatenate(cols, 1), w_ref[...]).astype(bf16)


def input_grad(pos, grads, ent, w, far):
    tokens = grads[0].shape[1]
    width, columns = w.shape

    def block(i, pos):
        return i + 2 * (pos[3] ^ far)

    stacked = [pl.BlockSpec((g.shape[0], BLOCK, LANES), lambda i, pos: (0, block(i, pos), 0)) for g in grads]
    return pl.pallas_call(
        functools.partial(input_grad_kernel, len(grads)),
        grid_spec=pltpu.PrefetchScalarGridSpec(
            num_scalar_prefetch=1,
            grid=(2,),
            in_specs=stacked
            + [
                pl.BlockSpec((BLOCK, LANES), lambda i, pos: (block(i, pos), 0)),
                pl.BlockSpec((width, columns), lambda i, pos: (0, 0)),
            ],
            out_specs=pl.BlockSpec((1, BLOCK, width), lambda i, pos: (i ^ (pos[0] % 2), 0, 0)),
        ),
        out_shape=jax.ShapeDtypeStruct((2, BLOCK, width), bf16),
        compiler_params=params(),
        cost_estimate=cost(tokens * width * columns, tokens * (columns + width), short=100),
        name="input_grad",
    )(pos, *grads, ent, w)


def all_sums(pos_ref, bias, sums_ref, gib_ref, out_ref):
    gwidth = bias.shape[1] // 6
    zeros = jnp.zeros((1, gwidth), f32)
    for row, part in enumerate((0, 1, 2, 3, 5)):
        own = bias[:1, gwidth * part : gwidth * (part + 1)]
        out_ref[row : row + 1] = jnp.concatenate(
            [jnp.where(pos_ref[0] == j, own, zeros) for j in range(out_ref.shape[1] // gwidth)], 1
        )
    rest = [sums_ref[i] for i in range(sums_ref.shape[0])] + [gib_ref[i] for i in range(gib_ref.shape[0])]
    for row, value in enumerate(rest):
        out_ref[5 + row : 6 + row] = value
    out_ref[5 + len(rest) :] = jnp.zeros((out_ref.shape[0] - 5 - len(rest), out_ref.shape[1]), f32)


def project_grad_kernel(pos_ref, x0, x1, x2, x3, *refs):
    (
        *grads, ent_ref, sums_ref, gib_ref, keep_ref, first_ref, second_ref, bias_ref, acc_ref, bias_acc,
        x_ref, sems,
    ) = refs
    step = pl.program_id(0)

    @pl.when(step == 0)
    def _():
        loads = copies([(ref, x_ref.at[m]) for m, ref in enumerate((x0, x1, x2, x3))], sems)
        acc_ref[...] = jnp.zeros_like(acc_ref)
        bias_acc[...] = jnp.zeros_like(bias_acc)
        for load in loads:
            load.wait()

    ent = ent_ref[...] > 0.5
    columns = jnp.concatenate([c for _, c in split_columns(list(zip(grads[::2], grads[1::2])), ent)], 1)
    acc_ref[...] += dot_nn(x_ref[step].T, columns)
    bias_acc[:1] += jnp.sum(columns.astype(f32), 0, keepdims=True)

    @pl.when(step == pl.num_programs(0) - 1)
    def _():
        chips, cores, rows, columns = keep_ref.shape
        heads = columns // (3 * LANES)
        all_sums(pos_ref, by_parts(bias_acc[...], heads), sums_ref, gib_ref, bias_ref)
        targets = [
            [keep_ref.at[0, 0], first_ref.at[0], keep_ref.at[1, 0], first_ref.at[1]],
            [keep_ref.at[0, 1], keep_ref.at[1, 1], second_ref.at[0], second_ref.at[1]],
        ]
        for mask in range(4):
            for core in range(2):
                at = block_rows(2 * ((pos_ref[2] // 2) ^ mask) + core, rows)
                targets[core][mask][...] = by_parts(acc_ref[at].astype(bf16), heads)


def project_grad_whole_kernel(*refs):
    *ins, out_ref, bias_ref, acc_ref, bias_acc, x_ref, sems = refs
    heads = out_ref.shape[1] // (3 * LANES)
    pos_ref, x0, x1, x2, x3, *grads, ent_ref, sums_ref, gib_ref = ins
    step = pl.program_id(0)

    @pl.when(step == 0)
    def _():
        loads = copies([(ref, x_ref.at[m]) for m, ref in enumerate((x0, x1, x2, x3))], sems)
        acc_ref[...] = jnp.zeros_like(acc_ref)
        bias_acc[...] = jnp.zeros_like(bias_acc)
        for load in loads:
            load.wait()

    ent = ent_ref[...] > 0.5
    columns = jnp.concatenate([c for _, c in split_columns(list(zip(grads[::2], grads[1::2])), ent)], 1)
    acc_ref[...] += dot_nn(x_ref[step].T, columns)
    bias_acc[:1] += jnp.sum(columns.astype(f32), 0, keepdims=True)

    @pl.when(step == pl.num_programs(0) - 1)
    def _():
        out_ref[...] = by_parts(acc_ref[...].astype(bf16), heads)
        all_sums(pos_ref, by_parts(bias_acc[...], heads), sums_ref, gib_ref, bias_ref)


def project_grad(pos, x, grads, ent, sums, gib, by_hops):
    heads = sum(g.shape[0] for g in grads) // 2
    tokens = grads[0].shape[1]
    own_rows, width = x[0].shape
    columns = 3 * LANES * heads
    rows = width // 8
    shapes = [(2, 2, rows, columns)] + [(2, rows, columns)] * 2 if by_hops else [(width, columns)]
    stacked = [pl.BlockSpec((g.shape[0], own_rows, LANES), lambda m, pos: (0, m ^ pos[0], 0)) for g in grads]

    def fixed(shape):
        return pl.BlockSpec(shape, lambda m, pos: (0,) * len(shape))

    return pl.pallas_call(
        project_grad_kernel if by_hops else project_grad_whole_kernel,
        grid_spec=pltpu.PrefetchScalarGridSpec(
            num_scalar_prefetch=1,
            grid=(len(x),),
            in_specs=[pl.BlockSpec(memory_space=pltpu.HBM)] * 4
            + stacked
            + [pl.BlockSpec((own_rows, LANES), lambda m, pos: (m ^ pos[0], 0))]
            + [fixed(sums.shape), fixed(gib.shape)],
            out_specs=[fixed(shape) for shape in shapes] + [fixed((16, width))],
            scratch_shapes=[
                pltpu.VMEM((width, columns), f32),
                pltpu.VMEM((8, columns), f32),
                pltpu.VMEM((len(x), own_rows, width), bf16),
                pltpu.SemaphoreType.DMA((len(x),)),
            ],
        ),
        out_shape=[jax.ShapeDtypeStruct(shape, bf16) for shape in shapes]
        + [jax.ShapeDtypeStruct((16, width), f32)],
        compiler_params=params(),
        cost_estimate=cost(2 * tokens * width * columns, 2 * tokens * (columns + width)),
        name="project_grad",
    )(pos, *x, *grads, ent, sums, gib)


def finish_project_kernel(kept_ref, arrived_ref, q_ref, k_ref, v_ref):
    total = kept_ref[...].astype(f32) + arrived_ref[...].astype(f32)
    width = k_ref.shape[1]
    for a in range(q_ref.shape[0]):
        q_ref[a] = total[:, width * a : width * (a + 1)]
    k_ref[...] = total[:, 4 * width : 5 * width]
    v_ref[...] = total[:, 5 * width :]


def finish_project(kept, arrived):
    rows, columns = kept.shape
    part = jax.ShapeDtypeStruct((rows, columns // 6), f32)
    return pl.pallas_call(
        finish_project_kernel,
        out_shape=[jax.ShapeDtypeStruct((4, rows, columns // 6), f32), part, part],
        compiler_params=params(),
        cost_estimate=cost(rows * columns, 8 * rows * columns),
        name="finish_project",
    )(kept, arrived)


def finish_ffn_kernel(kept_ref, arrived_ref, inter_ref, output_ref, out_ref):
    total = kept_ref[...].astype(f32) + arrived_ref[...].astype(f32)
    ffn = inter_ref.shape[1]
    inter_ref[...] = total[:, :ffn]
    output_ref[...] = total[:, ffn : 2 * ffn].T
    out_ref[...] = total[:, 2 * ffn :].T


def finish_ffn(kept, arrived, ffn):
    rows, columns = kept.shape
    shape = jax.ShapeDtypeStruct
    return pl.pallas_call(
        finish_ffn_kernel,
        out_shape=[shape((rows, ffn), f32), shape((ffn, rows), f32), shape((columns - 2 * ffn, rows), f32)],
        compiler_params=params(),
        cost_estimate=cost(rows * columns, 8 * rows * columns),
        name="finish_ffn",
    )(kept, arrived)


def local(
    hidden_in, token_types, lengths, cotangent, query_w, query_b, key_w, value_w, value_b, out_w,
    out_b, gain_one, shift_one, inter_w, inter_b, output_w, output_b, gain_two, shift_two,
):
    groups = lax.axis_size("tensor")
    dp = lax.axis_size("dp")
    z = lax.axis_index("tensor")
    d = lax.axis_index("dp")
    half = groups // 2
    core = d % 2
    upper = z // half
    me = z % half + half * core
    own_rows, width = hidden_in.shape
    length = own_rows * groups
    gwidth = query_w.shape[2]
    heads = gwidth // HD
    ffn = inter_w.shape[1]
    rows = key_w.shape[0]
    columns = 2 * ffn + gwidth
    total = dp * groups
    by_hops = dp == 8 and rows % 16 == 0

    def device(dd, zz):
        return dd * groups + zz

    def swapped(dev):
        dd, zz = dev // groups, dev % groups
        return device(dd - dd % 2 + zz // half, zz % half + half * (dd % 2))

    def member(dev, mask):
        dd, zz = dev // groups, dev % groups
        j = (zz % half + half * (dd % 2)) ^ mask
        return device(dd - dd % 2 + j // half, zz - zz % half + j % half)

    stays = core == upper

    def relocate(value):
        moves = [(i, swapped(i)) for i in range(total) if swapped(i) != i]
        return jnp.where(stays, value, lax.ppermute(value, ("dp", "tensor"), moves))

    def to_member(value, mask):
        return lax.ppermute(value, ("dp", "tensor"), [(i, member(i, mask)) for i in range(total)])

    def over_dp(value, mask):
        return lax.ppermute(value, "dp", [(i, i ^ mask) for i in range(dp)])

    def over_z(value, mask):
        return lax.ppermute(value, "tensor", [(i, i ^ mask) for i in range(groups)])

    def add(*terms):
        return functools.reduce(jnp.add, [t.astype(f32) for t in terms])

    def after(value, *others):
        return lax.optimization_barrier((value, *others))[0]

    own_project = jnp.concatenate([*query_w, key_w, value_w], 1)
    own_ffn = jnp.concatenate([inter_w, output_w.T, out_w.T], 1)

    def between(value, pairs):
        return lax.ppermute(value, ("dp", "tensor"), [p for p in pairs if p[0] != p[1]])

    swaps = [(i, swapped(i)) for i in range(total)]
    on_chips = [(i, member(i, 1)) for i in range(total)]
    stay_chips = [p for p in on_chips if swapped(p[0]) == p[0]]
    move_chips = [p for p in on_chips if swapped(p[0]) != p[0]]

    def phase(*values):
        return lax.optimization_barrier(values)

    near_chip = between(hidden_in, stay_chips)
    moved = between(hidden_in, swaps)
    facts = jnp.concatenate([token_types, lengths])
    facts_moved = over_dp(facts, 1)
    few = (query_b, value_b, out_b, gain_one, shift_one, output_b, gain_two, shift_two, inter_b)
    if by_hops:
        other = over_dp(own_project, 1)
        pair = jnp.where(core == 0, jnp.stack([own_project, other]), jnp.stack([other, own_project]))
        pair, facts_moved, facts, *few = phase(relocate(pair), facts_moved, facts, *few)
    query_b, value_b, *rest = few
    query_b_own = lax.dynamic_slice_in_dim(query_b, me * gwidth, gwidth, 1)
    value_b_own = lax.dynamic_slice_in_dim(value_b, me * gwidth, gwidth)
    b_project = jnp.concatenate([query_b_own.reshape(-1), jnp.zeros((gwidth,), bf16), value_b_own])
    b_project = b_project.reshape(1, 6 * gwidth).astype(f32)
    vectors = jnp.concatenate([v.astype(f32).reshape(-1, width // LANES, LANES) for v in rest])
    facts = jnp.where(stays, facts, facts_moved)
    pos = jnp.concatenate([jnp.stack([me, z, d, upper]).astype(jnp.int32), facts[length:]])
    ent = jnp.broadcast_to(facts[:length, None].astype(bf16), (length, LANES))
    valid_own = me * own_rows + jnp.arange(own_rows, dtype=jnp.int32) < facts[length]
    valid_own = jnp.broadcast_to(valid_own[:, None].astype(f32), (own_rows, LANES))
    if by_hops:
        moved, near_chip, own_z, own_ffn, b_project, vectors, pos, ent, valid_own = phase(
            moved, near_chip, over_z(own_ffn, 1), own_ffn, b_project, vectors, pos, ent, valid_own
        )
    hidden = jnp.where(stays, hidden_in, moved)
    from_chip = between(hidden, move_chips)
    if by_hops:
        pair_x, pair_y = over_dp(pair, 2), over_dp(pair, 4)
        from_chip, a_xy, b_xy, own_x, own_y = phase(
            from_chip, over_dp(pair_x[0], 4), over_dp(pair_y[1], 2), over_dp(own_ffn, 2), over_dp(own_ffn, 4)
        )
        from_chip = jnp.where(stays, near_chip, from_chip)
        x_2, x_3, own_ffn, own_x, own_z = phase(
            to_member(hidden, half), to_member(from_chip, half), own_ffn, own_x, own_z
        )
        both = ((0, 0), (0, 1))
        project_pieces = [pair, pair_x, pair_y, a_xy[None], b_xy[None]]
        project_layout = (both, tuple((1, c) for _, c in both), tuple((2, c) for _, c in both), ((3, 0),), ((3, 1),))
    else:
        project_pieces = [relocate(lax.all_gather(own_project, "dp", axis=0, tiled=True))]
        project_layout = (None,)
        from_chip = jnp.where(stays, near_chip, from_chip)
        x_2, x_3 = to_member(hidden, half), to_member(from_chip, half)
    x = [hidden, from_chip, x_2, x_3]

    qc, kc, kv, w_project = project(pos, x, project_pieces, project_layout, b_project, ent)
    if by_hops:
        token_pieces, token_layout = [], []

        def pieces(group_mask, **by):
            masks = [({"own": 0, "x": 2, "y": 4, "xy": 6}[axes], group_mask) for axes in by]
            token_layout.extend([tuple(masks), tuple((m + 1, g) for m, g in masks)])
            return jnp.stack(list(by.values()))

        qc, far, own_zx, own_zy, own_xy = phase(
            qc, over_z(own_ffn, 2), over_dp(own_z, 2), over_dp(own_z, 4), over_dp(own_x, 4)
        )
        quad = pieces(0, own=own_ffn, x=own_x, y=own_y, xy=own_xy)
        mixed, lse_0 = attend(pos, 0, 1, qc, kc, kv)
        mixed, far_z, far_x, far_y, quad_core = phase(
            mixed, over_z(far, 1), over_dp(far, 2), over_dp(far, 4), over_dp(quad, 1)
        )
        token_pieces += [quad, quad_core]
        mixed, lse_1 = attend(pos, 1, heads - 1, qc, kc, kv, (mixed,))
        mixed, far_zx, far_zy, far_xy, own_zxy, cot = phase(
            mixed, over_dp(far_z, 2), over_dp(far_z, 4), over_dp(far_x, 4), over_dp(own_zy, 2),
            between(after(cotangent, far_x), swaps),
        )
        cot = jnp.where(stays, cotangent, cot)
        quad = pieces(1, own=own_z, x=own_zx, y=own_zy, xy=own_zxy)
        mixed_own, far_zxy, quad_core, cot = phase(
            [mixed[:1]] + [to_member(mixed[m : m + 1], m) for m in range(1, groups)], over_dp(far_zy, 2),
            over_dp(quad, 1), cot
        )
        token_pieces += [quad, quad_core]
        for quad in (
            pieces(2, own=far, x=far_x, y=far_y, xy=far_xy),
            pieces(3, own=far_z, x=far_zx, y=far_zy, xy=far_zxy),
        ):
            token_pieces += [quad, over_dp(quad, 1)]
        token_layout = tuple(token_layout)
    else:
        token_pieces = [lax.all_gather(lax.all_gather(own_ffn, "tensor"), "dp", axis=1, tiled=True)]
        token_layout = (None,)
        mixed, lse_0 = attend(pos, 0, 1, qc, kc, kv)
        mixed, lse_1 = attend(pos, 1, heads - 1, qc, kc, kv, (mixed,))
        mixed_own = [mixed[:1]] + [to_member(mixed[m : m + 1], m) for m in range(1, groups)]
        cot = jnp.where(stays, cotangent, between(cotangent, swaps))
    y, mixt, nb, act, gi, gf, ga, gm, grad_resid_one, sums, gib = per_token(
        pos, mixed_own, hidden, cot, valid_own, vectors, token_pieces, token_layout, groups, columns
    )
    grad_mixed = jnp.concatenate([gm[:1]] + [to_member(gm[m : m + 1], m) for m in range(1, groups)])

    order = ((1, 2), (2, 1))
    if by_hops:
        near, far = weight_grads(pos, nb, gf, ga, act, gi, mixt, dp)
        arrived = over_dp(after(far, grad_mixed), 1)
        grads = attend_back(pos, 0, 1, qc, kc, kv, ent, lse_0, mixed, grad_mixed)
        groups_at = (slice(0, 2), slice(2, 4))
        kept = [add(near[:2, g], arrived[:2, g]).astype(bf16) for g in groups_at]
        sent = [add(near[2:, g], arrived[2:, g]).astype(bf16) for g in groups_at]
        grads, kept, sent, qc, y = phase(grads, kept, sent, qc, y)
        more = attend_back(pos, 1, heads - 1, qc, kc, kv, ent, lse_1, mixed, grad_mixed)
        more, moved, layer_moved = phase(
            more, [over_dp(v, 2 * one) for v, (one, _) in zip(sent, order)], between(y, swaps)
        )
    else:
        ffn_grads = weight_grads_whole(nb, gf, ga, act, gi, mixt)
        ffn_grads = lax.psum_scatter(ffn_grads, "tensor", scatter_dimension=0, tiled=False)
        ffn_grads = lax.psum_scatter(ffn_grads, "dp", scatter_dimension=0, tiled=True)
        grads = attend_back(pos, 0, 1, qc, kc, kv, ent, lse_0, mixed, grad_mixed)
        more = attend_back(pos, 1, heads - 1, qc, kc, kv, ent, lse_1, mixed, grad_mixed)
        layer_moved = between(y, swaps)
    layer_out = jnp.where(stays, y, layer_moved)
    grads = [*grads, *more]

    core_stay = [(i, i ^ groups) for i in range(total) if swapped(i) == i]
    core_move = [(i, i ^ groups) for i in range(total) if swapped(i) != i]
    if by_hops:
        sent = [add(k[1], m[1]).astype(bf16) for k, m in zip(kept, moved)]
        kept = [add(k[0], m[0]).astype(bf16) for k, m in zip(kept, moved)]
        first_x, sent, kept = phase(x[0], sent, kept)
        moved = [over_dp(v, 2 * two) for v, (_, two) in zip(sent, order)]
        project_kept, *project_sent, flat = project_grad(pos, [first_x, *x[1:]], grads, ent, sums, gib, True)
        project_kept, project_sent, flat, moved = phase(project_kept, project_sent, flat, moved)
        kept, sent_z = [add(k, m).astype(bf16) for k, m in zip(kept, moved)]
        kept, sent_z, first, project_sent = phase(kept, sent_z, grads[0], project_sent)
    else:
        project_grads, flat = project_grad(pos, x, grads, ent, sums, gib, False)
        first = grads[0]
    partial_far = input_grad(pos, [first, *grads[1:]], ent, w_project, 1)
    far_core = between(partial_far, core_stay)
    if by_hops:
        arrived = [over_dp(v, 2 * one) for v, (one, _) in zip(project_sent, order)]
        arrived_z = over_z(sent_z, 1)
        far_sum = add(partial_far, far_core)
        far_here, far_there, flat, second = phase(far_sum[0], far_sum[1].astype(bf16), flat, grads[3])
    else:
        far_sum = add(partial_far, far_core)
        far_here, far_there, second = far_sum[0], far_sum[1].astype(bf16), grads[3]
    far_chip = between(far_there, move_chips)
    partial_near = input_grad(pos, [*grads[:3], second], ent, w_project, 0)
    if by_hops:
        partial_near, arrived, arrived_z, hop = phase(partial_near, arrived, arrived_z, over_z(flat, 2))
        flat = flat + hop
        sent = [add(project_kept[1, s], m[1]).astype(bf16) for s, m in enumerate(arrived)]
        project_kept = [add(project_kept[0, s], m[0]).astype(bf16) for s, m in enumerate(arrived)]
        kept_z = add(kept, arrived_z)
        kept_z, last = kept_z[0], kept_z[1].astype(bf16)
        sent, last, flat, partial_near = phase(sent, last, flat, partial_near)
        far_chip, moved, last, near_core = phase(
            far_chip, [over_dp(v, 2 * two) for v, (_, two) in zip(sent, order)], over_z(last, 2),
            between(partial_near, core_move),
        )
        near_sum = add(partial_near, near_core)
        near_here, near_there = near_sum[0], near_sum[1].astype(bf16)
        far_sum = add(far_here, far_chip, grad_resid_one).astype(bf16)
        project_ends = jnp.stack([add(k, m).astype(bf16) for k, m in zip(project_kept, moved)])
        far_sum, project_ends, near_here, near_there, flat = phase(
            far_sum, project_ends, near_here, near_there, flat
        )
        flat = flat + over_z(flat, 1)
        for mask in (2, 4, 1):
            flat = flat + over_dp(flat, mask)
        project_moved = between(project_ends, swaps)
        far_moved, near_chip, flat = phase(between(far_sum, swaps), between(near_there, stay_chips), flat)
        project_ends = jnp.where(stays, project_ends, project_moved)
        project_kept = jnp.where(core == 0, project_ends[0], project_ends[1])
        sent = jnp.where(core == 0, project_ends[1], project_ends[0])
        query_grads, key_grads, value_grads = finish_project(project_kept, over_dp(sent, 1))
        inter_grads, output_grads, out_grads = finish_ffn(kept_z, last, ffn)
    else:
        far_moved = between(add(far_here, far_chip, grad_resid_one).astype(bf16), swaps)
        near_sum = add(partial_near, between(partial_near, core_move))
        near_here = near_sum[0]
        near_chip = between(near_sum[1].astype(bf16), stay_chips)
        project_grads = relocate(project_grads)
        project_grads = lax.psum_scatter(project_grads, "dp", scatter_dimension=0, tiled=True)
        query_grads, key_grads, value_grads = finish_project(project_grads, jnp.zeros_like(project_grads))
        inter_grads, output_grads, out_grads = finish_ffn(ffn_grads, jnp.zeros_like(ffn_grads), ffn)
        flat = lax.psum(flat, ("dp", "tensor"))
    near_sum = add(near_here, near_chip, grad_resid_one)
    grad_hidden = jnp.where(stays, near_sum, far_moved.astype(f32))
    return (
        layer_out,
        grad_hidden,
        query_grads,
        flat[:4],
        key_grads,
        value_grads,
        flat[4],
        out_grads,
        flat[5],
        flat[6],
        flat[7],
        inter_grads,
        flat[11 : 11 + groups].reshape(groups * ffn),
        output_grads,
        flat[8],
        flat[9],
        flat[10],
    )


def solution(mesh):
    weights = P("dp", "tensor")
    tokens = P(("dp", "tensor"), None)
    return jax.shard_map(
        local,
        mesh=mesh,
        in_specs=(
            tokens, P("dp"), P("dp"), tokens, P(None, "dp", "tensor"), P(), weights, weights, P(),
            P("tensor", "dp"), P(), P(), P(), weights, P(), P("tensor", "dp"), P(), P(), P(),
        ),
        out_specs=(
            tokens, tokens, P(None, "dp", "tensor"), P(), weights, weights, P(), P("tensor", "dp"),
            P(), P(), P(), weights, P(), P("tensor", "dp"), P(), P(), P(),
        ),
        check_vma=False,
    )
```

```python
import functools

import jax
import jax.numpy as jnp
from jax import lax
from jax.experimental import pallas as pl
from jax.experimental.pallas import tpu as pltpu
from jax.sharding import PartitionSpec as P

HD = 64
BLOCK = 512
KEY_PARTS = 2
LANES = 128
EPS = 1e-05
MASKED = -1e30
SQRT_HALF = 0.7071067811865476
INV_SQRT_2PI = 0.3989422804014327
VMEM_LIMIT = 60000 * 1024

f32 = jnp.float32
bf16 = jnp.bfloat16


def dot_nn(a, b):
    return lax.dot_general(a, b, (((1,), (0,)), ((), ())), preferred_element_type=f32)


def dot_nt(a, b):
    return lax.dot_general(a, b, (((1,), (1,)), ((), ())), preferred_element_type=f32)


def params(**kw):
    return pltpu.CompilerParams(vmem_limit_bytes=VMEM_LIMIT, **kw)


def cost(flops, nbytes, transcendentals=0, short=1):
    return pl.CostEstimate(
        flops=7 * flops // (2 * short), bytes_accessed=nbytes // short, transcendentals=transcendentals
    )


def copies(jobs, sems):
    started = []
    for at, (source, target) in enumerate(jobs):
        copy = pltpu.make_async_copy(source, target, sems.at[at])
        copy.start()
        started.append(copy)
    return started


def block_rows(index, rows):
    return pl.ds(pl.multiple_of(index * rows, rows), rows)


def head_columns(heads):
    return [[HD * (part * heads + h) for part in range(6)] for h in range(heads)]


def by_heads(value, heads):
    cols = [value[:, at : at + HD] for parts in head_columns(heads) for at in parts]
    return jnp.concatenate(cols, 1)


def by_parts(value, heads):
    cols = [value[:, HD * (6 * h + part) : HD * (6 * h + part + 1)] for part in range(6) for h in range(heads)]
    return jnp.concatenate(cols, 1)


def project_weight_jobs(layout, pos_ref, refs, w_ref):
    jobs = []
    chip = pos_ref[2] // 2
    for masks, ref in zip(layout, refs):
        if masks is None:
            jobs.append((ref, w_ref))
            continue
        for u, (mask, second) in enumerate(masks):
            jobs.append((ref.at[u], w_ref.at[block_rows(2 * (chip ^ mask) + second, ref.shape[1])]))
    return jobs


def project_kernel(heads, layout, pos_ref, x0, x1, x2, x3, b_ref, ent_ref, *rest):
    count = len(layout)
    pieces = rest[:count]
    qc_ref, kc_ref, kv_ref, w_ref, x_ref, raw_ref, b_scr, sems = rest[count:]

    @pl.when(pl.program_id(0) == 0)
    def _():
        jobs = [(ref, x_ref.at[m]) for m, ref in enumerate((x0, x1, x2, x3))]
        for copy in copies(jobs + project_weight_jobs(layout, pos_ref, pieces, raw_ref), sems):
            copy.wait()
        w_ref[...] = by_heads(raw_ref[...], heads)
        b_scr[...] = by_heads(jnp.broadcast_to(b_ref[...], b_scr.shape), heads)

    x = x_ref[pl.program_id(0)]
    ent = ent_ref[...] > 0.5
    lane = lax.broadcasted_iota(jnp.int32, (x.shape[0], LANES), 1)
    low_half = lane < HD
    keep = jnp.logical_xor(low_half, ent)
    every = dot_nn(x, w_ref[...]) + b_scr[:1]
    for h in range(heads):
        y = every[:, 3 * LANES * h : 3 * LANES * (h + 1)]
        q = jnp.where(ent, y[:, LANES : 2 * LANES], y[:, :LANES])
        qc_ref[h] = q.astype(bf16) * (HD ** (-0.5))
        kv = y[:, 2 * LANES :].astype(bf16).astype(f32)
        kv_ref[h] = kv.astype(bf16)
        twice = jnp.where(low_half, kv, pltpu.roll(kv, HD, 1))
        kc_ref[h] = jnp.where(keep, twice, 0.0).astype(bf16)


def project(pos, x, pieces, layout, b, ent):
    own_rows, width = x[0].shape
    tokens = own_rows * len(x)
    columns = b.shape[1]
    heads = columns // (3 * LANES)
    out = jax.ShapeDtypeStruct((heads, tokens, LANES), bf16)
    spec = pl.BlockSpec((heads, own_rows, LANES), lambda m, pos: (0, m ^ pos[0], 0))
    anywhere = pl.BlockSpec(memory_space=pltpu.HBM)
    jobs = sum(1 if masks is None else len(masks) for masks in layout)
    return pl.pallas_call(
        functools.partial(project_kernel, heads, layout),
        grid_spec=pltpu.PrefetchScalarGridSpec(
            num_scalar_prefetch=1,
            grid=(len(x),),
            in_specs=[anywhere] * 4
            + [
                pl.BlockSpec((1, columns), lambda m, pos: (0, 0)),
                pl.BlockSpec((own_rows, LANES), lambda m, pos: (m ^ pos[0], 0)),
            ]
            + [anywhere] * len(pieces),
            out_specs=[spec, spec, spec, pl.BlockSpec((width, columns), lambda m, pos: (0, 0))],
            scratch_shapes=[
                pltpu.VMEM((len(x), own_rows, width), bf16),
                pltpu.VMEM((width, columns), bf16),
                pltpu.VMEM((8, columns), f32),
                pltpu.SemaphoreType.DMA((len(x) + jobs,)),
            ],
        ),
        out_shape=[out, out, out, jax.ShapeDtypeStruct((width, columns), bf16)],
        compiler_params=params(),
        cost_estimate=cost(2 * tokens * width * columns, 2 * tokens * (width + columns)),
        name="project",
    )(pos, *x, b, ent, *pieces)


def masked_keys(pos_ref, scores, first=0):
    keys = first + lax.broadcasted_iota(jnp.int32, (scores.shape[0], 1), 0)
    return scores + jnp.where(keys < pos_ref[4], 0.0, MASKED)


def attend_kernel(pos_ref, q_ref, kc_ref, kv_ref, *rest):
    out_ref, lse_ref, vt_ref = rest[-3:]

    @pl.when(pl.program_id(1) == 0)
    def _():
        vt_ref[...] = kv_ref[0].T[HD:]

    scores = masked_keys(pos_ref, dot_nt(kc_ref[0], q_ref[0]))
    top = jnp.max(scores, 0, keepdims=True)
    exponent = jnp.exp(scores - top)
    total = jnp.sum(exponent, 0, keepdims=True)
    mixed = dot_nn(vt_ref[...], exponent.astype(bf16))
    out_ref[0] = (mixed / total).astype(bf16)
    lse_ref[0] = top + jnp.log(total)


def attend(pos, first, count, qc, kc, kv, before=()):
    heads, tokens, _ = qc.shape
    blocks = tokens // BLOCK
    full = pl.BlockSpec((1, tokens, LANES), lambda h, i, pos: (first + h, 0, 0))
    return pl.pallas_call(
        attend_kernel,
        grid_spec=pltpu.PrefetchScalarGridSpec(
            num_scalar_prefetch=1,
            grid=(count, blocks),
            in_specs=[pl.BlockSpec((1, BLOCK, LANES), lambda h, i, pos: (first + h, i, 0)), full, full]
            + [pl.BlockSpec(memory_space=pltpu.HBM)] * len(before),
            out_specs=[
                pl.BlockSpec((1, HD, BLOCK), lambda h, i, pos: (i ^ pos[0], first + h, 0)),
                pl.BlockSpec((1, 1, BLOCK), lambda h, i, pos: (h, 0, i)),
            ],
            scratch_shapes=[pltpu.VMEM((HD, tokens), bf16)],
        ),
        out_shape=[
            jax.ShapeDtypeStruct((blocks, heads * HD, BLOCK), bf16),
            jax.ShapeDtypeStruct((count, 1, tokens), f32),
        ],
        input_output_aliases={4: 0} if before else {},
        compiler_params=params(),
        cost_estimate=cost(count * tokens * tokens * 2 * 3 * LANES, count * tokens * 8 * LANES),
        name="attend",
    )(pos, qc, kc, kv, *before)


def attend_back_kernel(
    pos_ref, q_ref, kc_ref, kv_ref, ent_ref, lse_ref, out_ref, go_ref,
    dq_ref, dkv_ref, kt_ref, dk_acc, dv_acc, go_pad,
):
    step = pl.program_id(1)

    @pl.when(step == 0)
    def _():
        kt_ref[...] = kc_ref[0].T
        go_pad[:HD] = jnp.zeros((HD, go_pad.shape[1]), bf16)
        dk_acc[...] = jnp.zeros_like(dk_acc)
        dv_acc[...] = jnp.zeros_like(dv_acc)

    go = go_ref[0]
    go_pad[HD:] = go
    delta = jnp.sum(go.astype(f32) * out_ref[0].astype(f32), 0, keepdims=True)
    q = q_ref[0]
    rows = kc_ref.shape[1] // KEY_PARTS

    def keys_part(part, dq):
        at = block_rows(part, rows)
        scores = masked_keys(pos_ref, dot_nt(kc_ref[0, at], q), part * rows)
        probs = jnp.exp(scores - lse_ref[0])
        grad_probs = dot_nn(kv_ref[0, at], go_pad[...])
        grad_scores = (probs * (grad_probs - delta)).astype(bf16)
        dv_acc[at] += dot_nt(probs.astype(bf16), go_pad[...])
        dk_acc[at] += dot_nn(grad_scores, q)
        return dq + dot_nn(kt_ref[:, at], grad_scores)

    dq = lax.fori_loop(0, KEY_PARTS, keys_part, jnp.zeros((LANES, q.shape[0]), f32))
    dq_ref[0] = (dq * (HD ** (-0.5))).T.astype(bf16)

    @pl.when(step == pl.num_programs(1) - 1)
    def _():
        lane = lax.broadcasted_iota(jnp.int32, dk_acc.shape, 1)
        dk = dk_acc[...]
        dk = jnp.where(ent_ref[...] > 0.5, pltpu.roll(dk, HD, 1), dk)
        dkv_ref[0] = jnp.where(lane < HD, dk, dv_acc[...]).astype(bf16)


def attend_back(pos, first, count, qc, kc, kv, ent, lse, mixed, grad_mixed):
    tokens = qc.shape[1]
    blocks = tokens // BLOCK
    full = pl.BlockSpec((1, tokens, LANES), lambda h, i, pos: (first + h, 0, 0))
    slot = pl.BlockSpec((1, HD, BLOCK), lambda h, i, pos: (i ^ pos[0], first + h, 0))
    out = jax.ShapeDtypeStruct((count, tokens, LANES), bf16)
    return pl.pallas_call(
        attend_back_kernel,
        grid_spec=pltpu.PrefetchScalarGridSpec(
            num_scalar_prefetch=1,
            grid=(count, blocks),
            in_specs=[
                pl.BlockSpec((1, BLOCK, LANES), lambda h, i, pos: (first + h, i, 0)),
                full, full,
                pl.BlockSpec((tokens, LANES), lambda h, i, pos: (0, 0)),
                pl.BlockSpec((1, 1, BLOCK), lambda h, i, pos: (h, 0, i)),
                slot, slot,
            ],
            out_specs=[
                pl.BlockSpec((1, BLOCK, LANES), lambda h, i, pos: (h, i, 0)),
                pl.BlockSpec((1, tokens, LANES), lambda h, i, pos: (h, 0, 0)),
            ],
            scratch_shapes=[
                pltpu.VMEM((LANES, tokens), bf16),
                pltpu.VMEM((tokens, LANES), f32),
                pltpu.VMEM((tokens, LANES), f32),
                pltpu.VMEM((LANES, BLOCK), bf16),
            ],
        ),
        out_shape=[out, out],
        compiler_params=params(),
        cost_estimate=cost(count * tokens * tokens * 2 * 5 * LANES, count * tokens * 16 * LANES),
        name="attend_back",
    )(pos, qc, kc, kv, ent, lse, mixed, grad_mixed)


def normed(residual, gain, shift):
    center = residual - jnp.mean(residual, -1, keepdims=True)
    inv = lax.rsqrt(jnp.mean(center * center, -1, keepdims=True) + EPS)
    unit = center * inv
    return unit, inv, unit * gain + shift


def norm_back(grad, unit, inv, gain):
    scaled = grad * gain
    return (
        scaled
        - jnp.mean(scaled, -1, keepdims=True)
        - unit * jnp.mean(scaled * unit, -1, keepdims=True)
    ) * inv


def token_weight_jobs(layout, pos_ref, refs, w_ref):
    jobs = []
    for masks, ref in zip(layout, refs):
        if masks is None:
            jobs.append((ref, w_ref))
            continue
        for u, (mask, group_mask) in enumerate(masks):
            where = block_rows(pos_ref[2] ^ mask, ref.shape[1])
            jobs.append((ref.at[u], w_ref.at[pos_ref[1] ^ group_mask, where]))
    return jobs


def token_kernel(
    layout, pos_ref, m0, m1, m2, m3, hid_ref, cot_ref, valid_ref, vec_ref, *rest
):
    count = len(layout)
    pieces = rest[:count]
    (
        y_ref, mixt_ref, nb_ref, act_ref, gi_ref, gf_ref, ga_ref, gm_ref, gr_ref, sums_ref, gib_ref,
        slope_ref, w_ref, sum_ref, unit_ref, inv_ref, sems,
    ) = rest[count:]
    me = pos_ref[0]
    groups, width, _ = w_ref.shape
    tokens = hid_ref.shape[0]
    ffn = act_ref.shape[2]
    gwidth = mixt_ref.shape[1]
    out_at = 2 * ffn
    jobs = token_weight_jobs(layout, pos_ref, pieces, w_ref)
    early = slice(out_at, out_at + gwidth)
    loads = copies([(s.at[..., early], t.at[..., early]) for s, t in jobs], sems.at[0])
    late = copies([(s.at[..., :out_at], t.at[..., :out_at]) for s, t in jobs], sems.at[1])
    for load in loads:
        load.wait()
    for m, ref in enumerate((m0, m1, m2, m3)):
        mixt_ref[me ^ m] = ref[0]

    def vector(at):
        value = vec_ref[at]
        return jnp.concatenate([value[i : i + 1] for i in range(value.shape[0])], 1)

    out_b, gain_one, shift_one, output_b, gain_two, shift_two = (vector(at) for at in range(6))
    few = min(LANES, tokens)
    sums_ref[...] = jnp.zeros_like(sums_ref)
    gib_ref[...] = jnp.zeros_like(gib_ref)

    def by_blocks(body):
        lax.fori_loop(0, tokens // few, lambda r, _: (body(block_rows(r, few)), 0)[1], 0)

    def total(at, value):
        sums_ref[at] += jnp.sum(value, 0, keepdims=True)

    def first_norm(at):
        attended = out_b
        for g in range(groups):
            part = dot_nt(mixt_ref[g, :, at].T, w_ref[g, :, early])
            attended = attended + part.astype(bf16).astype(f32)
        unit, inv, value = normed(hid_ref[at].astype(f32) + attended, gain_one, shift_one)
        unit_ref[at] = unit
        inv_ref[at] = jnp.broadcast_to(inv, (inv.shape[0], LANES))
        nb_ref[at] = value.astype(bf16)
        sum_ref[at] = jnp.broadcast_to(output_b, value.shape)

    first_norm(slice(0, tokens))
    for load in late:
        load.wait()
    halves = 2
    part_rows = tokens // halves

    def forward(step, _):
        g, at = step // halves, block_rows(step % halves, part_rows)
        pre = dot_nn(nb_ref[at], w_ref[g, :, :ffn]) + vector(6 + g)
        cdf = 0.5 * (1.0 + lax.erf(pre * SQRT_HALF))
        slope_ref[g, at] = cdf + pre * (jnp.exp(-0.5 * pre * pre) * INV_SQRT_2PI)
        active = (pre * cdf).astype(bf16)
        act_ref[g, at] = active
        part = dot_nt(active, w_ref[g, :, ffn:out_at])
        sum_ref[at] += part.astype(bf16).astype(f32)
        return 0

    lax.fori_loop(0, groups * halves, forward, 0)

    def second_norm(at):
        valid = valid_ref[at, :1]
        normed_one = unit_ref[at] * gain_one + shift_one
        unit, inv, value = normed(normed_one + sum_ref[at], gain_two, shift_two)
        y_ref[at] = (value * valid).astype(bf16)
        grad_top = cot_ref[at].astype(f32) * valid
        grad = norm_back(grad_top, unit, inv, gain_two)
        grad_ffn = grad.astype(bf16)
        gf_ref[at] = grad_ffn
        sum_ref[at] = grad
        total(3, grad_ffn.astype(f32))
        total(4, grad_top * unit)
        total(5, grad_top)

    by_blocks(second_norm)

    def backward(step, _):
        g, at = step // halves, block_rows(step % halves, part_rows)
        grad_active = dot_nn(gf_ref[at], w_ref[g, :, ffn:out_at])
        grad_inner = (slope_ref[g, at] * grad_active).astype(bf16)
        gi_ref[g, at] = grad_inner
        gib_ref[g] += jnp.sum(grad_inner.astype(f32), 0, keepdims=True)
        part = dot_nt(grad_inner, w_ref[g, :, :ffn])
        sum_ref[at] += part.astype(bf16).astype(f32)
        return 0

    lax.fori_loop(0, groups * halves, backward, 0)

    def first_norm_back(at):
        grad_normed = sum_ref[at]
        unit = unit_ref[at]
        grad = norm_back(grad_normed, unit, inv_ref[at, :1], gain_one)
        gr_ref[at] = grad
        grad_att = grad.astype(bf16)
        ga_ref[at] = grad_att
        total(0, grad_att.astype(f32))
        total(1, grad_normed * unit)
        total(2, grad_normed)

    by_blocks(first_norm_back)

    def mixed_back(m, _):
        out_rows = w_ref[me ^ m, :, early].T
        gm_ref[m] = dot_nt(out_rows, ga_ref[...]).astype(bf16)
        return 0

    for m in range(groups):
        mixed_back(m, 0)


def per_token(
    pos, mixed, hidden, cot, valid, vectors, pieces, layout, groups, columns
):
    tokens, width = hidden.shape
    ffn = vectors.shape[1] * vectors.shape[2]
    gwidth = mixed[0].shape[1]
    vmem = pl.BlockSpec(memory_space=pltpu.VMEM)
    shape = jax.ShapeDtypeStruct
    jobs = sum(1 if masks is None else len(masks) for masks in layout)
    return pl.pallas_call(
        functools.partial(token_kernel, layout),
        in_specs=[pl.BlockSpec(memory_space=pltpu.SMEM)]
        + [vmem] * 8
        + [pl.BlockSpec(memory_space=pltpu.HBM)] * len(pieces),
        out_specs=[vmem] * 11,
        out_shape=[
            shape((tokens, width), bf16),
            shape((groups, gwidth, tokens), bf16),
            shape((tokens, width), bf16),
            shape((groups, tokens, ffn), bf16),
            shape((groups, tokens, ffn), bf16),
            shape((tokens, width), bf16),
            shape((tokens, width), bf16),
            shape((groups, gwidth, tokens), bf16),
            shape((tokens, width), f32),
            shape((6, 1, width), f32),
            shape((groups, 1, ffn), f32),
        ],
        scratch_shapes=[
            pltpu.VMEM((groups, tokens, ffn), f32),
            pltpu.VMEM((groups, width, columns), bf16),
            pltpu.VMEM((tokens, width), f32),
            pltpu.VMEM((tokens, width), f32),
            pltpu.VMEM((tokens, LANES), f32),
            pltpu.SemaphoreType.DMA((2, jobs)),
        ],
        compiler_params=params(),
        cost_estimate=cost(
            8 * tokens * width * ffn * groups + 4 * tokens * width * width,
            2 * groups * width * columns + 4 * tokens * ffn * groups,
            2 * tokens * ffn * groups,
        ),
        name="per_token",
    )(pos, *mixed, hidden, cot, valid, vectors, *pieces)


def weight_grad_kernel(
    pos_ref, nb_ref, gf_ref, ga_ref, act_ref, gi_ref, mixt_ref, near_ref, far_ref, nbt, gft, gat, turn
):
    ffn = act_ref.shape[2]
    gwidth = mixt_ref.shape[1]
    chips, _, rows, _ = near_ref.shape

    @pl.when(pl.program_id(0) == 0)
    def _():
        for target, source in ((nbt, nb_ref), (gft, gf_ref), (gat, ga_ref)):
            turn[...] = source[...].T
            for mine in range(2):
                for mask in range(chips):
                    block = pos_ref[2] ^ (2 * mask + mine)
                    at = (mine * chips + mask) * rows
                    target[at : at + rows] = turn[block_rows(block, rows)]

    second_half = (pl.program_id(0) ^ pos_ref[1]) % 2

    def put(value, start, stop):
        for mine, out_ref in enumerate((near_ref, far_ref)):
            for mask in range(chips):
                slot = mask + second_half - 1 if mask == 2 else mask + 1 - second_half if mask == 1 else mask
                at = (mine * chips + mask) * rows
                out_ref[slot, 0, :, start:stop] = value[at : at + rows].astype(bf16)

    put(dot_nn(nbt[...], gi_ref[0]), 0, ffn)
    put(dot_nn(gft[...], act_ref[0]), ffn, 2 * ffn)
    put(dot_nt(gat[...], mixt_ref[0]), 2 * ffn, 2 * ffn + gwidth)


def weight_grads(pos, nb, gf, ga, act, gi, mixt, dp):
    groups, tokens, ffn = act.shape
    width = nb.shape[1]
    gwidth = mixt.shape[1]
    rows = width // dp
    whole = pl.BlockSpec((tokens, width), lambda g, pos: (0, 0))
    group = pl.BlockSpec((1, tokens, ffn), lambda g, pos: (g, 0, 0))
    columns = 2 * ffn + gwidth
    out = jax.ShapeDtypeStruct((dp // 2, groups, rows, columns), bf16)

    def slot(g, pos):
        mask = g ^ pos[1]
        return (0, 2 * (mask % 2) + mask // 2, 0, 0)

    spec = pl.BlockSpec((dp // 2, 1, rows, columns), slot)
    return pl.pallas_call(
        weight_grad_kernel,
        grid_spec=pltpu.PrefetchScalarGridSpec(
            num_scalar_prefetch=1,
            grid=(groups,),
            in_specs=[
                whole, whole, whole, group, group,
                pl.BlockSpec((1, gwidth, tokens), lambda g, pos: (g, 0, 0)),
            ],
            out_specs=[spec, spec],
            scratch_shapes=[pltpu.VMEM((width, tokens), bf16)] * 4,
        ),
        out_shape=[out, out],
        compiler_params=params(),
        cost_estimate=cost(2 * tokens * width * columns * groups, 2 * groups * width * columns),
        name="weight_grads",
    )(pos, nb, gf, ga, act, gi, mixt)


def weight_grad_whole_kernel(nb_ref, gf_ref, ga_ref, act_ref, gi_ref, mixt_ref, out_ref, nbt, gft, gat):
    ffn = act_ref.shape[2]
    gwidth = mixt_ref.shape[1]

    @pl.when(pl.program_id(0) == 0)
    def _():
        nbt[...] = nb_ref[...].T
        gft[...] = gf_ref[...].T
        gat[...] = ga_ref[...].T

    out_ref[0, :, :ffn] = dot_nn(nbt[...], gi_ref[0]).astype(bf16)
    out_ref[0, :, ffn : 2 * ffn] = dot_nn(gft[...], act_ref[0]).astype(bf16)
    out_ref[0, :, 2 * ffn : 2 * ffn + gwidth] = dot_nt(gat[...], mixt_ref[0]).astype(bf16)


def weight_grads_whole(nb, gf, ga, act, gi, mixt):
    groups, tokens, ffn = act.shape
    width = nb.shape[1]
    gwidth = mixt.shape[1]
    whole = pl.BlockSpec((tokens, width), lambda g: (0, 0))
    group = pl.BlockSpec((1, tokens, ffn), lambda g: (g, 0, 0))
    columns = 2 * ffn + gwidth
    return pl.pallas_call(
        weight_grad_whole_kernel,
        grid=(groups,),
        in_specs=[whole, whole, whole, group, group, pl.BlockSpec((1, gwidth, tokens), lambda g: (g, 0, 0))],
        out_specs=pl.BlockSpec((1, width, columns), lambda g: (g, 0, 0)),
        out_shape=jax.ShapeDtypeStruct((groups, width, columns), bf16),
        scratch_shapes=[pltpu.VMEM((width, tokens), bf16)] * 3,
        compiler_params=params(),
        cost_estimate=cost(2 * tokens * width * columns * groups, 2 * groups * width * columns),
        name="weight_grads_whole",
    )(nb, gf, ga, act, gi, mixt)


def split_columns(pairs, ent):
    h = 0
    for dq_ref, dkv_ref in pairs:
        for u in range(dq_ref.shape[0]):
            dq = dq_ref[u]
            nothing = jnp.zeros_like(dq)
            yield 3 * h, jnp.where(ent, nothing, dq)
            yield 3 * h + 1, jnp.where(ent, dq, nothing)
            yield 3 * h + 2, dkv_ref[u]
            h += 1


def input_grad_kernel(count, pos_ref, *refs):
    grads, (ent_ref, w_ref, out_ref) = refs[:count], refs[count:]
    ent = ent_ref[...] > 0.5
    cols = [c for _, c in split_columns(list(zip(grads[::2], grads[1::2])), ent)]
    out_ref[0] = dot_nt(jnp.concatenate(cols, 1), w_ref[...]).astype(bf16)


def input_grad(pos, grads, ent, w, far):
    tokens = grads[0].shape[1]
    width, columns = w.shape

    def block(i, pos):
        return i + 2 * (pos[3] ^ far)

    stacked = [pl.BlockSpec((g.shape[0], BLOCK, LANES), lambda i, pos: (0, block(i, pos), 0)) for g in grads]
    return pl.pallas_call(
        functools.partial(input_grad_kernel, len(grads)),
        grid_spec=pltpu.PrefetchScalarGridSpec(
            num_scalar_prefetch=1,
            grid=(2,),
            in_specs=stacked
            + [
                pl.BlockSpec((BLOCK, LANES), lambda i, pos: (block(i, pos), 0)),
                pl.BlockSpec((width, columns), lambda i, pos: (0, 0)),
            ],
            out_specs=pl.BlockSpec((1, BLOCK, width), lambda i, pos: (i ^ (pos[0] % 2), 0, 0)),
        ),
        out_shape=jax.ShapeDtypeStruct((2, BLOCK, width), bf16),
        compiler_params=params(),
        cost_estimate=cost(tokens * width * columns, tokens * (columns + width), short=100),
        name="input_grad",
    )(pos, *grads, ent, w)


def all_sums(pos_ref, bias, sums_ref, gib_ref, out_ref):
    gwidth = bias.shape[1] // 6
    zeros = jnp.zeros((1, gwidth), f32)
    for row, part in enumerate((0, 1, 2, 3, 5)):
        own = bias[:1, gwidth * part : gwidth * (part + 1)]
        out_ref[row : row + 1] = jnp.concatenate(
            [jnp.where(pos_ref[0] == j, own, zeros) for j in range(out_ref.shape[1] // gwidth)], 1
        )
    rest = [sums_ref[i] for i in range(sums_ref.shape[0])] + [gib_ref[i] for i in range(gib_ref.shape[0])]
    for row, value in enumerate(rest):
        out_ref[5 + row : 6 + row] = value
    out_ref[5 + len(rest) :] = jnp.zeros((out_ref.shape[0] - 5 - len(rest), out_ref.shape[1]), f32)


def project_grad_kernel(pos_ref, x0, x1, x2, x3, *refs):
    (
        *grads, ent_ref, sums_ref, gib_ref, keep_ref, first_ref, second_ref, bias_ref, acc_ref, bias_acc,
        x_ref, sems,
    ) = refs
    step = pl.program_id(0)

    @pl.when(step == 0)
    def _():
        loads = copies([(ref, x_ref.at[m]) for m, ref in enumerate((x0, x1, x2, x3))], sems)
        acc_ref[...] = jnp.zeros_like(acc_ref)
        bias_acc[...] = jnp.zeros_like(bias_acc)
        for load in loads:
            load.wait()

    ent = ent_ref[...] > 0.5
    columns = jnp.concatenate([c for _, c in split_columns(list(zip(grads[::2], grads[1::2])), ent)], 1)
    acc_ref[...] += dot_nn(x_ref[step].T, columns)
    bias_acc[:1] += jnp.sum(columns.astype(f32), 0, keepdims=True)

    @pl.when(step == pl.num_programs(0) - 1)
    def _():
        chips, cores, rows, columns = keep_ref.shape
        heads = columns // (3 * LANES)
        all_sums(pos_ref, by_parts(bias_acc[...], heads), sums_ref, gib_ref, bias_ref)
        targets = [
            [keep_ref.at[0, 0], first_ref.at[0], keep_ref.at[1, 0], first_ref.at[1]],
            [keep_ref.at[0, 1], keep_ref.at[1, 1], second_ref.at[0], second_ref.at[1]],
        ]
        for mask in range(4):
            for core in range(2):
                at = block_rows(2 * ((pos_ref[2] // 2) ^ mask) + core, rows)
                targets[core][mask][...] = by_parts(acc_ref[at].astype(bf16), heads)


def project_grad_whole_kernel(*refs):
    *ins, out_ref, bias_ref, acc_ref, bias_acc, x_ref, sems = refs
    heads = out_ref.shape[1] // (3 * LANES)
    pos_ref, x0, x1, x2, x3, *grads, ent_ref, sums_ref, gib_ref = ins
    step = pl.program_id(0)

    @pl.when(step == 0)
    def _():
        loads = copies([(ref, x_ref.at[m]) for m, ref in enumerate((x0, x1, x2, x3))], sems)
        acc_ref[...] = jnp.zeros_like(acc_ref)
        bias_acc[...] = jnp.zeros_like(bias_acc)
        for load in loads:
            load.wait()

    ent = ent_ref[...] > 0.5
    columns = jnp.concatenate([c for _, c in split_columns(list(zip(grads[::2], grads[1::2])), ent)], 1)
    acc_ref[...] += dot_nn(x_ref[step].T, columns)
    bias_acc[:1] += jnp.sum(columns.astype(f32), 0, keepdims=True)

    @pl.when(step == pl.num_programs(0) - 1)
    def _():
        out_ref[...] = by_parts(acc_ref[...].astype(bf16), heads)
        all_sums(pos_ref, by_parts(bias_acc[...], heads), sums_ref, gib_ref, bias_ref)


def project_grad(pos, x, grads, ent, sums, gib, by_hops):
    heads = sum(g.shape[0] for g in grads) // 2
    tokens = grads[0].shape[1]
    own_rows, width = x[0].shape
    columns = 3 * LANES * heads
    rows = width // 8
    shapes = [(2, 2, rows, columns)] + [(2, rows, columns)] * 2 if by_hops else [(width, columns)]
    stacked = [pl.BlockSpec((g.shape[0], own_rows, LANES), lambda m, pos: (0, m ^ pos[0], 0)) for g in grads]

    def fixed(shape):
        return pl.BlockSpec(shape, lambda m, pos: (0,) * len(shape))

    return pl.pallas_call(
        project_grad_kernel if by_hops else project_grad_whole_kernel,
        grid_spec=pltpu.PrefetchScalarGridSpec(
            num_scalar_prefetch=1,
            grid=(len(x),),
            in_specs=[pl.BlockSpec(memory_space=pltpu.HBM)] * 4
            + stacked
            + [pl.BlockSpec((own_rows, LANES), lambda m, pos: (m ^ pos[0], 0))]
            + [fixed(sums.shape), fixed(gib.shape)],
            out_specs=[fixed(shape) for shape in shapes] + [fixed((16, width))],
            scratch_shapes=[
                pltpu.VMEM((width, columns), f32),
                pltpu.VMEM((8, columns), f32),
                pltpu.VMEM((len(x), own_rows, width), bf16),
                pltpu.SemaphoreType.DMA((len(x),)),
            ],
        ),
        out_shape=[jax.ShapeDtypeStruct(shape, bf16) for shape in shapes]
        + [jax.ShapeDtypeStruct((16, width), f32)],
        compiler_params=params(),
        cost_estimate=cost(2 * tokens * width * columns, 2 * tokens * (columns + width)),
        name="project_grad",
    )(pos, *x, *grads, ent, sums, gib)


def finish_project_kernel(kept_ref, arrived_ref, q_ref, k_ref, v_ref):
    total = kept_ref[...].astype(f32) + arrived_ref[...].astype(f32)
    width = k_ref.shape[1]
    for a in range(q_ref.shape[0]):
        q_ref[a] = total[:, width * a : width * (a + 1)]
    k_ref[...] = total[:, 4 * width : 5 * width]
    v_ref[...] = total[:, 5 * width :]


def finish_project(kept, arrived):
    rows, columns = kept.shape
    part = jax.ShapeDtypeStruct((rows, columns // 6), f32)
    return pl.pallas_call(
        finish_project_kernel,
        out_shape=[jax.ShapeDtypeStruct((4, rows, columns // 6), f32), part, part],
        compiler_params=params(),
        cost_estimate=cost(rows * columns, 8 * rows * columns),
        name="finish_project",
    )(kept, arrived)


def finish_ffn_kernel(kept_ref, arrived_ref, inter_ref, output_ref, out_ref):
    total = kept_ref[...].astype(f32) + arrived_ref[...].astype(f32)
    ffn = inter_ref.shape[1]
    inter_ref[...] = total[:, :ffn]
    output_ref[...] = total[:, ffn : 2 * ffn].T
    out_ref[...] = total[:, 2 * ffn :].T


def finish_ffn(kept, arrived, ffn):
    rows, columns = kept.shape
    shape = jax.ShapeDtypeStruct
    return pl.pallas_call(
        finish_ffn_kernel,
        out_shape=[shape((rows, ffn), f32), shape((ffn, rows), f32), shape((columns - 2 * ffn, rows), f32)],
        compiler_params=params(),
        cost_estimate=cost(rows * columns, 8 * rows * columns),
        name="finish_ffn",
    )(kept, arrived)


def local(
    hidden_in, token_types, lengths, cotangent, query_w, query_b, key_w, value_w, value_b, out_w,
    out_b, gain_one, shift_one, inter_w, inter_b, output_w, output_b, gain_two, shift_two,
):
    groups = lax.axis_size("tensor")
    dp = lax.axis_size("dp")
    z = lax.axis_index("tensor")
    d = lax.axis_index("dp")
    half = groups // 2
    core = d % 2
    upper = z // half
    me = z % half + half * core
    own_rows, width = hidden_in.shape
    length = own_rows * groups
    gwidth = query_w.shape[2]
    heads = gwidth // HD
    ffn = inter_w.shape[1]
    rows = key_w.shape[0]
    columns = 2 * ffn + gwidth
    total = dp * groups
    by_hops = dp == 8 and rows % 16 == 0

    def device(dd, zz):
        return dd * groups + zz

    def swapped(dev):
        dd, zz = dev // groups, dev % groups
        return device(dd - dd % 2 + zz // half, zz % half + half * (dd % 2))

    def member(dev, mask):
        dd, zz = dev // groups, dev % groups
        j = (zz % half + half * (dd % 2)) ^ mask
        return device(dd - dd % 2 + j // half, zz - zz % half + j % half)

    stays = core == upper

    def relocate(value):
        moves = [(i, swapped(i)) for i in range(total) if swapped(i) != i]
        return jnp.where(stays, value, lax.ppermute(value, ("dp", "tensor"), moves))

    def to_member(value, mask):
        return lax.ppermute(value, ("dp", "tensor"), [(i, member(i, mask)) for i in range(total)])

    def over_dp(value, mask):
        return lax.ppermute(value, "dp", [(i, i ^ mask) for i in range(dp)])

    def over_z(value, mask):
        return lax.ppermute(value, "tensor", [(i, i ^ mask) for i in range(groups)])

    def add(*terms):
        return functools.reduce(jnp.add, [t.astype(f32) for t in terms])

    def after(value, *others):
        return lax.optimization_barrier((value, *others))[0]

    own_project = jnp.concatenate([*query_w, key_w, value_w], 1)
    own_ffn = jnp.concatenate([inter_w, output_w.T, out_w.T], 1)

    def between(value, pairs):
        return lax.ppermute(value, ("dp", "tensor"), [p for p in pairs if p[0] != p[1]])

    swaps = [(i, swapped(i)) for i in range(total)]
    on_chips = [(i, member(i, 1)) for i in range(total)]
    stay_chips = [p for p in on_chips if swapped(p[0]) == p[0]]
    move_chips = [p for p in on_chips if swapped(p[0]) != p[0]]

    def phase(*values):
        return lax.optimization_barrier(values)

    near_chip = between(hidden_in, stay_chips)
    moved = between(hidden_in, swaps)
    facts = jnp.concatenate([token_types, lengths])
    facts_moved = over_dp(facts, 1)
    few = (query_b, value_b, out_b, gain_one, shift_one, output_b, gain_two, shift_two, inter_b)
    if by_hops:
        other = over_dp(own_project, 1)
        pair = jnp.where(core == 0, jnp.stack([own_project, other]), jnp.stack([other, own_project]))
        pair, facts_moved, facts, *few = phase(relocate(pair), facts_moved, facts, *few)
    query_b, value_b, *rest = few
    query_b_own = lax.dynamic_slice_in_dim(query_b, me * gwidth, gwidth, 1)
    value_b_own = lax.dynamic_slice_in_dim(value_b, me * gwidth, gwidth)
    b_project = jnp.concatenate([query_b_own.reshape(-1), jnp.zeros((gwidth,), bf16), value_b_own])
    b_project = b_project.reshape(1, 6 * gwidth).astype(f32)
    vectors = jnp.concatenate([v.astype(f32).reshape(-1, width // LANES, LANES) for v in rest])
    facts = jnp.where(stays, facts, facts_moved)
    pos = jnp.concatenate([jnp.stack([me, z, d, upper]).astype(jnp.int32), facts[length:]])
    ent = jnp.broadcast_to(facts[:length, None].astype(bf16), (length, LANES))
    valid_own = me * own_rows + jnp.arange(own_rows, dtype=jnp.int32) < facts[length]
    valid_own = jnp.broadcast_to(valid_own[:, None].astype(f32), (own_rows, LANES))
    if by_hops:
        pair_x, pair_y, b_project, vectors, pos, ent, valid_own = phase(
            over_dp(pair, 2), over_dp(pair, 4), b_project, vectors, pos, ent, valid_own
        )
        moved, near_chip, own_z, own_ffn, a_x, b_y = phase(
            moved, near_chip, over_z(own_ffn, 1), own_ffn, pair_x[0], pair_y[1]
        )
    hidden = jnp.where(stays, hidden_in, moved)
    from_chip = between(hidden, move_chips)
    if by_hops:
        from_chip, a_xy, b_xy, own_x, own_y = phase(
            from_chip, over_dp(a_x, 4), over_dp(b_y, 2), over_dp(own_ffn, 2), over_dp(own_ffn, 4)
        )
        from_chip = jnp.where(stays, near_chip, from_chip)
        x_2, x_3, own_ffn, own_x, own_z = phase(
            to_member(hidden, half), to_member(from_chip, half), own_ffn, own_x, own_z
        )
        both = ((0, 0), (0, 1))
        project_pieces = [pair, pair_x, pair_y, a_xy[None], b_xy[None]]
        project_layout = (both, tuple((1, c) for _, c in both), tuple((2, c) for _, c in both), ((3, 0),), ((3, 1),))
    else:
        project_pieces = [relocate(lax.all_gather(own_project, "dp", axis=0, tiled=True))]
        project_layout = (None,)
        from_chip = jnp.where(stays, near_chip, from_chip)
        x_2, x_3 = to_member(hidden, half), to_member(from_chip, half)
    x = [hidden, from_chip, x_2, x_3]

    qc, kc, kv, w_project = project(pos, x, project_pieces, project_layout, b_project, ent)
    if by_hops:
        token_pieces, token_layout = [], []

        def pieces(group_mask, **by):
            masks = [({"own": 0, "x": 2, "y": 4, "xy": 6}[axes], group_mask) for axes in by]
            token_layout.extend([tuple(masks), tuple((m + 1, g) for m, g in masks)])
            return jnp.stack(list(by.values()))

        qc, far, own_zx, own_zy, own_xy = phase(
            qc, over_z(own_ffn, 2), over_dp(own_z, 2), over_dp(own_z, 4), over_dp(own_x, 4)
        )
        quad = pieces(0, own=own_ffn, x=own_x, y=own_y, xy=own_xy)
        mixed, lse_0 = attend(pos, 0, 1, qc, kc, kv)
        mixed, far_z, far_x, far_y, quad_core = phase(
            mixed, over_z(far, 1), over_dp(far, 2), over_dp(far, 4), over_dp(quad, 1)
        )
        token_pieces += [quad, quad_core]
        mixed, lse_1 = attend(pos, 1, heads - 1, qc, kc, kv, (mixed,))
        mixed, far_zx, far_zy, far_xy, own_zxy, cot = phase(
            mixed, over_dp(far_z, 2), over_dp(far_z, 4), over_dp(far_x, 4), over_dp(own_zy, 2),
            between(after(cotangent, far_x), swaps),
        )
        cot = jnp.where(stays, cotangent, cot)
        quad = pieces(1, own=own_z, x=own_zx, y=own_zy, xy=own_zxy)
        mixed_own, far_zxy, quad_core, cot = phase(
            [mixed[:1]] + [to_member(mixed[m : m + 1], m) for m in range(1, groups)], over_dp(far_zy, 2),
            over_dp(quad, 1), cot
        )
        token_pieces += [quad, quad_core]
        for quad in (
            pieces(2, own=far, x=far_x, y=far_y, xy=far_xy),
            pieces(3, own=far_z, x=far_zx, y=far_zy, xy=far_zxy),
        ):
            token_pieces += [quad, over_dp(quad, 1)]
        token_layout = tuple(token_layout)
    else:
        token_pieces = [lax.all_gather(lax.all_gather(own_ffn, "tensor"), "dp", axis=1, tiled=True)]
        token_layout = (None,)
        mixed, lse_0 = attend(pos, 0, 1, qc, kc, kv)
        mixed, lse_1 = attend(pos, 1, heads - 1, qc, kc, kv, (mixed,))
        mixed_own = [mixed[:1]] + [to_member(mixed[m : m + 1], m) for m in range(1, groups)]
        cot = jnp.where(stays, cotangent, between(cotangent, swaps))
    y, mixt, nb, act, gi, gf, ga, gm, grad_resid_one, sums, gib = per_token(
        pos, mixed_own, hidden, cot, valid_own, vectors, token_pieces, token_layout, groups, columns
    )
    grad_mixed = jnp.concatenate([gm[:1]] + [to_member(gm[m : m + 1], m) for m in range(1, groups)])

    order = ((1, 2), (2, 1))
    if by_hops:
        near, far = weight_grads(pos, nb, gf, ga, act, gi, mixt, dp)
        arrived = over_dp(after(far, grad_mixed), 1)
        grads = attend_back(pos, 0, 1, qc, kc, kv, ent, lse_0, mixed, grad_mixed)
        groups_at = (slice(0, 2), slice(2, 4))
        kept = [add(near[:2, g], arrived[:2, g]).astype(bf16) for g in groups_at]
        sent = [add(near[2:, g], arrived[2:, g]).astype(bf16) for g in groups_at]
        grads, kept, sent, qc, y = phase(grads, kept, sent, qc, y)
        more = attend_back(pos, 1, heads - 1, qc, kc, kv, ent, lse_1, mixed, grad_mixed)
        more, moved, layer_moved = phase(
            more, [over_dp(v, 2 * one) for v, (one, _) in zip(sent, order)], between(y, swaps)
        )
    else:
        ffn_grads = weight_grads_whole(nb, gf, ga, act, gi, mixt)
        ffn_grads = lax.psum_scatter(ffn_grads, "tensor", scatter_dimension=0, tiled=False)
        ffn_grads = lax.psum_scatter(ffn_grads, "dp", scatter_dimension=0, tiled=True)
        grads = attend_back(pos, 0, 1, qc, kc, kv, ent, lse_0, mixed, grad_mixed)
        more = attend_back(pos, 1, heads - 1, qc, kc, kv, ent, lse_1, mixed, grad_mixed)
        layer_moved = between(y, swaps)
    layer_out = jnp.where(stays, y, layer_moved)
    grads = [*grads, *more]

    core_stay = [(i, i ^ groups) for i in range(total) if swapped(i) == i]
    core_move = [(i, i ^ groups) for i in range(total) if swapped(i) != i]
    if by_hops:
        sent = [add(k[1], m[1]).astype(bf16) for k, m in zip(kept, moved)]
        kept = [add(k[0], m[0]).astype(bf16) for k, m in zip(kept, moved)]
        first_x, sent, kept = phase(x[0], sent, kept)
        moved = [over_dp(v, 2 * two) for v, (_, two) in zip(sent, order)]
        project_kept, *project_sent, flat = project_grad(pos, [first_x, *x[1:]], grads, ent, sums, gib, True)
        project_kept, project_sent, flat, moved = phase(project_kept, project_sent, flat, moved)
        kept, sent_z = [add(k, m).astype(bf16) for k, m in zip(kept, moved)]
        kept, sent_z, first, project_sent = phase(kept, sent_z, grads[0], project_sent)
    else:
        project_grads, flat = project_grad(pos, x, grads, ent, sums, gib, False)
        first = grads[0]
    partial_far = input_grad(pos, [first, *grads[1:]], ent, w_project, 1)
    far_core = between(partial_far, core_stay)
    if by_hops:
        arrived = [over_dp(v, 2 * one) for v, (one, _) in zip(project_sent, order)]
        arrived_z = over_z(sent_z, 1)
        far_sum = add(partial_far, far_core)
        far_here, far_there, flat, second = phase(far_sum[0], far_sum[1].astype(bf16), flat, grads[3])
    else:
        far_sum = add(partial_far, far_core)
        far_here, far_there, second = far_sum[0], far_sum[1].astype(bf16), grads[3]
    far_chip = between(far_there, move_chips)
    partial_near = input_grad(pos, [*grads[:3], second], ent, w_project, 0)
    if by_hops:
        partial_near, arrived, arrived_z, hop = phase(partial_near, arrived, arrived_z, over_z(flat, 2))
        flat = flat + hop
        sent = [add(project_kept[1, s], m[1]).astype(bf16) for s, m in enumerate(arrived)]
        project_kept = [add(project_kept[0, s], m[0]).astype(bf16) for s, m in enumerate(arrived)]
        kept_z = add(kept, arrived_z)
        kept_z, last = kept_z[0], kept_z[1].astype(bf16)
        sent, last, flat, partial_near = phase(sent, last, flat, partial_near)
        far_chip, moved, last, near_core = phase(
            far_chip, [over_dp(v, 2 * two) for v, (_, two) in zip(sent, order)], over_z(last, 2),
            between(partial_near, core_move),
        )
        near_sum = add(partial_near, near_core)
        near_here, near_there = near_sum[0], near_sum[1].astype(bf16)
        far_sum = add(far_here, far_chip, grad_resid_one).astype(bf16)
        project_ends = jnp.stack([add(k, m).astype(bf16) for k, m in zip(project_kept, moved)])
        far_sum, project_ends, near_here, near_there, flat = phase(
            far_sum, project_ends, near_here, near_there, flat
        )
        flat = flat + over_z(flat, 1)
        for mask in (2, 4, 1):
            flat = flat + over_dp(flat, mask)
        project_moved = between(project_ends, swaps)
        far_moved, near_chip, flat = phase(between(far_sum, swaps), between(near_there, stay_chips), flat)
        project_ends = jnp.where(stays, project_ends, project_moved)
        project_kept = jnp.where(core == 0, project_ends[0], project_ends[1])
        sent = jnp.where(core == 0, project_ends[1], project_ends[0])
        query_grads, key_grads, value_grads = finish_project(project_kept, over_dp(sent, 1))
        inter_grads, output_grads, out_grads = finish_ffn(kept_z, last, ffn)
    else:
        far_moved = between(add(far_here, far_chip, grad_resid_one).astype(bf16), swaps)
        near_sum = add(partial_near, between(partial_near, core_move))
        near_here = near_sum[0]
        near_chip = between(near_sum[1].astype(bf16), stay_chips)
        project_grads = relocate(project_grads)
        project_grads = lax.psum_scatter(project_grads, "dp", scatter_dimension=0, tiled=True)
        query_grads, key_grads, value_grads = finish_project(project_grads, jnp.zeros_like(project_grads))
        inter_grads, output_grads, out_grads = finish_ffn(ffn_grads, jnp.zeros_like(ffn_grads), ffn)
        flat = lax.psum(flat, ("dp", "tensor"))
    near_sum = add(near_here, near_chip, grad_resid_one)
    grad_hidden = jnp.where(stays, near_sum, far_moved.astype(f32))
    return (
        layer_out,
        grad_hidden,
        query_grads,
        flat[:4],
        key_grads,
        value_grads,
        flat[4],
        out_grads,
        flat[5],
        flat[6],
        flat[7],
        inter_grads,
        flat[11 : 11 + groups].reshape(groups * ffn),
        output_grads,
        flat[8],
        flat[9],
        flat[10],
    )


def solution(mesh):
    weights = P("dp", "tensor")
    tokens = P(("dp", "tensor"), None)
    return jax.shard_map(
        local,
        mesh=mesh,
        in_specs=(
            tokens, P("dp"), P("dp"), tokens, P(None, "dp", "tensor"), P(), weights, weights, P(),
            P("tensor", "dp"), P(), P(), P(), weights, P(), P("tensor", "dp"), P(), P(), P(),
        ),
        out_specs=(
            tokens, tokens, P(None, "dp", "tensor"), P(), weights, weights, P(), P("tensor", "dp"),
            P(), P(), P(), weights, P(), P("tensor", "dp"), P(), P(), P(),
        ),
        check_vma=False,
    )
```
